32 devices in a mesh: groups: 2 (over x), seq: 16 (over z, y, core).
Axes of the slice: x: 2, y: 2, z: 4, core: 2. Of those that a mesh axis runs over, the one named last changes fastest.
Arguments:
- inner_x: bfloat16 [32768, 2048], P(('groups', 'seq')), parts along dimension 0, may hold values from -6 to 6
- input_map: bfloat16 [32768, 128], P(('groups', 'seq')), parts along dimension 0, may hold values from -6 to 6
- output_map: bfloat16 [32768, 128], P(('groups', 'seq')), parts along dimension 0, may hold values from -6 to 6
- step_raw: float32 [32768, 32], P(('groups', 'seq')), parts along dimension 0, may hold values from -3 to 3
- kernel_x: float32 [4, 2048], replicated, may hold values from -3 to 3
- kernel_b: float32 [4, 128], replicated, may hold values from -3 to 3
- kernel_c: float32 [4, 128], replicated, may hold values from -3 to 3
- log_rate: float32 [32], replicated
- step_bias: float32 [32], replicated
- skip_gain: float32 [32], replicated, may hold values from 0.5 to 2
Outputs:
- mixed_out: bfloat16 [32768, 2048], P(('groups', 'seq')), parts along dimension 0
The draws below stay inside these ranges and needn't reach their ends.
There are 2 independent parts, one for each index of `groups`. The reference program is written for one: setup_inputs(seed, part) draws one part's arguments, and reference() takes and returns one part's arrays. A program takes and returns all parts, laid end to end along the dimension named above; an argument that names none is the same for every part. Nothing has to cross between parts.
All inputs are finite; a program needn't handle non-finite values.
Results may differ from the reference program's by a relative error of at most 0.0034.
Values may be sent and summed in bfloat16 or wider, within the bound.
A program may use at most 128 MiB of HBM per device.

```python
import math
import jax
import jax.numpy as jnp
from jax import lax

HEADS = 32
HEADDIM = 64
STATE = 128
BLOCK_LEN = 256
KW = 4
TOKENS = 16384
D_INNER = 2048


def head_windows(key):
    order_key = jax.random.fold_in(key, 11)
    fast_key = jax.random.fold_in(key, 12)
    slow_key = jax.random.fold_in(key, 13)
    ranking = jax.random.permutation(order_key, HEADS)
    slow_count = HEADS // 2
    fast_span = jnp.exp(jax.random.uniform(fast_key, (HEADS,), jnp.float32, math.log(BLOCK_LEN / 8.0), math.log(BLOCK_LEN / 5.0)))
    slow_span = jax.random.uniform(slow_key, (HEADS,), jnp.float32, 0.6, 3.0) * TOKENS
    return jnp.where(ranking < slow_count, slow_span, fast_span)


def draw_log_rate(key, part):
    return (-0.5 * jnp.log(head_windows(key))).astype(jnp.float32)


def draw_step_bias(key, part):
    target = head_windows(key) ** (-0.5)
    return jnp.log(jnp.expm1(target)).astype(jnp.float32)


def level_of(rng, dims, cuts, least, largest):
    factor_of, own = 1.0, jax.random.fold_in(rng, 6)
    for position, shards_of in cuts:
        steps = jnp.exp(jax.random.uniform(jax.random.fold_in(own, position), (shards_of,), jnp.float32, least / len(cuts), largest / len(cuts)))
        factor_of = factor_of * jnp.repeat(steps, dims[position] // shards_of).reshape([-1 if axis == position else 1 for axis in range(len(dims))])
    return factor_of


def normal_values(stream_key, dims, scale, most, cuts=(), dtype=jnp.bfloat16):
    values = jax.random.normal(stream_key, dims, jnp.float32) * scale
    if len(cuts) > 0:
        values = level_of(stream_key, dims, cuts, -0.22, 0.18) * values
    return jnp.clip(values, min=-most, max=most).astype(dtype)


def setup_inputs(seed: int = 0, part: int = 0) -> dict:
    streams_of = jax.random.split(jax.random.key(seed), 11)
    part_keys = jax.random.split(jax.random.fold_in(streams_of[10], part), 11)
    inner_x = normal_values(part_keys[0], (TOKENS, D_INNER), 1.0, 6.0, ((0, 16),))
    input_map = normal_values(part_keys[1], (TOKENS, STATE), 1.0, 6.0, ((0, 16),))
    output_map = normal_values(part_keys[2], (TOKENS, STATE), 1.0, 6.0, ((0, 16),))
    step_raw = normal_values(part_keys[3], (TOKENS, HEADS), 0.5, 3.0, ((0, 16),), jnp.float32)
    kernel_x = normal_values(streams_of[4], (KW, D_INNER), KW ** -0.5, 3.0, (), jnp.float32)
    kernel_b = normal_values(streams_of[5], (KW, STATE), KW ** -0.5, 3.0, (), jnp.float32)
    kernel_c = normal_values(streams_of[6], (KW, STATE), KW ** -0.5, 3.0, (), jnp.float32)
    log_rate = draw_log_rate(jax.random.fold_in(streams_of[10], 71), part)
    step_bias = draw_step_bias(jax.random.fold_in(streams_of[10], 71), part)
    skip_gain = jnp.clip(jnp.exp(jax.random.uniform(streams_of[9], (HEADS,), jnp.float32, math.log(0.5), math.log(2.0))), 0.5, 2.0)
    return {"inner_x": inner_x, "input_map": input_map, "output_map": output_map, "step_raw": step_raw, "kernel_x": kernel_x, "kernel_b": kernel_b, "kernel_c": kernel_c, "log_rate": log_rate, "step_bias": step_bias, "skip_gain": skip_gain}


def conv_silu(window, kernel):
    taps = kernel.shape[0]
    length = window.shape[0] - taps + 1
    summed = jnp.zeros((length, window.shape[1]), jnp.float32)
    for offset in range(taps):
        summed = summed + kernel[offset][None, :] * window[offset:offset + length].astype(jnp.float32)
    return jax.nn.silu(summed).astype(jnp.bfloat16)


def block_local(xconv, bconv, cconv, step_dt, decay_rate):
    length = xconv.shape[0]
    head_count = step_dt.shape[1]
    cumulative = jnp.cumsum(step_dt * decay_rate[None, :], axis=0)
    block_total = cumulative[-1]
    score_gram = jnp.dot(cconv, bconv.T, preferred_element_type=jnp.float32)
    by_head = cumulative.T
    places = jnp.arange(length)
    causal = (places[:, None] >= places[None, :])[None]
    spread = jnp.where(causal, by_head[:, :, None] - by_head[:, None, :], 0.0)
    weights = jnp.where(causal, score_gram[None] * jnp.exp(spread) * step_dt.T[:, None, :], 0.0).astype(jnp.bfloat16)
    weights = lax.optimization_barrier(weights).astype(jnp.float32)
    per_head = xconv.reshape(length, head_count, -1).astype(jnp.float32)
    inner_sum = jnp.einsum("hts,shp->thp", weights, per_head)
    scaled = (per_head * (jnp.exp(block_total[None, :] - cumulative) * step_dt)[:, :, None]).astype(jnp.bfloat16)
    scaled = lax.optimization_barrier(scaled).astype(jnp.float32)
    block_state = jnp.einsum("thp,tn->hpn", scaled, bconv.astype(jnp.float32))
    return inner_sum, block_state, cumulative, block_total


def finish_block(inner_sum, entering, cconv, cumulative, xconv, skip_gain):
    length, head_count = cumulative.shape
    enter_low = lax.optimization_barrier(entering.astype(jnp.bfloat16)).astype(jnp.float32)
    carried = jnp.einsum("tn,hpn->thp", cconv.astype(jnp.float32), enter_low)
    per_head = xconv.reshape(length, head_count, -1).astype(jnp.float32)
    summed = inner_sum + jnp.exp(cumulative)[:, :, None] * carried + skip_gain[None, :, None] * per_head
    return summed.reshape(length, -1).astype(jnp.bfloat16)


def reference(inner_x, input_map, output_map, step_raw, kernel_x, kernel_b, kernel_c, log_rate, step_bias, skip_gain):
    length = BLOCK_LEN
    block_count = TOKENS // BLOCK_LEN
    history = KW - 1
    decay_rate = -jnp.exp(log_rate)
    inputs = (inner_x.reshape(block_count, length, -1), input_map.reshape(block_count, length, -1),
              output_map.reshape(block_count, length, -1), step_raw.reshape(block_count, length, -1))
    initial = (jnp.zeros((HEADS, HEADDIM, STATE), jnp.float32),
               jnp.zeros((history, inner_x.shape[1]), jnp.bfloat16),
               jnp.zeros((history, STATE), jnp.bfloat16),
               jnp.zeros((history, STATE), jnp.bfloat16))

    def advance(carried_in, blocks):
        entering, tail_x, tail_b, tail_c = carried_in
        block_x, block_b, block_c, block_dt = blocks
        xconv = conv_silu(jnp.concatenate([tail_x, block_x], axis=0), kernel_x)
        bconv = conv_silu(jnp.concatenate([tail_b, block_b], axis=0), kernel_b)
        cconv = conv_silu(jnp.concatenate([tail_c, block_c], axis=0), kernel_c)
        step_dt = jax.nn.softplus(block_dt + step_bias[None, :])
        inner_sum, block_state, cumulative, block_total = block_local(xconv, bconv, cconv, step_dt, decay_rate)
        mixed_block = finish_block(inner_sum, entering, cconv, cumulative, xconv, skip_gain)
        following = jnp.exp(block_total)[:, None, None] * entering + block_state
        return (following, block_x[length - history:], block_b[length - history:], block_c[length - history:]), mixed_block

    last_carry, outputs = lax.scan(advance, initial, inputs)
    return outputs.reshape(TOKENS, -1)
```

```python
import functools

import jax
import jax.numpy as jnp
from jax import lax
from jax.experimental import pallas as pl
from jax.experimental.pallas import tpu as pltpu
from jax.sharding import PartitionSpec as P

CHUNK = 128
ROWS = 256
LANES = 128
LOG2E = 1.4426950408889634
HALO = 8
VMEM_LIMIT = 60 << 20
DECAY_ROWS = 16


def split_low(value):
    high = value.astype(jnp.bfloat16)
    return high, (value - high.astype(jnp.float32)).astype(jnp.bfloat16)


def silu(value):
    half = 0.5 * value
    return half + half * jnp.tanh(half)


def expander(heads, width, parts):
    shape = (parts * heads, heads * width)
    row = lax.broadcasted_iota(jnp.int32, shape, 0) % heads
    col = lax.broadcasted_iota(jnp.int32, shape, 1) // width
    return (row == col).astype(jnp.bfloat16)


def state_kernel(
    heads, x_ref, b_ref, c_ref, raw_ref, tail_ref, kx_ref, kb_ref, kc_ref, rate_ref, bias_ref,
    xconv_ref, bc_ref, aux_ref, prefix_ref, run_ref,
    xwin, bwin, cwin, spread, scaled, expand, state, logrun,
):
    step = pl.program_id(0)
    inner = x_ref.shape[1]
    wide = b_ref.shape[1]
    pairs = inner // LANES

    @pl.when(step == 0)
    def _():
        tail = tail_ref[...].astype(jnp.float32)
        xwin[0:HALO, :] = tail[:, :inner]
        bwin[0:HALO, :] = tail[:, inner : inner + wide]
        cwin[0:HALO, :] = tail[:, inner + wide :]
        expand[...] = expander(heads, inner // heads, 2)
        state[...] = jnp.zeros_like(state)
        logrun[...] = jnp.zeros_like(logrun)

    @pl.when(step > 0)
    def _():
        xwin[0:HALO, :] = xwin[ROWS : ROWS + HALO, :]
        bwin[0:HALO, :] = bwin[ROWS : ROWS + HALO, :]
        cwin[0:HALO, :] = cwin[ROWS : ROWS + HALO, :]

    bwin[HALO:, :] = b_ref[...].astype(jnp.float32)
    cwin[HALO:, :] = c_ref[...].astype(jnp.float32)

    def small_conv(win, taps):
        count = taps.shape[0]
        total = jnp.zeros((ROWS, win.shape[1]), jnp.float32)
        for k in range(count):
            at = HALO - (count - 1) + k
            total = total + taps[k : k + 1, :] * win[at : at + ROWS, :]
        return silu(total).astype(jnp.bfloat16)

    bconv = small_conv(bwin, kb_ref)
    cconv = small_conv(cwin, kc_ref)
    bc_ref[:, :wide] = bconv
    bc_ref[:, wide:] = cconv

    shifted = raw_ref[...] + bias_ref[...]
    dt = jnp.maximum(shifted, 0.0) + jnp.log1p(jnp.exp(-jnp.abs(shifted)))
    logdec = -(jnp.exp(rate_ref[...]) * LOG2E) * dt
    part0, rest = logdec.astype(jnp.bfloat16), None
    rest = logdec - part0.astype(jnp.float32)
    part1 = rest.astype(jnp.bfloat16)
    part2 = (rest - part1.astype(jnp.float32)).astype(jnp.bfloat16)
    row = lax.broadcasted_iota(jnp.int32, (CHUNK, CHUNK), 0)
    col = lax.broadcasted_iota(jnp.int32, (CHUNK, CHUNK), 1)
    lower = (row >= col).astype(jnp.bfloat16)
    parts = jnp.concatenate([part0, part1, part2, jnp.zeros_like(part0)], axis=1)
    logdt = jnp.log(dt) * LOG2E
    totals = []
    for q in range(ROWS // CHUNK):
        span = slice(q * CHUNK, (q + 1) * CHUNK)
        sums = jnp.dot(lower, parts[span], preferred_element_type=jnp.float32)
        cum = sums[:, :heads] + sums[:, heads : 2 * heads] + sums[:, 2 * heads : 3 * heads]
        total = cum[CHUNK - 1 :, :]
        totals.append(total)
        shift = cum - logdt[span]
        run = logrun[...] + cum
        logrun[...] = logrun[...] + total
        aux_ref[span, :] = jnp.concatenate([cum, shift, run, jnp.zeros_like(run)], axis=1)
        high, low = split_low(jnp.exp2(total - shift))
        spread[span, :] = jnp.dot(
            jnp.concatenate([high, low], axis=1), expand[...], preferred_element_type=jnp.float32
        )

    @pl.loop(0, pairs)
    def _(j):
        lanes = pl.ds(pl.multiple_of(j * LANES, LANES), LANES)
        xwin[HALO:, lanes] = x_ref[:, lanes].astype(jnp.float32)
        count = kx_ref.shape[0]
        total = jnp.zeros((ROWS, LANES), jnp.float32)
        for k in range(count):
            at = HALO - (count - 1) + k
            total = total + kx_ref[k : k + 1, lanes] * xwin[at : at + ROWS, lanes]
        xc = silu(total).astype(jnp.bfloat16)
        xconv_ref[:, lanes] = xc
        scaled[:, lanes] = (xc.astype(jnp.float32) * spread[:, lanes]).astype(jnp.bfloat16)

    btrans = bconv.astype(jnp.float32).T.astype(jnp.bfloat16)
    for q in range(ROWS // CHUNK):
        span = slice(q * CHUNK, (q + 1) * CHUNK)
        prefix_ref[q] = state[...].astype(jnp.bfloat16)
        factor = jnp.broadcast_to(jnp.exp2(totals[q]), (8, heads))
        high, low = split_low(factor)
        decay = jnp.dot(
            jnp.concatenate([high, low], axis=1), expand[...], preferred_element_type=jnp.float32
        )[0:1, :]
        state[...] = decay * state[...] + jnp.dot(
            btrans[:, span], scaled[span, :], preferred_element_type=jnp.float32
        )

    @pl.when(step == pl.num_programs(0) - 1)
    def _():
        high, low = split_low(jnp.broadcast_to(jnp.exp2(logrun[...]), (8, heads)))
        zero = jnp.zeros_like(high)
        high = jnp.dot(jnp.concatenate([high, zero], axis=1), expand[...], preferred_element_type=jnp.float32)
        low = jnp.dot(jnp.concatenate([low, zero], axis=1), expand[...], preferred_element_type=jnp.float32)
        both = jnp.concatenate([high, low], axis=0).astype(jnp.bfloat16)
        for j in range(pairs):
            lanes = slice(j * LANES, (j + 1) * LANES)
            run_ref[j, 0 : state.shape[0], :] = state[:, lanes].astype(jnp.bfloat16)
            run_ref[j, state.shape[0] :, :] = both[:, lanes]


def local_states(x, b, c, raw, tail, kx, kb, kc, rate, bias):
    rows, inner = x.shape
    wide = b.shape[1]
    heads = raw.shape[1]
    pairs = inner // LANES
    whole = lambda a: pl.BlockSpec(a.shape, lambda i: (0,) * a.ndim)
    block = lambda w: pl.BlockSpec((ROWS, w), lambda i: (i, 0))
    per = ROWS // CHUNK
    f32, bf16 = jnp.float32, jnp.bfloat16
    return pl.pallas_call(
        functools.partial(state_kernel, heads),
        grid=(rows // ROWS,),
        in_specs=[block(inner), block(wide), block(wide), block(heads), whole(tail), whole(kx),
                  whole(kb), whole(kc), whole(rate), whole(bias)],
        out_specs=[
            block(inner), block(2 * wide), block(LANES),
            pl.BlockSpec((per, wide, inner), lambda i: (i, 0, 0)),
            pl.BlockSpec((pairs, wide + DECAY_ROWS, LANES), lambda i: (0, 0, 0)),
        ],
        out_shape=[
            jax.ShapeDtypeStruct((rows, inner), bf16),
            jax.ShapeDtypeStruct((rows, 2 * wide), bf16),
            jax.ShapeDtypeStruct((rows, LANES), f32),
            jax.ShapeDtypeStruct((rows // CHUNK, wide, inner), bf16),
            jax.ShapeDtypeStruct((pairs, wide + DECAY_ROWS, LANES), bf16),
        ],
        scratch_shapes=[
            pltpu.VMEM((ROWS + HALO, inner), f32), pltpu.VMEM((ROWS + HALO, wide), f32),
            pltpu.VMEM((ROWS + HALO, wide), f32), pltpu.VMEM((ROWS, inner), f32),
            pltpu.VMEM((ROWS, inner), bf16), pltpu.VMEM((2 * heads, inner), bf16),
            pltpu.VMEM((wide, inner), f32), pltpu.VMEM((1, heads), f32),
        ],
        compiler_params=pltpu.CompilerParams(vmem_limit_bytes=VMEM_LIMIT),
        cost_estimate=pl.CostEstimate(flops=2 * 10**9, bytes_accessed=12 << 20, transcendentals=1 << 21),
        name="local_states",
    )(x, b, c, raw, tail, kx, kb, kc, rate, bias)


def inner_kernel(heads, xconv_ref, bc_ref, aux_ref, prefix_ref, gain_ref, y_ref):
    wide = bc_ref.shape[1] // 2
    pairs = xconv_ref.shape[1] // LANES
    aux = aux_ref[...]
    turned = aux.T
    bconv, cconv = bc_ref[:, :wide], bc_ref[:, wide:]
    row = lax.broadcasted_iota(jnp.int32, (CHUNK, CHUNK), 0)
    col = lax.broadcasted_iota(jnp.int32, (CHUNK, CHUNK), 1)
    gram = lax.dot_general(cconv, bconv, (((1,), (1,)), ((), ())), preferred_element_type=jnp.float32)
    gram = jnp.where(row >= col, gram, 0.0)
    left = lax.broadcasted_iota(jnp.int32, (CHUNK, LANES), 1) < LANES // 2
    for j in range(pairs):
        lanes = slice(j * LANES, (j + 1) * LANES)
        xc = xconv_ref[:, lanes]
        weights = []
        cums = []
        for h in (2 * j, 2 * j + 1):
            cum = jnp.broadcast_to(aux[:, h : h + 1], (CHUNK, CHUNK))
            cums.append(cum)
            power = jnp.minimum(cum - turned[heads + h : heads + h + 1, :], 126.0)
            weights.append((gram * jnp.exp2(power)).astype(jnp.bfloat16))
        zero = jnp.zeros_like(xc)
        both = jnp.concatenate([jnp.where(left, xc, zero), jnp.where(left, zero, xc)], axis=0)
        inner = jnp.dot(jnp.concatenate(weights, axis=1), both, preferred_element_type=jnp.float32)
        carried = jnp.dot(cconv, prefix_ref[0, :, lanes], preferred_element_type=jnp.float32)
        decay = jnp.exp2(jnp.where(left, cums[0], cums[1]))
        y_ref[:, lanes] = inner + decay * carried + gain_ref[:, lanes] * xc.astype(jnp.float32)


def local_mix(first, count, xconv, bc, aux, prefix, gain):
    inner = xconv.shape[1]
    heads = gain.shape[1] // 64
    wide = bc.shape[1] // 2
    block = lambda w: pl.BlockSpec((CHUNK, w), lambda i: (i + first, 0))
    return pl.pallas_call(
        functools.partial(inner_kernel, heads),
        grid=(count,),
        in_specs=[block(inner), block(2 * wide), block(LANES),
                  pl.BlockSpec((1, wide, inner), lambda i: (i + first, 0, 0)),
                  pl.BlockSpec((1, inner), lambda i: (0, 0))],
        out_specs=pl.BlockSpec((CHUNK, inner), lambda i: (i, 0)),
        out_shape=jax.ShapeDtypeStruct((count * CHUNK, inner), jnp.float32),
        compiler_params=pltpu.CompilerParams(vmem_limit_bytes=VMEM_LIMIT),
        cost_estimate=pl.CostEstimate(flops=10**10, bytes_accessed=24 << 20, transcendentals=1 << 22),
        name="local_mix",
    )(xconv, bc, aux, prefix, gain)


def scan_kernel(got_ref, out_ref):
    members, rows, width = out_ref.shape
    entering = jnp.zeros((rows, width), jnp.float32)
    for k in range(members):
        out_ref[k] = entering.astype(jnp.bfloat16)
        decay = got_ref[k, rows : rows + 1, :].astype(jnp.float32) + got_ref[
            k, rows + 8 : rows + 9, :
        ].astype(jnp.float32)
        entering = decay * entering + got_ref[k, 0:rows, :].astype(jnp.float32)


def scan_members(got):
    members, rows, width = got.shape
    return pl.pallas_call(
        scan_kernel,
        out_shape=jax.ShapeDtypeStruct((members, rows - DECAY_ROWS, width), jnp.bfloat16),
        compiler_params=pltpu.CompilerParams(vmem_limit_bytes=VMEM_LIMIT),
        name="scan_members",
    )(got)


def finish_kernel(heads, ya_ref, yb_ref, bc_ref, aux_ref, inc_ref, out_ref, expand):
    wide = bc_ref.shape[1] // 2
    pairs = out_ref.shape[1] // LANES

    @pl.when(pl.program_id(0) == 0)
    def _():
        expand[...] = expander(heads, out_ref.shape[1] // heads, 2)

    high, low = split_low(jnp.exp2(aux_ref[:, 2 * heads : 3 * heads]))
    factors = jnp.concatenate([high, low], axis=1)
    cconv = bc_ref[:, wide:]
    early = pl.program_id(0) < pl.num_programs(0) // 2

    def emit(y_ref):
        for j in range(pairs):
            lanes = slice(j * LANES, (j + 1) * LANES)
            decay = jnp.dot(factors, expand[:, lanes], preferred_element_type=jnp.float32)
            carried = jnp.dot(cconv, inc_ref[j], preferred_element_type=jnp.float32)
            out_ref[:, lanes] = (y_ref[:, lanes] + decay * carried).astype(jnp.bfloat16)

    @pl.when(early)
    def _():
        emit(ya_ref)

    @pl.when(jnp.logical_not(early))
    def _():
        emit(yb_ref)


def finish(heads, ya, yb, bc, aux, inc):
    rows, inner = bc.shape[0], ya.shape[1]
    wide = bc.shape[1] // 2
    steps = rows // CHUNK
    half = steps // 2
    block = lambda w: pl.BlockSpec((CHUNK, w), lambda i: (i, 0))
    return pl.pallas_call(
        functools.partial(finish_kernel, heads),
        grid=(steps,),
        in_specs=[
            pl.BlockSpec((CHUNK, inner), lambda i: (jnp.minimum(i, half - 1), 0)),
            pl.BlockSpec((CHUNK, inner), lambda i: (jnp.maximum(i - half, 0), 0)),
            block(2 * wide), block(LANES), pl.BlockSpec(inc.shape, lambda i: (0, 0, 0)),
        ],
        out_specs=block(inner),
        out_shape=jax.ShapeDtypeStruct((rows, inner), jnp.bfloat16),
        scratch_shapes=[pltpu.VMEM((2 * heads, inner), jnp.bfloat16)],
        compiler_params=pltpu.CompilerParams(vmem_limit_bytes=VMEM_LIMIT),
        name="finish",
    )(ya, yb, bc, aux, inc)


def exchange(x):
    return lax.all_to_all(x, "seq", split_axis=0, concat_axis=0, tiled=True)


def regroup(x, count):
    groups, rows, width = x.shape
    if groups == count:
        return x
    flat = x.transpose(1, 0, 2).reshape(rows, groups * width)
    return flat.reshape(rows, count, groups * width // count).transpose(1, 0, 2)


FUSED_CHIPS = 8
PAD = 16
QUAD = 2 * LANES
BIG = 1e38


def fused_kernel(
    x_hbm, b_hbm, c_hbm, raw_ref, kx_ref, kb_ref, kc_ref, rate_ref, bias_ref, gain_ref,
    y, cconv, decays, incoming,
    xbuf, bbuf, cbuf, xc, bconv, aux, turned, expand, gains, falls, ends, factors, grown, btrans, prefix, window,
    run, core_got, chip_sum, got, entered, back, core_out, arrived,
    load_sem, small_sem, tail_send, tail_recv, core_send, core_recv,
    give_send, give_recv, take_send, take_recv, last_send, last_recv,
):
    f32, bf16 = jnp.float32, jnp.bfloat16
    members = 2 * FUSED_CHIPS
    me = lax.axis_index("seq")
    chip, core = me // 2, me % 2
    partner = chip * 2 + 1 - core
    first_core = core == 0
    rows, inner = xc.shape
    wide = bconv.shape[1]
    heads = rate_ref.shape[1]
    pairs = inner // LANES
    blocks = rows // ROWS
    chunks = rows // CHUNK
    half = pairs // 2
    steps = pairs // 2

    def place(i):
        k = i // 2
        m = (k * 2) % 4 + (k * 2) // 4
        mine = i % 2
        owner = mine * core + (1 - mine) * (1 - core)
        return m, owner * (half // 2) + m

    def quad_lanes(i):
        return pl.ds(pl.multiple_of(place(i)[1] * QUAD, QUAD), QUAD)

    def load(i):
        lanes = quad_lanes(i)
        return pltpu.make_async_copy(
            x_hbm.at[:, lanes], xbuf.at[pl.ds(PAD, rows), lanes], load_sem.at[i]
        )

    small = [
        pltpu.make_async_copy(b_hbm, bbuf.at[pl.ds(PAD, rows)], small_sem.at[0]),
        pltpu.make_async_copy(c_hbm, cbuf.at[pl.ds(PAD, rows)], small_sem.at[1]),
    ]
    small[0].start()
    for i in range(steps):
        load(i).start()
    small[1].start()

    barrier = pltpu.get_barrier_semaphore()
    for off in range(1, members):
        pl.semaphore_signal(
            barrier, inc=1, device_id={"seq": lax.rem(me + off, members)},
            device_id_type=pl.DeviceIdType.MESH,
        )

    def remote(src, dst, send, recv, to):
        return pltpu.make_async_remote_copy(
            src_ref=src, dst_ref=dst, send_sem=send, recv_sem=recv, device_id={"seq": to},
            device_id_type=pl.DeviceIdType.MESH,
        )

    after = lax.rem(me + 1, members)
    tails = [
        remote(h.at[pl.ds(rows - PAD, PAD)], v.at[pl.ds(0, PAD)], tail_send.at[i], tail_recv.at[i], after)
        for i, (h, v) in enumerate(((x_hbm, xbuf), (b_hbm, bbuf), (c_hbm, cbuf)))
    ]

    expand[...] = expander(heads, inner // heads, 2)
    high, middle = split_low(jnp.broadcast_to(gain_ref[...], (8, heads)))
    low = (gain_ref[...] - high.astype(f32) - middle.astype(f32)).astype(bf16)
    gains[...] = jnp.dot(
        jnp.concatenate([high, middle], axis=1), expand[...], preferred_element_type=f32
    ) + jnp.dot(
        jnp.concatenate([low, jnp.zeros_like(low)], axis=1), expand[...], preferred_element_type=f32
    )
    row = lax.broadcasted_iota(jnp.int32, (CHUNK, CHUNK), 0)
    col = lax.broadcasted_iota(jnp.int32, (CHUNK, CHUNK), 1)
    params = jnp.concatenate([rate_ref[...], bias_ref[...], rate_ref[...], bias_ref[...]], axis=1)
    params = jnp.broadcast_to(params, (CHUNK, CHUNK)).T
    speed = jnp.exp(params[:heads]) * LOG2E
    bias = params[heads : 2 * heads]
    upper = (row <= col).astype(bf16)
    log_before = jnp.zeros((heads, CHUNK), f32)
    chunk_falls = []
    for q in range(chunks):
        span = slice(q * CHUNK, (q + 1) * CHUNK)
        shifted = raw_ref[:, span] + bias
        dt = jnp.maximum(shifted, 0.0) + jnp.log1p(jnp.exp(-jnp.abs(shifted)))
        logdec = -speed * dt
        part0 = logdec.astype(bf16)
        rest = logdec - part0.astype(f32)
        part1 = rest.astype(bf16)
        part2 = (rest - part1.astype(f32)).astype(bf16)
        sums = jnp.dot(
            jnp.concatenate([part0, part1, part2], axis=0), upper, preferred_element_type=f32
        )
        cum = sums[:heads] + sums[heads : 2 * heads] + sums[2 * heads :]
        total = jnp.broadcast_to(cum[:, CHUNK - 1 :], cum.shape)
        shift = cum - jnp.log(dt) * LOG2E
        flat = jnp.concatenate(
            [cum, shift, jnp.exp2(log_before + cum), jnp.exp2(total - shift)], axis=0
        )
        log_before = log_before + total
        stood = flat.T
        turned[q] = flat
        aux[q] = stood
        factors[span, :] = stood[:, 3 * heads :].astype(bf16)
        high, low = split_low(stood[:, 2 * heads : 3 * heads])
        grown[span, :] = jnp.concatenate([high, low], axis=1)
        chunk_falls.append(jnp.exp2(stood[CHUNK - 1 :, :heads]))
    high, low = split_low(jnp.concatenate(chunk_falls, axis=0))
    falls[...] = jnp.dot(
        jnp.concatenate([high, low], axis=1), expand[...], preferred_element_type=f32
    )
    high, low = split_low(
        jnp.broadcast_to(stood[CHUNK - 1 :, 2 * heads : 3 * heads], (8, heads))
    )
    zero = jnp.zeros_like(high)
    high = jnp.dot(jnp.concatenate([high, zero], axis=1), expand[...], preferred_element_type=f32)
    low = jnp.dot(jnp.concatenate([low, zero], axis=1), expand[...], preferred_element_type=f32)
    ends[...] = jnp.concatenate([high, low], axis=0).astype(bf16)
    pl.semaphore_wait(barrier, members - 1)

    @pl.when(me < members - 1)
    def _():
        for copy in tails:
            copy.start()

    def convolve(buf, taps_ref, out, block, lanes, slot):
        slot[...] = buf[block * ROWS : block * ROWS + ROWS + PAD, lanes].astype(f32)
        taps = 0.5 * taps_ref[:, lanes]
        count = taps.shape[0]
        total = taps[0:1] * slot[PAD - count + 1 : PAD - count + 1 + ROWS, :]
        for k in range(1, count):
            at = PAD - count + 1 + k
            total = total + taps[k : k + 1] * slot[at : at + ROWS, :]
        out[block * ROWS : (block + 1) * ROWS, lanes] = (total + total * jnp.tanh(total)).astype(bf16)

    def convolve_quad(i, block):
        for part in range(2):
            lanes = pl.ds(pl.multiple_of(place(i)[1] * QUAD + part * LANES, LANES), LANES)
            convolve(xbuf, kx_ref, xc, block, lanes, window.at[part])

    everything = slice(0, LANES)

    def early(i):
        load(i).wait()

        @pl.loop(1, blocks)
        def _(block):
            at = pl.multiple_of(block * ROWS, ROWS)
            for part in range(2):
                lanes = pl.ds(pl.multiple_of(place(i)[1] * QUAD + part * LANES, LANES), LANES)
                slot = window.at[part]
                slot[...] = xbuf[pl.ds(at, ROWS + PAD), lanes].astype(f32)
                taps = 0.5 * kx_ref[:, lanes]
                count = taps.shape[0]
                total = taps[0:1] * slot[PAD - count + 1 : PAD - count + 1 + ROWS, :]
                for k in range(1, count):
                    to = PAD - count + 1 + k
                    total = total + taps[k : k + 1] * slot[to : to + ROWS, :]
                xc[pl.ds(at, ROWS), lanes] = (total + total * jnp.tanh(total)).astype(bf16)

    small[0].wait()
    for block in range(1, blocks):
        convolve(bbuf, kb_ref, bconv, block, everything, window.at[block % 2])
    early(0)
    early(1)
    small[1].wait()
    for block in range(1, blocks):
        convolve(cbuf, kc_ref, cconv, block, everything, window.at[block % 2])

    @pl.when(me > 0)
    def _():
        for copy in tails:
            copy.wait_recv()

    @pl.when(me == 0)
    def _():
        xbuf[0:PAD, :] = jnp.zeros((PAD, inner), bf16)
        bbuf[0:PAD, :] = jnp.zeros((PAD, wide), bf16)
        cbuf[0:PAD, :] = jnp.zeros((PAD, wide), bf16)

    convolve(bbuf, kb_ref, bconv, 0, everything, window.at[0])
    convolve(cbuf, kc_ref, cconv, 0, everything, window.at[1])
    for block in range(blocks):
        span = slice(block * ROWS, (block + 1) * ROWS)
        btrans[:, span] = bconv[span, :].astype(f32).T.astype(bf16)

    def quad_state(i):
        lanes = quad_lanes(i)
        first = place(i)[1] * 2
        held = jnp.zeros((wide, QUAD), f32)
        for q in range(chunks):
            span = slice(q * CHUNK, (q + 1) * CHUNK)
            spread = jnp.dot(factors[span, :], expand[:heads, lanes], preferred_element_type=f32)
            scaled = xc[span, lanes] * spread.astype(bf16)
            prefix[q, :, lanes] = held.astype(bf16)
            held = falls[q : q + 1, lanes] * held + jnp.dot(
                btrans[:, span], scaled, preferred_element_type=f32
            )
        held = held.astype(bf16)
        tip = ends[:, lanes]
        for part in range(2):
            piece = slice(part * LANES, (part + 1) * LANES)
            run[first + part, 0:wide, :] = held[:, piece]
            run[first + part, wide:, :] = tip[:, piece]

    def to_core(m):
        return remote(
            run.at[pl.ds((1 - core) * half + 2 * m, 2)], core_got.at[pl.ds(2 * m, 2)],
            core_send.at[m], core_recv.at[m], partner,
        )

    def give(other):
        return remote(
            chip_sum.at[other], got.at[chip], give_send.at[other], give_recv.at[chip],
            other * 2 + core,
        )

    def given(other):
        return remote(
            chip_sum.at[other], got.at[other], give_send.at[other], give_recv.at[other],
            other * 2 + core,
        )

    def take(other):
        return remote(
            entered.at[other], back.at[chip], take_send.at[other], take_recv.at[chip],
            other * 2 + core,
        )

    def taken(other):
        return remote(
            entered.at[other], back.at[other], take_send.at[other], take_recv.at[other],
            other * 2 + core,
        )

    def last():
        return remote(
            core_out, arrived, last_send.at[0], last_recv.at[0], partner,
        )

    def decay_of(piece):
        return piece[wide : wide + 1].astype(f32) + piece[wide + 8 : wide + 9].astype(f32)

    def add_cores(m):
        to_core(m).wait_recv()
        for part in range(2):
            j = 2 * m + part
            mine, other = run[core * half + j], core_got[j]
            lead = jnp.where(first_core, mine.astype(f32), other.astype(f32))
            trail = jnp.where(first_core, other.astype(f32), mine.astype(f32))
            fall = trail[wide : wide + 1] + trail[wide + 8 : wide + 9]
            whole = (lead[wide : wide + 1] + lead[wide + 8 : wide + 9]) * fall
            high, low = split_low(jnp.broadcast_to(whole, (8, LANES)))
            chip_sum[j, 0:wide, :] = (fall * lead[:wide] + trail[:wide]).astype(bf16)
            chip_sum[j, wide:, :] = jnp.concatenate(
                [high.astype(f32), low.astype(f32)], axis=0
            ).astype(bf16)

            @pl.when(j != chip)
            def _():
                give(j).start()

            @pl.when(j == chip)
            def _():
                got[chip] = chip_sum[chip]

    def others(act):
        for k in range(FUSED_CHIPS):

            @pl.when(k != chip)
            def _():
                act(k)

    def scan_chips():
        others(lambda k: given(k).wait_recv())
        value = jnp.zeros((wide, LANES), f32)
        for k in range(FUSED_CHIPS):
            entered[k] = value.astype(bf16)
            if k < FUSED_CHIPS - 1:
                piece = got[k]
                value = decay_of(piece) * value + piece[:wide].astype(f32)
        others(lambda k: take(k).start())
        back[chip] = entered[chip]

    def split_cores():
        others(lambda k: taken(k).wait_recv())
        for j in range(half):
            lead = jnp.where(
                first_core, run[core * half + j].astype(f32), core_got[j].astype(f32)
            )
            entering = back[j].astype(f32)
            fall = lead[wide : wide + 1] + lead[wide + 8 : wide + 9]
            later = fall * entering + lead[:wide]
            core_out[j] = jnp.where(first_core, later, entering).astype(bf16)
            incoming[core * half + j] = jnp.where(first_core, entering, later).astype(bf16)
        last().start()

    @pl.loop(0, steps)
    def _(i):
        convolve_quad(i, 0)
        quad_state(i)
        m = place(i)[0]

        @pl.when(i % 2 == 0)
        def _():
            to_core(m).start()

        @pl.when(i + 2 < steps)
        def _():
            early(i + 2)

        @pl.when(i % 2 == 1)
        def _():
            add_cores(m)

    @pl.when(me < members - 1)
    def _():
        for copy in tails:
            copy.wait_send()

    left = lax.broadcasted_iota(jnp.int32, (CHUNK, LANES), 1) < LANES // 2

    @pl.loop(0, chunks)
    def _(q):
        at = pl.ds(pl.multiple_of(q * CHUNK, CHUNK), CHUNK)
        cc = cconv[at, :]
        gram = lax.dot_general(
            cc, bconv[at, :], (((1,), (1,)), ((), ())), preferred_element_type=f32
        )
        gram = jnp.where(row >= col, gram, 0.0).astype(bf16)
        for g in range(pairs // 2):
            wider = slice(g * QUAD, (g + 1) * QUAD)
            carried = jnp.dot(cc, prefix[q, :, wider], preferred_element_type=f32)
            for part in range(2):
                j = 2 * g + part
                lanes = slice(j * LANES, (j + 1) * LANES)
                values = xc[at, lanes]
                weights, cums = [], []
                for h in (2 * j, 2 * j + 1):
                    cum = jnp.broadcast_to(aux[q, :, h : h + 1], (CHUNK, CHUNK))
                    cums.append(cum)
                    grow = jnp.exp2(cum - turned[q, heads + h : heads + h + 1, :]).astype(bf16)
                    weights.append(gram * jnp.minimum(grow, jnp.asarray(BIG, bf16)))
                zero = jnp.zeros_like(values)
                both = jnp.concatenate(
                    [jnp.where(left, values, zero), jnp.where(left, zero, values)], axis=0
                )
                mixed = jnp.dot(jnp.concatenate(weights, axis=1), both, preferred_element_type=f32)
                decay = jnp.exp2(jnp.where(left, cums[0], cums[1]))
                y[at, lanes] = (
                    mixed + decay * carried[:, part * LANES : (part + 1) * LANES]
                    + gains[0:1, lanes] * values.astype(f32)
                )

        @pl.when(q == SCAN_AT)
        def _():
            scan_chips()

        @pl.when(q == SPLIT_AT)
        def _():
            split_cores()

    @pl.loop(0, chunks)
    def _(q):
        at = pl.ds(pl.multiple_of(q * CHUNK, CHUNK), CHUNK)
        for g in range(pairs // 2):
            wider = slice(g * QUAD, (g + 1) * QUAD)
            decays[at, wider] = jnp.dot(grown[at, :], expand[:, wider], preferred_element_type=f32)

    for m in range(half // 2):
        to_core(m).wait_send()
    others(lambda k: give(k).wait_send())
    others(lambda k: take(k).wait_send())
    last().wait()
    incoming[pl.ds((1 - core) * half, half)] = arrived[...]


SCAN_AT = 3
SPLIT_AT = 7


def output_kernel(y_ref, c_ref, decay_ref, inc_ref, out_ref):
    q = pl.program_id(0)
    at = pl.ds(pl.multiple_of(q * CHUNK, CHUNK), CHUNK)
    cc = c_ref[at, :]
    for g in range(inc_ref.shape[0] // 2):
        wider = slice(g * QUAD, (g + 1) * QUAD)
        entering = jnp.concatenate([inc_ref[2 * g], inc_ref[2 * g + 1]], axis=1)
        carried = jnp.dot(cc, entering, preferred_element_type=jnp.float32)
        out_ref[:, wider] = (y_ref[at, wider] + decay_ref[at, wider] * carried).astype(jnp.bfloat16)


def fused(inner_x, input_map, output_map, raw, kernel_x, kernel_b, kernel_c, rate, bias, gain):
    rows, inner = inner_x.shape
    wide = input_map.shape[1]
    heads = rate.shape[1]
    pairs = inner // LANES
    half = pairs // 2
    chunks = rows // CHUNK
    f32, bf16 = jnp.float32, jnp.bfloat16
    anywhere = pl.BlockSpec(memory_space=pl.ANY)
    near = pl.BlockSpec(memory_space=pltpu.VMEM)
    tall = wide + DECAY_ROWS
    chips = FUSED_CHIPS
    dma = pltpu.SemaphoreType.DMA
    y, cconv, decays, incoming = pl.pallas_call(
        fused_kernel,
        in_specs=[anywhere] * 3 + [near] * 7,
        out_specs=[near] * 4,
        out_shape=[
            pltpu.VMEM((rows, inner), f32), pltpu.VMEM((rows, wide), bf16),
            pltpu.VMEM((rows, inner), f32), pltpu.VMEM((pairs, wide, LANES), bf16),
        ],
        scratch_shapes=[
            pltpu.VMEM((PAD + rows, inner), bf16), pltpu.VMEM((PAD + rows, wide), bf16),
            pltpu.VMEM((PAD + rows, wide), bf16), pltpu.VMEM((rows, inner), bf16),
            pltpu.VMEM((rows, wide), bf16), pltpu.VMEM((chunks, CHUNK, LANES), f32),
            pltpu.VMEM((chunks, LANES, CHUNK), f32), pltpu.VMEM((2 * heads, inner), bf16),
            pltpu.VMEM((8, inner), f32), pltpu.VMEM((chunks, inner), f32),
            pltpu.VMEM((DECAY_ROWS, inner), bf16), pltpu.VMEM((rows, heads), bf16),
            pltpu.VMEM((rows, 2 * heads), bf16), pltpu.VMEM((wide, rows), bf16),
            pltpu.VMEM((chunks, wide, inner), bf16), pltpu.VMEM((2, ROWS + PAD, LANES), f32),
            pltpu.VMEM((pairs, tall, LANES), bf16), pltpu.VMEM((half, tall, LANES), bf16),
            pltpu.VMEM((chips, tall, LANES), bf16), pltpu.VMEM((chips, tall, LANES), bf16),
            pltpu.VMEM((chips, wide, LANES), bf16), pltpu.VMEM((chips, wide, LANES), bf16),
            pltpu.VMEM((half, wide, LANES), bf16), pltpu.VMEM((half, wide, LANES), bf16),
            dma((pairs // 2,)), dma((2,)), dma((3,)), dma((3,)), dma((half // 2,)),
            dma((half // 2,)), dma((chips,)), dma((chips,)), dma((chips,)), dma((chips,)),
            dma((1,)), dma((1,)),
        ],
        compiler_params=pltpu.CompilerParams(
            vmem_limit_bytes=FUSED_VMEM, collective_id=0, has_side_effects=True
        ),
        name="fused_mixer",
    )(inner_x, input_map, output_map, raw, kernel_x, kernel_b, kernel_c, rate, bias, gain)
    return pl.pallas_call(
        output_kernel,
        grid=(chunks,),
        in_specs=[near] * 4,
        out_specs=pl.BlockSpec((CHUNK, inner), lambda q: (q, 0)),
        out_shape=jax.ShapeDtypeStruct((rows, inner), bf16),
        compiler_params=pltpu.CompilerParams(vmem_limit_bytes=OUTPUT_VMEM),
        name="output_rows",
    )(y, cconv, decays, incoming)


FUSED_VMEM = 36 << 20
OUTPUT_VMEM = 16 << 20


def on_device(
    inner_x, input_map, output_map, step_raw, kernel_x, kernel_b, kernel_c, log_rate, step_bias,
    skip_gain,
):
    rows, inner = inner_x.shape
    heads = log_rate.shape[0]
    members = lax.axis_size("seq")
    if members == 2 * FUSED_CHIPS and inner == members * LANES and rows % ROWS == 0:
        return fused(
            inner_x, input_map, output_map, step_raw.T, kernel_x, kernel_b, kernel_c,
            log_rate[None, :], step_bias[None, :], skip_gain[None, :],
        )
    last = jnp.concatenate([a[rows - HALO :] for a in (inner_x, input_map, output_map)], axis=1)
    tail = lax.ppermute(last, "seq", [(i, i + 1) for i in range(members - 1)])
    xconv, bc, aux, prefix, run = local_states(
        inner_x, input_map, output_map, step_raw, tail, kernel_x, kernel_b, kernel_c,
        log_rate[None, :], step_bias[None, :],
    )
    gain = jnp.repeat(skip_gain, inner // heads)[None, :]
    half = rows // CHUNK // 2
    got = exchange(regroup(run, members))
    ya = local_mix(0, half, xconv, bc, aux, prefix, gain)
    got, ya = lax.optimization_barrier((got, ya))
    back = exchange(scan_members(got))
    yb = local_mix(half, half, xconv, bc, aux, prefix, gain)
    incoming = regroup(back, inner // LANES)
    return finish(heads, ya, yb, bc, aux, incoming)


def solution(mesh):
    split = P(("groups", "seq"), None)
    return jax.shard_map(
        on_device, mesh=mesh, in_specs=(split,) * 4 + (P(),) * 6, out_specs=split, check_vma=False
    )
```

```python
import functools

import jax
import jax.numpy as jnp
from jax import lax
from jax.experimental import pallas as pl
from jax.experimental.pallas import tpu as pltpu
from jax.sharding import PartitionSpec as P

CHUNK = 128
ROWS = 256
LANES = 128
LOG2E = 1.4426950408889634
HALO = 8
VMEM_LIMIT = 60 << 20
DECAY_ROWS = 16


def split_low(value):
    high = value.astype(jnp.bfloat16)
    return high, (value - high.astype(jnp.float32)).astype(jnp.bfloat16)


def silu(value):
    half = 0.5 * value
    return half + half * jnp.tanh(half)


def expander(heads, width, parts):
    shape = (parts * heads, heads * width)
    row = lax.broadcasted_iota(jnp.int32, shape, 0) % heads
    col = lax.broadcasted_iota(jnp.int32, shape, 1) // width
    return (row == col).astype(jnp.bfloat16)


def state_kernel(
    heads, x_ref, b_ref, c_ref, raw_ref, tail_ref, kx_ref, kb_ref, kc_ref, rate_ref, bias_ref,
    xconv_ref, bc_ref, aux_ref, prefix_ref, run_ref,
    xwin, bwin, cwin, spread, scaled, expand, state, logrun,
):
    step = pl.program_id(0)
    inner = x_ref.shape[1]
    wide = b_ref.shape[1]
    pairs = inner // LANES

    @pl.when(step == 0)
    def _():
        tail = tail_ref[...].astype(jnp.float32)
        xwin[0:HALO, :] = tail[:, :inner]
        bwin[0:HALO, :] = tail[:, inner : inner + wide]
        cwin[0:HALO, :] = tail[:, inner + wide :]
        expand[...] = expander(heads, inner // heads, 2)
        state[...] = jnp.zeros_like(state)
        logrun[...] = jnp.zeros_like(logrun)

    @pl.when(step > 0)
    def _():
        xwin[0:HALO, :] = xwin[ROWS : ROWS + HALO, :]
        bwin[0:HALO, :] = bwin[ROWS : ROWS + HALO, :]
        cwin[0:HALO, :] = cwin[ROWS : ROWS + HALO, :]

    bwin[HALO:, :] = b_ref[...].astype(jnp.float32)
    cwin[HALO:, :] = c_ref[...].astype(jnp.float32)

    def small_conv(win, taps):
        count = taps.shape[0]
        total = jnp.zeros((ROWS, win.shape[1]), jnp.float32)
        for k in range(count):
            at = HALO - (count - 1) + k
            total = total + taps[k : k + 1, :] * win[at : at + ROWS, :]
        return silu(total).astype(jnp.bfloat16)

    bconv = small_conv(bwin, kb_ref)
    cconv = small_conv(cwin, kc_ref)
    bc_ref[:, :wide] = bconv
    bc_ref[:, wide:] = cconv

    shifted = raw_ref[...] + bias_ref[...]
    dt = jnp.maximum(shifted, 0.0) + jnp.log1p(jnp.exp(-jnp.abs(shifted)))
    logdec = -(jnp.exp(rate_ref[...]) * LOG2E) * dt
    part0, rest = logdec.astype(jnp.bfloat16), None
    rest = logdec - part0.astype(jnp.float32)
    part1 = rest.astype(jnp.bfloat16)
    part2 = (rest - part1.astype(jnp.float32)).astype(jnp.bfloat16)
    row = lax.broadcasted_iota(jnp.int32, (CHUNK, CHUNK), 0)
    col = lax.broadcasted_iota(jnp.int32, (CHUNK, CHUNK), 1)
    lower = (row >= col).astype(jnp.bfloat16)
    parts = jnp.concatenate([part0, part1, part2, jnp.zeros_like(part0)], axis=1)
    logdt = jnp.log(dt) * LOG2E
    totals = []
    for q in range(ROWS // CHUNK):
        span = slice(q * CHUNK, (q + 1) * CHUNK)
        sums = jnp.dot(lower, parts[span], preferred_element_type=jnp.float32)
        cum = sums[:, :heads] + sums[:, heads : 2 * heads] + sums[:, 2 * heads : 3 * heads]
        total = cum[CHUNK - 1 :, :]
        totals.append(total)
        shift = cum - logdt[span]
        run = logrun[...] + cum
        logrun[...] = logrun[...] + total
        aux_ref[span, :] = jnp.concatenate([cum, shift, run, jnp.zeros_like(run)], axis=1)
        high, low = split_low(jnp.exp2(total - shift))
        spread[span, :] = jnp.dot(
            jnp.concatenate([high, low], axis=1), expand[...], preferred_element_type=jnp.float32
        )

    @pl.loop(0, pairs)
    def _(j):
        lanes = pl.ds(pl.multiple_of(j * LANES, LANES), LANES)
        xwin[HALO:, lanes] = x_ref[:, lanes].astype(jnp.float32)
        count = kx_ref.shape[0]
        total = jnp.zeros((ROWS, LANES), jnp.float32)
        for k in range(count):
            at = HALO - (count - 1) + k
            total = total + kx_ref[k : k + 1, lanes] * xwin[at : at + ROWS, lanes]
        xc = silu(total).astype(jnp.bfloat16)
        xconv_ref[:, lanes] = xc
        scaled[:, lanes] = (xc.astype(jnp.float32) * spread[:, lanes]).astype(jnp.bfloat16)

    btrans = bconv.astype(jnp.float32).T.astype(jnp.bfloat16)
    for q in range(ROWS // CHUNK):
        span = slice(q * CHUNK, (q + 1) * CHUNK)
        prefix_ref[q] = state[...].astype(jnp.bfloat16)
        factor = jnp.broadcast_to(jnp.exp2(totals[q]), (8, heads))
        high, low = split_low(factor)
        decay = jnp.dot(
            jnp.concatenate([high, low], axis=1), expand[...], preferred_element_type=jnp.float32
        )[0:1, :]
        state[...] = decay * state[...] + jnp.dot(
            btrans[:, span], scaled[span, :], preferred_element_type=jnp.float32
        )

    @pl.when(step == pl.num_programs(0) - 1)
    def _():
        high, low = split_low(jnp.broadcast_to(jnp.exp2(logrun[...]), (8, heads)))
        zero = jnp.zeros_like(high)
        high = jnp.dot(jnp.concatenate([high, zero], axis=1), expand[...], preferred_element_type=jnp.float32)
        low = jnp.dot(jnp.concatenate([low, zero], axis=1), expand[...], preferred_element_type=jnp.float32)
        both = jnp.concatenate([high, low], axis=0).astype(jnp.bfloat16)
        for j in range(pairs):
            lanes = slice(j * LANES, (j + 1) * LANES)
            run_ref[j, 0 : state.shape[0], :] = state[:, lanes].astype(jnp.bfloat16)
            run_ref[j, state.shape[0] :, :] = both[:, lanes]


def local_states(x, b, c, raw, tail, kx, kb, kc, rate, bias):
    rows, inner = x.shape
    wide = b.shape[1]
    heads = raw.shape[1]
    pairs = inner // LANES
    whole = lambda a: pl.BlockSpec(a.shape, lambda i: (0,) * a.ndim)
    block = lambda w: pl.BlockSpec((ROWS, w), lambda i: (i, 0))
    per = ROWS // CHUNK
    f32, bf16 = jnp.float32, jnp.bfloat16
    return pl.pallas_call(
        functools.partial(state_kernel, heads),
        grid=(rows // ROWS,),
        in_specs=[block(inner), block(wide), block(wide), block(heads), whole(tail), whole(kx),
                  whole(kb), whole(kc), whole(rate), whole(bias)],
        out_specs=[
            block(inner), block(2 * wide), block(LANES),
            pl.BlockSpec((per, wide, inner), lambda i: (i, 0, 0)),
            pl.BlockSpec((pairs, wide + DECAY_ROWS, LANES), lambda i: (0, 0, 0)),
        ],
        out_shape=[
            jax.ShapeDtypeStruct((rows, inner), bf16),
            jax.ShapeDtypeStruct((rows, 2 * wide), bf16),
            jax.ShapeDtypeStruct((rows, LANES), f32),
            jax.ShapeDtypeStruct((rows // CHUNK, wide, inner), bf16),
            jax.ShapeDtypeStruct((pairs, wide + DECAY_ROWS, LANES), bf16),
        ],
        scratch_shapes=[
            pltpu.VMEM((ROWS + HALO, inner), f32), pltpu.VMEM((ROWS + HALO, wide), f32),
            pltpu.VMEM((ROWS + HALO, wide), f32), pltpu.VMEM((ROWS, inner), f32),
            pltpu.VMEM((ROWS, inner), bf16), pltpu.VMEM((2 * heads, inner), bf16),
            pltpu.VMEM((wide, inner), f32), pltpu.VMEM((1, heads), f32),
        ],
        compiler_params=pltpu.CompilerParams(vmem_limit_bytes=VMEM_LIMIT),
        cost_estimate=pl.CostEstimate(flops=2 * 10**9, bytes_accessed=12 << 20, transcendentals=1 << 21),
        name="local_states",
    )(x, b, c, raw, tail, kx, kb, kc, rate, bias)


def inner_kernel(heads, xconv_ref, bc_ref, aux_ref, prefix_ref, gain_ref, y_ref):
    wide = bc_ref.shape[1] // 2
    pairs = xconv_ref.shape[1] // LANES
    aux = aux_ref[...]
    turned = aux.T
    bconv, cconv = bc_ref[:, :wide], bc_ref[:, wide:]
    row = lax.broadcasted_iota(jnp.int32, (CHUNK, CHUNK), 0)
    col = lax.broadcasted_iota(jnp.int32, (CHUNK, CHUNK), 1)
    gram = lax.dot_general(cconv, bconv, (((1,), (1,)), ((), ())), preferred_element_type=jnp.float32)
    gram = jnp.where(row >= col, gram, 0.0)
    left = lax.broadcasted_iota(jnp.int32, (CHUNK, LANES), 1) < LANES // 2
    for j in range(pairs):
        lanes = slice(j * LANES, (j + 1) * LANES)
        xc = xconv_ref[:, lanes]
        weights = []
        cums = []
        for h in (2 * j, 2 * j + 1):
            cum = jnp.broadcast_to(aux[:, h : h + 1], (CHUNK, CHUNK))
            cums.append(cum)
            power = jnp.minimum(cum - turned[heads + h : heads + h + 1, :], 126.0)
            weights.append((gram * jnp.exp2(power)).astype(jnp.bfloat16))
        zero = jnp.zeros_like(xc)
        both = jnp.concatenate([jnp.where(left, xc, zero), jnp.where(left, zero, xc)], axis=0)
        inner = jnp.dot(jnp.concatenate(weights, axis=1), both, preferred_element_type=jnp.float32)
        carried = jnp.dot(cconv, prefix_ref[0, :, lanes], preferred_element_type=jnp.float32)
        decay = jnp.exp2(jnp.where(left, cums[0], cums[1]))
        y_ref[:, lanes] = inner + decay * carried + gain_ref[:, lanes] * xc.astype(jnp.float32)


def local_mix(first, count, xconv, bc, aux, prefix, gain):
    inner = xconv.shape[1]
    heads = gain.shape[1] // 64
    wide = bc.shape[1] // 2
    block = lambda w: pl.BlockSpec((CHUNK, w), lambda i: (i + first, 0))
    return pl.pallas_call(
        functools.partial(inner_kernel, heads),
        grid=(count,),
        in_specs=[block(inner), block(2 * wide), block(LANES),
                  pl.BlockSpec((1, wide, inner), lambda i: (i + first, 0, 0)),
                  pl.BlockSpec((1, inner), lambda i: (0, 0))],
        out_specs=pl.BlockSpec((CHUNK, inner), lambda i: (i, 0)),
        out_shape=jax.ShapeDtypeStruct((count * CHUNK, inner), jnp.float32),
        compiler_params=pltpu.CompilerParams(vmem_limit_bytes=VMEM_LIMIT),
        cost_estimate=pl.CostEstimate(flops=10**10, bytes_accessed=24 << 20, transcendentals=1 << 22),
        name="local_mix",
    )(xconv, bc, aux, prefix, gain)


def scan_kernel(got_ref, out_ref):
    members, rows, width = out_ref.shape
    entering = jnp.zeros((rows, width), jnp.float32)
    for k in range(members):
        out_ref[k] = entering.astype(jnp.bfloat16)
        decay = got_ref[k, rows : rows + 1, :].astype(jnp.float32) + got_ref[
            k, rows + 8 : rows + 9, :
        ].astype(jnp.float32)
        entering = decay * entering + got_ref[k, 0:rows, :].astype(jnp.float32)


def scan_members(got):
    members, rows, width = got.shape
    return pl.pallas_call(
        scan_kernel,
        out_shape=jax.ShapeDtypeStruct((members, rows - DECAY_ROWS, width), jnp.bfloat16),
        compiler_params=pltpu.CompilerParams(vmem_limit_bytes=VMEM_LIMIT),
        name="scan_members",
    )(got)


def finish_kernel(heads, ya_ref, yb_ref, bc_ref, aux_ref, inc_ref, out_ref, expand):
    wide = bc_ref.shape[1] // 2
    pairs = out_ref.shape[1] // LANES

    @pl.when(pl.program_id(0) == 0)
    def _():
        expand[...] = expander(heads, out_ref.shape[1] // heads, 2)

    high, low = split_low(jnp.exp2(aux_ref[:, 2 * heads : 3 * heads]))
    factors = jnp.concatenate([high, low], axis=1)
    cconv = bc_ref[:, wide:]
    early = pl.program_id(0) < pl.num_programs(0) // 2

    def emit(y_ref):
        for j in range(pairs):
            lanes = slice(j * LANES, (j + 1) * LANES)
            decay = jnp.dot(factors, expand[:, lanes], preferred_element_type=jnp.float32)
            carried = jnp.dot(cconv, inc_ref[j], preferred_element_type=jnp.float32)
            out_ref[:, lanes] = (y_ref[:, lanes] + decay * carried).astype(jnp.bfloat16)

    @pl.when(early)
    def _():
        emit(ya_ref)

    @pl.when(jnp.logical_not(early))
    def _():
        emit(yb_ref)


def finish(heads, ya, yb, bc, aux, inc):
    rows, inner = bc.shape[0], ya.shape[1]
    wide = bc.shape[1] // 2
    steps = rows // CHUNK
    half = steps // 2
    block = lambda w: pl.BlockSpec((CHUNK, w), lambda i: (i, 0))
    return pl.pallas_call(
        functools.partial(finish_kernel, heads),
        grid=(steps,),
        in_specs=[
            pl.BlockSpec((CHUNK, inner), lambda i: (jnp.minimum(i, half - 1), 0)),
            pl.BlockSpec((CHUNK, inner), lambda i: (jnp.maximum(i - half, 0), 0)),
            block(2 * wide), block(LANES), pl.BlockSpec(inc.shape, lambda i: (0, 0, 0)),
        ],
        out_specs=block(inner),
        out_shape=jax.ShapeDtypeStruct((rows, inner), jnp.bfloat16),
        scratch_shapes=[pltpu.VMEM((2 * heads, inner), jnp.bfloat16)],
        compiler_params=pltpu.CompilerParams(vmem_limit_bytes=VMEM_LIMIT),
        name="finish",
    )(ya, yb, bc, aux, inc)


def exchange(x):
    return lax.all_to_all(x, "seq", split_axis=0, concat_axis=0, tiled=True)


def regroup(x, count):
    groups, rows, width = x.shape
    if groups == count:
        return x
    flat = x.transpose(1, 0, 2).reshape(rows, groups * width)
    return flat.reshape(rows, count, groups * width // count).transpose(1, 0, 2)


FUSED_CHIPS = 8
PAD = 16
QUAD = 2 * LANES
BIG = 1e38


def fused_kernel(
    x_hbm, b_hbm, c_hbm, raw_hbm, kx_hbm, kb_hbm, kc_hbm, rate_hbm, bias_hbm, gain_hbm,
    y, cconv, decays, incoming,
    raw_ref, kx_ref, kb_ref, kc_ref, rate_ref, bias_ref, gain_ref,
    xbuf, bbuf, cbuf, xc, bconv, aux, turned, expand, gains, falls, ends, factors, grown, btrans, prefix, window,
    run, core_got, chip_sum, got, entered, back, core_out, arrived,
    load_sem, small_sem, param_sem, tail_send, tail_recv, core_send, core_recv,
    give_send, give_recv, take_send, take_recv, last_send, last_recv,
):
    f32, bf16 = jnp.float32, jnp.bfloat16
    members = 2 * FUSED_CHIPS
    me = lax.axis_index("seq")
    chip, core = me // 2, me % 2
    partner = chip * 2 + 1 - core
    first_core = core == 0
    rows, inner = xc.shape
    wide = bconv.shape[1]
    heads = rate_ref.shape[1]
    pairs = inner // LANES
    blocks = rows // ROWS
    chunks = rows // CHUNK
    half = pairs // 2
    steps = pairs // 2

    def place(i):
        k = i // 2
        m = (k * 2) % 4 + (k * 2) // 4
        mine = i % 2
        owner = mine * core + (1 - mine) * (1 - core)
        return m, owner * (half // 2) + m

    def quad_lanes(i):
        return pl.ds(pl.multiple_of(place(i)[1] * QUAD, QUAD), QUAD)

    def load(i):
        lanes = quad_lanes(i)
        return pltpu.make_async_copy(
            x_hbm.at[:, lanes], xbuf.at[pl.ds(PAD, rows), lanes], load_sem.at[i]
        )

    small = [
        pltpu.make_async_copy(b_hbm, bbuf.at[pl.ds(PAD, rows)], small_sem.at[0]),
        pltpu.make_async_copy(c_hbm, cbuf.at[pl.ds(PAD, rows)], small_sem.at[1]),
    ]
    params = [
        pltpu.make_async_copy(src, dst, param_sem.at[i])
        for i, (src, dst) in enumerate((
            (rate_hbm, rate_ref), (bias_hbm, bias_ref), (gain_hbm, gain_ref), (raw_hbm, raw_ref),
            (kx_hbm, kx_ref), (kb_hbm, kb_ref), (kc_hbm, kc_ref),
        ))
    ]
    for copy in params + small[:1]:
        copy.start()
    for i in range(steps):
        load(i).start()
    small[1].start()

    barrier = pltpu.get_barrier_semaphore()
    for off in range(1, members):
        pl.semaphore_signal(
            barrier, inc=1, device_id={"seq": lax.rem(me + off, members)},
            device_id_type=pl.DeviceIdType.MESH,
        )

    def remote(src, dst, send, recv, to):
        return pltpu.make_async_remote_copy(
            src_ref=src, dst_ref=dst, send_sem=send, recv_sem=recv, device_id={"seq": to},
            device_id_type=pl.DeviceIdType.MESH,
        )

    after = lax.rem(me + 1, members)
    tails = [
        remote(h.at[pl.ds(rows - PAD, PAD)], v.at[pl.ds(0, PAD)], tail_send.at[i], tail_recv.at[i], after)
        for i, (h, v) in enumerate(((x_hbm, xbuf), (b_hbm, bbuf), (c_hbm, cbuf)))
    ]

    expand[...] = expander(heads, inner // heads, 2)
    for copy in params:
        copy.wait()
    high, middle = split_low(jnp.broadcast_to(gain_ref[...], (8, heads)))
    low = (gain_ref[...] - high.astype(f32) - middle.astype(f32)).astype(bf16)
    gains[...] = jnp.dot(
        jnp.concatenate([high, middle], axis=1), expand[...], preferred_element_type=f32
    ) + jnp.dot(
        jnp.concatenate([low, jnp.zeros_like(low)], axis=1), expand[...], preferred_element_type=f32
    )
    row = lax.broadcasted_iota(jnp.int32, (CHUNK, CHUNK), 0)
    col = lax.broadcasted_iota(jnp.int32, (CHUNK, CHUNK), 1)
    turns = jnp.concatenate([rate_ref[...], bias_ref[...], rate_ref[...], bias_ref[...]], axis=1)
    turns = jnp.broadcast_to(turns, (CHUNK, CHUNK)).T
    speed = jnp.exp(turns[:heads]) * LOG2E
    bias = turns[heads : 2 * heads]
    upper = (row <= col).astype(bf16)
    log_before = jnp.zeros((heads, CHUNK), f32)
    chunk_falls = []
    for q in range(chunks):
        span = slice(q * CHUNK, (q + 1) * CHUNK)
        shifted = raw_ref[:, span] + bias
        dt = jnp.maximum(shifted, 0.0) + jnp.log1p(jnp.exp(-jnp.abs(shifted)))
        logdec = -speed * dt
        part0 = logdec.astype(bf16)
        rest = logdec - part0.astype(f32)
        part1 = rest.astype(bf16)
        part2 = (rest - part1.astype(f32)).astype(bf16)
        sums = jnp.dot(
            jnp.concatenate([part0, part1, part2], axis=0), upper, preferred_element_type=f32
        )
        cum = sums[:heads] + sums[heads : 2 * heads] + sums[2 * heads :]
        total = jnp.broadcast_to(cum[:, CHUNK - 1 :], cum.shape)
        shift = cum - jnp.log(dt) * LOG2E
        flat = jnp.concatenate(
            [cum, shift, jnp.exp2(log_before + cum), jnp.exp2(total - shift)], axis=0
        )
        log_before = log_before + total
        stood = flat.T
        turned[q] = flat
        aux[q] = stood
        factors[span, :] = stood[:, 3 * heads :].astype(bf16)
        high, low = split_low(stood[:, 2 * heads : 3 * heads])
        grown[span, :] = jnp.concatenate([high, low], axis=1)
        chunk_falls.append(jnp.exp2(stood[CHUNK - 1 :, :heads]))
    high, low = split_low(jnp.concatenate(chunk_falls, axis=0))
    falls[...] = jnp.dot(
        jnp.concatenate([high, low], axis=1), expand[...], preferred_element_type=f32
    )
    high, low = split_low(
        jnp.broadcast_to(stood[CHUNK - 1 :, 2 * heads : 3 * heads], (8, heads))
    )
    zero = jnp.zeros_like(high)
    high = jnp.dot(jnp.concatenate([high, zero], axis=1), expand[...], preferred_element_type=f32)
    low = jnp.dot(jnp.concatenate([low, zero], axis=1), expand[...], preferred_element_type=f32)
    ends[...] = jnp.concatenate([high, low], axis=0).astype(bf16)
    pl.semaphore_wait(barrier, members - 1)

    @pl.when(me < members - 1)
    def _():
        for copy in tails:
            copy.start()

    def convolve(buf, taps_ref, out, block, lanes, slot):
        slot[...] = buf[block * ROWS : block * ROWS + ROWS + PAD, lanes].astype(f32)
        taps = 0.5 * taps_ref[:, lanes]
        count = taps.shape[0]
        total = taps[0:1] * slot[PAD - count + 1 : PAD - count + 1 + ROWS, :]
        for k in range(1, count):
            at = PAD - count + 1 + k
            total = total + taps[k : k + 1] * slot[at : at + ROWS, :]
        out[block * ROWS : (block + 1) * ROWS, lanes] = (total + total * jnp.tanh(total)).astype(bf16)

    def convolve_quad(i, block):
        for part in range(2):
            lanes = pl.ds(pl.multiple_of(place(i)[1] * QUAD + part * LANES, LANES), LANES)
            convolve(xbuf, kx_ref, xc, block, lanes, window.at[part])

    everything = slice(0, LANES)

    def early(i):
        load(i).wait()

        @pl.loop(1, blocks)
        def _(block):
            at = pl.multiple_of(block * ROWS, ROWS)
            for part in range(2):
                lanes = pl.ds(pl.multiple_of(place(i)[1] * QUAD + part * LANES, LANES), LANES)
                slot = window.at[part]
                slot[...] = xbuf[pl.ds(at, ROWS + PAD), lanes].astype(f32)
                taps = 0.5 * kx_ref[:, lanes]
                count = taps.shape[0]
                total = taps[0:1] * slot[PAD - count + 1 : PAD - count + 1 + ROWS, :]
                for k in range(1, count):
                    to = PAD - count + 1 + k
                    total = total + taps[k : k + 1] * slot[to : to + ROWS, :]
                xc[pl.ds(at, ROWS), lanes] = (total + total * jnp.tanh(total)).astype(bf16)

    small[0].wait()
    for block in range(1, blocks):
        convolve(bbuf, kb_ref, bconv, block, everything, window.at[block % 2])
    early(0)
    early(1)
    small[1].wait()
    for block in range(1, blocks):
        convolve(cbuf, kc_ref, cconv, block, everything, window.at[block % 2])

    @pl.when(me > 0)
    def _():
        for copy in tails:
            copy.wait_recv()

    @pl.when(me == 0)
    def _():
        xbuf[0:PAD, :] = jnp.zeros((PAD, inner), bf16)
        bbuf[0:PAD, :] = jnp.zeros((PAD, wide), bf16)
        cbuf[0:PAD, :] = jnp.zeros((PAD, wide), bf16)

    convolve(bbuf, kb_ref, bconv, 0, everything, window.at[0])
    convolve(cbuf, kc_ref, cconv, 0, everything, window.at[1])
    for block in range(blocks):
        span = slice(block * ROWS, (block + 1) * ROWS)
        btrans[:, span] = bconv[span, :].astype(f32).T.astype(bf16)

    def quad_state(i):
        lanes = quad_lanes(i)
        first = place(i)[1] * 2
        held = jnp.zeros((wide, QUAD), f32)
        for q in range(chunks):
            span = slice(q * CHUNK, (q + 1) * CHUNK)
            spread = jnp.dot(factors[span, :], expand[:heads, lanes], preferred_element_type=f32)
            scaled = xc[span, lanes] * spread.astype(bf16)
            prefix[q, :, lanes] = held.astype(bf16)
            held = falls[q : q + 1, lanes] * held + jnp.dot(
                btrans[:, span], scaled, preferred_element_type=f32
            )
        held = held.astype(bf16)
        tip = ends[:, lanes]
        for part in range(2):
            piece = slice(part * LANES, (part + 1) * LANES)
            run[first + part, 0:wide, :] = held[:, piece]
            run[first + part, wide:, :] = tip[:, piece]

    def to_core(m):
        return remote(
            run.at[pl.ds((1 - core) * half + 2 * m, 2)], core_got.at[pl.ds(2 * m, 2)],
            core_send.at[m], core_recv.at[m], partner,
        )

    def give(other):
        return remote(
            chip_sum.at[other], got.at[chip], give_send.at[other], give_recv.at[chip],
            other * 2 + core,
        )

    def given(other):
        return remote(
            chip_sum.at[other], got.at[other], give_send.at[other], give_recv.at[other],
            other * 2 + core,
        )

    def take(other):
        return remote(
            entered.at[other], back.at[chip], take_send.at[other], take_recv.at[chip],
            other * 2 + core,
        )

    def taken(other):
        return remote(
            entered.at[other], back.at[other], take_send.at[other], take_recv.at[other],
            other * 2 + core,
        )

    def last():
        return remote(
            core_out, arrived, last_send.at[0], last_recv.at[0], partner,
        )

    def decay_of(piece):
        return piece[wide : wide + 1].astype(f32) + piece[wide + 8 : wide + 9].astype(f32)

    def add_cores(m):
        to_core(m).wait_recv()
        for part in range(2):
            j = 2 * m + part
            mine, other = run[core * half + j], core_got[j]
            lead = jnp.where(first_core, mine.astype(f32), other.astype(f32))
            trail = jnp.where(first_core, other.astype(f32), mine.astype(f32))
            fall = trail[wide : wide + 1] + trail[wide + 8 : wide + 9]
            whole = (lead[wide : wide + 1] + lead[wide + 8 : wide + 9]) * fall
            high, low = split_low(jnp.broadcast_to(whole, (8, LANES)))
            chip_sum[j, 0:wide, :] = (fall * lead[:wide] + trail[:wide]).astype(bf16)
            chip_sum[j, wide:, :] = jnp.concatenate(
                [high.astype(f32), low.astype(f32)], axis=0
            ).astype(bf16)

            @pl.when(j != chip)
            def _():
                give(j).start()

            @pl.when(j == chip)
            def _():
                got[chip] = chip_sum[chip]

    def others(act):
        for k in range(FUSED_CHIPS):

            @pl.when(k != chip)
            def _():
                act(k)

    def scan_chips():
        others(lambda k: given(k).wait_recv())
        value = jnp.zeros((wide, LANES), f32)
        for k in range(FUSED_CHIPS):
            entered[k] = value.astype(bf16)
            if k < FUSED_CHIPS - 1:
                piece = got[k]
                value = decay_of(piece) * value + piece[:wide].astype(f32)
        others(lambda k: take(k).start())
        back[chip] = entered[chip]

    def split_cores():
        others(lambda k: taken(k).wait_recv())
        for j in range(half):
            lead = jnp.where(
                first_core, run[core * half + j].astype(f32), core_got[j].astype(f32)
            )
            entering = back[j].astype(f32)
            fall = lead[wide : wide + 1] + lead[wide + 8 : wide + 9]
            later = fall * entering + lead[:wide]
            core_out[j] = jnp.where(first_core, later, entering).astype(bf16)
            incoming[core * half + j] = jnp.where(first_core, entering, later).astype(bf16)
        last().start()

    @pl.loop(0, steps)
    def _(i):
        convolve_quad(i, 0)
        quad_state(i)
        m = place(i)[0]

        @pl.when(i % 2 == 0)
        def _():
            to_core(m).start()

        @pl.when(i + 2 < steps)
        def _():
            early(i + 2)

        @pl.when(i % 2 == 1)
        def _():
            add_cores(m)

    @pl.when(me < members - 1)
    def _():
        for copy in tails:
            copy.wait_send()

    left = lax.broadcasted_iota(jnp.int32, (CHUNK, LANES), 1) < LANES // 2

    @pl.loop(0, chunks)
    def _(q):
        at = pl.ds(pl.multiple_of(q * CHUNK, CHUNK), CHUNK)
        cc = cconv[at, :]
        gram = lax.dot_general(
            cc, bconv[at, :], (((1,), (1,)), ((), ())), preferred_element_type=f32
        )
        gram = jnp.where(row >= col, gram, 0.0).astype(bf16)
        for g in range(pairs // 2):
            wider = slice(g * QUAD, (g + 1) * QUAD)
            carried = jnp.dot(cc, prefix[q, :, wider], preferred_element_type=f32)
            for part in range(2):
                j = 2 * g + part
                lanes = slice(j * LANES, (j + 1) * LANES)
                values = xc[at, lanes]
                weights, cums = [], []
                for h in (2 * j, 2 * j + 1):
                    cum = jnp.broadcast_to(aux[q, :, h : h + 1], (CHUNK, CHUNK))
                    cums.append(cum)
                    grow = jnp.exp2(cum - turned[q, heads + h : heads + h + 1, :]).astype(bf16)
                    weights.append(gram * jnp.minimum(grow, jnp.asarray(BIG, bf16)))
                zero = jnp.zeros_like(values)
                both = jnp.concatenate(
                    [jnp.where(left, values, zero), jnp.where(left, zero, values)], axis=0
                )
                mixed = jnp.dot(jnp.concatenate(weights, axis=1), both, preferred_element_type=f32)
                decay = jnp.exp2(jnp.where(left, cums[0], cums[1]))
                y[at, lanes] = (
                    mixed + decay * carried[:, part * LANES : (part + 1) * LANES]
                    + gains[0:1, lanes] * values.astype(f32)
                )

        @pl.when(q == SCAN_AT)
        def _():
            scan_chips()

        @pl.when(q == SPLIT_AT)
        def _():
            split_cores()

    @pl.loop(0, chunks)
    def _(q):
        at = pl.ds(pl.multiple_of(q * CHUNK, CHUNK), CHUNK)
        for g in range(pairs // 2):
            wider = slice(g * QUAD, (g + 1) * QUAD)
            decays[at, wider] = jnp.dot(grown[at, :], expand[:, wider], preferred_element_type=f32)

    for m in range(half // 2):
        to_core(m).wait_send()
    others(lambda k: give(k).wait_send())
    others(lambda k: take(k).wait_send())
    last().wait()
    incoming[pl.ds((1 - core) * half, half)] = arrived[...]


SCAN_AT = 3
SPLIT_AT = 7


def output_kernel(y_ref, c_ref, decay_ref, inc_ref, out_ref):
    q = pl.program_id(0)
    at = pl.ds(pl.multiple_of(q * CHUNK, CHUNK), CHUNK)
    cc = c_ref[at, :]
    for g in range(inc_ref.shape[0] // 2):
        wider = slice(g * QUAD, (g + 1) * QUAD)
        entering = jnp.concatenate([inc_ref[2 * g], inc_ref[2 * g + 1]], axis=1)
        carried = jnp.dot(cc, entering, preferred_element_type=jnp.float32)
        out_ref[:, wider] = (y_ref[at, wider] + decay_ref[at, wider] * carried).astype(jnp.bfloat16)


def fused(inner_x, input_map, output_map, raw, kernel_x, kernel_b, kernel_c, rate, bias, gain):
    rows, inner = inner_x.shape
    wide = input_map.shape[1]
    heads = rate.shape[1]
    pairs = inner // LANES
    half = pairs // 2
    chunks = rows // CHUNK
    f32, bf16 = jnp.float32, jnp.bfloat16
    far = pl.BlockSpec(memory_space=pltpu.HBM)
    near = pl.BlockSpec(memory_space=pltpu.VMEM)
    tall = wide + DECAY_ROWS
    chips = FUSED_CHIPS
    dma = pltpu.SemaphoreType.DMA
    y, cconv, decays, incoming = pl.pallas_call(
        fused_kernel,
        in_specs=[far] * 10,
        out_specs=[near] * 4,
        out_shape=[
            pltpu.VMEM((rows, inner), f32), pltpu.VMEM((rows, wide), bf16),
            pltpu.VMEM((rows, inner), f32), pltpu.VMEM((pairs, wide, LANES), bf16),
        ],
        scratch_shapes=[
            pltpu.VMEM(raw.shape, f32), pltpu.VMEM(kernel_x.shape, f32),
            pltpu.VMEM(kernel_b.shape, f32), pltpu.VMEM(kernel_c.shape, f32),
            pltpu.VMEM(rate.shape, f32), pltpu.VMEM(bias.shape, f32), pltpu.VMEM(gain.shape, f32),
            pltpu.VMEM((PAD + rows, inner), bf16), pltpu.VMEM((PAD + rows, wide), bf16),
            pltpu.VMEM((PAD + rows, wide), bf16), pltpu.VMEM((rows, inner), bf16),
            pltpu.VMEM((rows, wide), bf16), pltpu.VMEM((chunks, CHUNK, LANES), f32),
            pltpu.VMEM((chunks, LANES, CHUNK), f32), pltpu.VMEM((2 * heads, inner), bf16),
            pltpu.VMEM((8, inner), f32), pltpu.VMEM((chunks, inner), f32),
            pltpu.VMEM((DECAY_ROWS, inner), bf16), pltpu.VMEM((rows, heads), bf16),
            pltpu.VMEM((rows, 2 * heads), bf16), pltpu.VMEM((wide, rows), bf16),
            pltpu.VMEM((chunks, wide, inner), bf16), pltpu.VMEM((2, ROWS + PAD, LANES), f32),
            pltpu.VMEM((pairs, tall, LANES), bf16), pltpu.VMEM((half, tall, LANES), bf16),
            pltpu.VMEM((chips, tall, LANES), bf16), pltpu.VMEM((chips, tall, LANES), bf16),
            pltpu.VMEM((chips, wide, LANES), bf16), pltpu.VMEM((chips, wide, LANES), bf16),
            pltpu.VMEM((half, wide, LANES), bf16), pltpu.VMEM((half, wide, LANES), bf16),
            dma((pairs // 2,)), dma((2,)), dma((7,)), dma((3,)), dma((3,)), dma((half // 2,)),
            dma((half // 2,)), dma((chips,)), dma((chips,)), dma((chips,)), dma((chips,)),
            dma((1,)), dma((1,)),
        ],
        compiler_params=pltpu.CompilerParams(
            vmem_limit_bytes=FUSED_VMEM, collective_id=0, has_side_effects=True
        ),
        name="fused_mixer",
    )(inner_x, input_map, output_map, raw, kernel_x, kernel_b, kernel_c, rate, bias, gain)
    return pl.pallas_call(
        output_kernel,
        grid=(chunks,),
        in_specs=[near] * 4,
        out_specs=pl.BlockSpec((CHUNK, inner), lambda q: (q, 0)),
        out_shape=jax.ShapeDtypeStruct((rows, inner), bf16),
        compiler_params=pltpu.CompilerParams(vmem_limit_bytes=OUTPUT_VMEM),
        name="output_rows",
    )(y, cconv, decays, incoming)


FUSED_VMEM = (47 << 20) + (160 << 10)
OUTPUT_VMEM = 16 << 20


def on_device(
    inner_x, input_map, output_map, step_raw, kernel_x, kernel_b, kernel_c, log_rate, step_bias,
    skip_gain,
):
    rows, inner = inner_x.shape
    heads = log_rate.shape[0]
    members = lax.axis_size("seq")
    if members == 2 * FUSED_CHIPS and inner == members * LANES and rows % ROWS == 0:
        return fused(
            inner_x, input_map, output_map, step_raw.T, kernel_x, kernel_b, kernel_c,
            log_rate[None, :], step_bias[None, :], skip_gain[None, :],
        )
    last = jnp.concatenate([a[rows - HALO :] for a in (inner_x, input_map, output_map)], axis=1)
    tail = lax.ppermute(last, "seq", [(i, i + 1) for i in range(members - 1)])
    xconv, bc, aux, prefix, run = local_states(
        inner_x, input_map, output_map, step_raw, tail, kernel_x, kernel_b, kernel_c,
        log_rate[None, :], step_bias[None, :],
    )
    gain = jnp.repeat(skip_gain, inner // heads)[None, :]
    half = rows // CHUNK // 2
    got = exchange(regroup(run, members))
    ya = local_mix(0, half, xconv, bc, aux, prefix, gain)
    got, ya = lax.optimization_barrier((got, ya))
    back = exchange(scan_members(got))
    yb = local_mix(half, half, xconv, bc, aux, prefix, gain)
    incoming = regroup(back, inner // LANES)
    return finish(heads, ya, yb, bc, aux, incoming)


def solution(mesh):
    split = P(("groups", "seq"), None)
    return jax.shard_map(
        on_device, mesh=mesh, in_specs=(split,) * 4 + (P(),) * 6, out_specs=split, check_vma=False
    )
```

```python
import functools

import jax
import jax.numpy as jnp
from jax import lax
from jax.experimental import pallas as pl
from jax.experimental.pallas import tpu as pltpu
from jax.sharding import PartitionSpec as P

CHUNK = 128
ROWS = 256
LANES = 128
LOG2E = 1.4426950408889634
HALO = 8
VMEM_LIMIT = 60 << 20
DECAY_ROWS = 16


def split_low(value):
    high = value.astype(jnp.bfloat16)
    return high, (value - high.astype(jnp.float32)).astype(jnp.bfloat16)


def silu(value):
    half = 0.5 * value
    return half + half * jnp.tanh(half)


def expander(heads, width, parts):
    shape = (parts * heads, heads * width)
    row = lax.broadcasted_iota(jnp.int32, shape, 0) % heads
    col = lax.broadcasted_iota(jnp.int32, shape, 1) // width
    return (row == col).astype(jnp.bfloat16)


def state_kernel(
    heads, x_ref, b_ref, c_ref, raw_ref, tail_ref, kx_ref, kb_ref, kc_ref, rate_ref, bias_ref,
    xconv_ref, bc_ref, aux_ref, prefix_ref, run_ref,
    xwin, bwin, cwin, spread, scaled, expand, state, logrun,
):
    step = pl.program_id(0)
    inner = x_ref.shape[1]
    wide = b_ref.shape[1]
    pairs = inner // LANES

    @pl.when(step == 0)
    def _():
        tail = tail_ref[...].astype(jnp.float32)
        xwin[0:HALO, :] = tail[:, :inner]
        bwin[0:HALO, :] = tail[:, inner : inner + wide]
        cwin[0:HALO, :] = tail[:, inner + wide :]
        expand[...] = expander(heads, inner // heads, 2)
        state[...] = jnp.zeros_like(state)
        logrun[...] = jnp.zeros_like(logrun)

    @pl.when(step > 0)
    def _():
        xwin[0:HALO, :] = xwin[ROWS : ROWS + HALO, :]
        bwin[0:HALO, :] = bwin[ROWS : ROWS + HALO, :]
        cwin[0:HALO, :] = cwin[ROWS : ROWS + HALO, :]

    bwin[HALO:, :] = b_ref[...].astype(jnp.float32)
    cwin[HALO:, :] = c_ref[...].astype(jnp.float32)

    def small_conv(win, taps):
        count = taps.shape[0]
        total = jnp.zeros((ROWS, win.shape[1]), jnp.float32)
        for k in range(count):
            at = HALO - (count - 1) + k
            total = total + taps[k : k + 1, :] * win[at : at + ROWS, :]
        return silu(total).astype(jnp.bfloat16)

    bconv = small_conv(bwin, kb_ref)
    cconv = small_conv(cwin, kc_ref)
    bc_ref[:, :wide] = bconv
    bc_ref[:, wide:] = cconv

    shifted = raw_ref[...] + bias_ref[...]
    dt = jnp.maximum(shifted, 0.0) + jnp.log1p(jnp.exp(-jnp.abs(shifted)))
    logdec = -(jnp.exp(rate_ref[...]) * LOG2E) * dt
    part0, rest = logdec.astype(jnp.bfloat16), None
    rest = logdec - part0.astype(jnp.float32)
    part1 = rest.astype(jnp.bfloat16)
    part2 = (rest - part1.astype(jnp.float32)).astype(jnp.bfloat16)
    row = lax.broadcasted_iota(jnp.int32, (CHUNK, CHUNK), 0)
    col = lax.broadcasted_iota(jnp.int32, (CHUNK, CHUNK), 1)
    lower = (row >= col).astype(jnp.bfloat16)
    parts = jnp.concatenate([part0, part1, part2, jnp.zeros_like(part0)], axis=1)
    logdt = jnp.log(dt) * LOG2E
    totals = []
    for q in range(ROWS // CHUNK):
        span = slice(q * CHUNK, (q + 1) * CHUNK)
        sums = jnp.dot(lower, parts[span], preferred_element_type=jnp.float32)
        cum = sums[:, :heads] + sums[:, heads : 2 * heads] + sums[:, 2 * heads : 3 * heads]
        total = cum[CHUNK - 1 :, :]
        totals.append(total)
        shift = cum - logdt[span]
        run = logrun[...] + cum
        logrun[...] = logrun[...] + total
        aux_ref[span, :] = jnp.concatenate([cum, shift, run, jnp.zeros_like(run)], axis=1)
        high, low = split_low(jnp.exp2(total - shift))
        spread[span, :] = jnp.dot(
            jnp.concatenate([high, low], axis=1), expand[...], preferred_element_type=jnp.float32
        )

    @pl.loop(0, pairs)
    def _(j):
        lanes = pl.ds(pl.multiple_of(j * LANES, LANES), LANES)
        xwin[HALO:, lanes] = x_ref[:, lanes].astype(jnp.float32)
        count = kx_ref.shape[0]
        total = jnp.zeros((ROWS, LANES), jnp.float32)
        for k in range(count):
            at = HALO - (count - 1) + k
            total = total + kx_ref[k : k + 1, lanes] * xwin[at : at + ROWS, lanes]
        xc = silu(total).astype(jnp.bfloat16)
        xconv_ref[:, lanes] = xc
        scaled[:, lanes] = (xc.astype(jnp.float32) * spread[:, lanes]).astype(jnp.bfloat16)

    btrans = bconv.astype(jnp.float32).T.astype(jnp.bfloat16)
    for q in range(ROWS // CHUNK):
        span = slice(q * CHUNK, (q + 1) * CHUNK)
        prefix_ref[q] = state[...].astype(jnp.bfloat16)
        factor = jnp.broadcast_to(jnp.exp2(totals[q]), (8, heads))
        high, low = split_low(factor)
        decay = jnp.dot(
            jnp.concatenate([high, low], axis=1), expand[...], preferred_element_type=jnp.float32
        )[0:1, :]
        state[...] = decay * state[...] + jnp.dot(
            btrans[:, span], scaled[span, :], preferred_element_type=jnp.float32
        )

    @pl.when(step == pl.num_programs(0) - 1)
    def _():
        high, low = split_low(jnp.broadcast_to(jnp.exp2(logrun[...]), (8, heads)))
        zero = jnp.zeros_like(high)
        high = jnp.dot(jnp.concatenate([high, zero], axis=1), expand[...], preferred_element_type=jnp.float32)
        low = jnp.dot(jnp.concatenate([low, zero], axis=1), expand[...], preferred_element_type=jnp.float32)
        both = jnp.concatenate([high, low], axis=0).astype(jnp.bfloat16)
        for j in range(pairs):
            lanes = slice(j * LANES, (j + 1) * LANES)
            run_ref[j, 0 : state.shape[0], :] = state[:, lanes].astype(jnp.bfloat16)
            run_ref[j, state.shape[0] :, :] = both[:, lanes]


def local_states(x, b, c, raw, tail, kx, kb, kc, rate, bias):
    rows, inner = x.shape
    wide = b.shape[1]
    heads = raw.shape[1]
    pairs = inner // LANES
    whole = lambda a: pl.BlockSpec(a.shape, lambda i: (0,) * a.ndim)
    block = lambda w: pl.BlockSpec((ROWS, w), lambda i: (i, 0))
    per = ROWS // CHUNK
    f32, bf16 = jnp.float32, jnp.bfloat16
    return pl.pallas_call(
        functools.partial(state_kernel, heads),
        grid=(rows // ROWS,),
        in_specs=[block(inner), block(wide), block(wide), block(heads), whole(tail), whole(kx),
                  whole(kb), whole(kc), whole(rate), whole(bias)],
        out_specs=[
            block(inner), block(2 * wide), block(LANES),
            pl.BlockSpec((per, wide, inner), lambda i: (i, 0, 0)),
            pl.BlockSpec((pairs, wide + DECAY_ROWS, LANES), lambda i: (0, 0, 0)),
        ],
        out_shape=[
            jax.ShapeDtypeStruct((rows, inner), bf16),
            jax.ShapeDtypeStruct((rows, 2 * wide), bf16),
            jax.ShapeDtypeStruct((rows, LANES), f32),
            jax.ShapeDtypeStruct((rows // CHUNK, wide, inner), bf16),
            jax.ShapeDtypeStruct((pairs, wide + DECAY_ROWS, LANES), bf16),
        ],
        scratch_shapes=[
            pltpu.VMEM((ROWS + HALO, inner), f32), pltpu.VMEM((ROWS + HALO, wide), f32),
            pltpu.VMEM((ROWS + HALO, wide), f32), pltpu.VMEM((ROWS, inner), f32),
            pltpu.VMEM((ROWS, inner), bf16), pltpu.VMEM((2 * heads, inner), bf16),
            pltpu.VMEM((wide, inner), f32), pltpu.VMEM((1, heads), f32),
        ],
        compiler_params=pltpu.CompilerParams(vmem_limit_bytes=VMEM_LIMIT),
        cost_estimate=pl.CostEstimate(flops=2 * 10**9, bytes_accessed=12 << 20, transcendentals=1 << 21),
        name="local_states",
    )(x, b, c, raw, tail, kx, kb, kc, rate, bias)


def inner_kernel(heads, xconv_ref, bc_ref, aux_ref, prefix_ref, gain_ref, y_ref):
    wide = bc_ref.shape[1] // 2
    pairs = xconv_ref.shape[1] // LANES
    aux = aux_ref[...]
    turned = aux.T
    bconv, cconv = bc_ref[:, :wide], bc_ref[:, wide:]
    row = lax.broadcasted_iota(jnp.int32, (CHUNK, CHUNK), 0)
    col = lax.broadcasted_iota(jnp.int32, (CHUNK, CHUNK), 1)
    gram = lax.dot_general(cconv, bconv, (((1,), (1,)), ((), ())), preferred_element_type=jnp.float32)
    gram = jnp.where(row >= col, gram, 0.0)
    left = lax.broadcasted_iota(jnp.int32, (CHUNK, LANES), 1) < LANES // 2
    for j in range(pairs):
        lanes = slice(j * LANES, (j + 1) * LANES)
        xc = xconv_ref[:, lanes]
        weights = []
        cums = []
        for h in (2 * j, 2 * j + 1):
            cum = jnp.broadcast_to(aux[:, h : h + 1], (CHUNK, CHUNK))
            cums.append(cum)
            power = jnp.minimum(cum - turned[heads + h : heads + h + 1, :], 126.0)
            weights.append((gram * jnp.exp2(power)).astype(jnp.bfloat16))
        zero = jnp.zeros_like(xc)
        both = jnp.concatenate([jnp.where(left, xc, zero), jnp.where(left, zero, xc)], axis=0)
        inner = jnp.dot(jnp.concatenate(weights, axis=1), both, preferred_element_type=jnp.float32)
        carried = jnp.dot(cconv, prefix_ref[0, :, lanes], preferred_element_type=jnp.float32)
        decay = jnp.exp2(jnp.where(left, cums[0], cums[1]))
        y_ref[:, lanes] = inner + decay * carried + gain_ref[:, lanes] * xc.astype(jnp.float32)


def local_mix(first, count, xconv, bc, aux, prefix, gain):
    inner = xconv.shape[1]
    heads = gain.shape[1] // 64
    wide = bc.shape[1] // 2
    block = lambda w: pl.BlockSpec((CHUNK, w), lambda i: (i + first, 0))
    return pl.pallas_call(
        functools.partial(inner_kernel, heads),
        grid=(count,),
        in_specs=[block(inner), block(2 * wide), block(LANES),
                  pl.BlockSpec((1, wide, inner), lambda i: (i + first, 0, 0)),
                  pl.BlockSpec((1, inner), lambda i: (0, 0))],
        out_specs=pl.BlockSpec((CHUNK, inner), lambda i: (i, 0)),
        out_shape=jax.ShapeDtypeStruct((count * CHUNK, inner), jnp.float32),
        compiler_params=pltpu.CompilerParams(vmem_limit_bytes=VMEM_LIMIT),
        cost_estimate=pl.CostEstimate(flops=10**10, bytes_accessed=24 << 20, transcendentals=1 << 22),
        name="local_mix",
    )(xconv, bc, aux, prefix, gain)


def scan_kernel(got_ref, out_ref):
    members, rows, width = out_ref.shape
    entering = jnp.zeros((rows, width), jnp.float32)
    for k in range(members):
        out_ref[k] = entering.astype(jnp.bfloat16)
        decay = got_ref[k, rows : rows + 1, :].astype(jnp.float32) + got_ref[
            k, rows + 8 : rows + 9, :
        ].astype(jnp.float32)
        entering = decay * entering + got_ref[k, 0:rows, :].astype(jnp.float32)


def scan_members(got):
    members, rows, width = got.shape
    return pl.pallas_call(
        scan_kernel,
        out_shape=jax.ShapeDtypeStruct((members, rows - DECAY_ROWS, width), jnp.bfloat16),
        compiler_params=pltpu.CompilerParams(vmem_limit_bytes=VMEM_LIMIT),
        name="scan_members",
    )(got)


def finish_kernel(heads, ya_ref, yb_ref, bc_ref, aux_ref, inc_ref, out_ref, expand):
    wide = bc_ref.shape[1] // 2
    pairs = out_ref.shape[1] // LANES

    @pl.when(pl.program_id(0) == 0)
    def _():
        expand[...] = expander(heads, out_ref.shape[1] // heads, 2)

    high, low = split_low(jnp.exp2(aux_ref[:, 2 * heads : 3 * heads]))
    factors = jnp.concatenate([high, low], axis=1)
    cconv = bc_ref[:, wide:]
    early = pl.program_id(0) < pl.num_programs(0) // 2

    def emit(y_ref):
        for j in range(pairs):
            lanes = slice(j * LANES, (j + 1) * LANES)
            decay = jnp.dot(factors, expand[:, lanes], preferred_element_type=jnp.float32)
            carried = jnp.dot(cconv, inc_ref[j], preferred_element_type=jnp.float32)
            out_ref[:, lanes] = (y_ref[:, lanes] + decay * carried).astype(jnp.bfloat16)

    @pl.when(early)
    def _():
        emit(ya_ref)

    @pl.when(jnp.logical_not(early))
    def _():
        emit(yb_ref)


def finish(heads, ya, yb, bc, aux, inc):
    rows, inner = bc.shape[0], ya.shape[1]
    wide = bc.shape[1] // 2
    steps = rows // CHUNK
    half = steps // 2
    block = lambda w: pl.BlockSpec((CHUNK, w), lambda i: (i, 0))
    return pl.pallas_call(
        functools.partial(finish_kernel, heads),
        grid=(steps,),
        in_specs=[
            pl.BlockSpec((CHUNK, inner), lambda i: (jnp.minimum(i, half - 1), 0)),
            pl.BlockSpec((CHUNK, inner), lambda i: (jnp.maximum(i - half, 0), 0)),
            block(2 * wide), block(LANES), pl.BlockSpec(inc.shape, lambda i: (0, 0, 0)),
        ],
        out_specs=block(inner),
        out_shape=jax.ShapeDtypeStruct((rows, inner), jnp.bfloat16),
        scratch_shapes=[pltpu.VMEM((2 * heads, inner), jnp.bfloat16)],
        compiler_params=pltpu.CompilerParams(vmem_limit_bytes=VMEM_LIMIT),
        name="finish",
    )(ya, yb, bc, aux, inc)


def exchange(x):
    return lax.all_to_all(x, "seq", split_axis=0, concat_axis=0, tiled=True)


def regroup(x, count):
    groups, rows, width = x.shape
    if groups == count:
        return x
    flat = x.transpose(1, 0, 2).reshape(rows, groups * width)
    return flat.reshape(rows, count, groups * width // count).transpose(1, 0, 2)


FUSED_CHIPS = 8
PAD = 16
QUAD = 2 * LANES
BIG = 1e38


def fused_kernel(
    x_hbm, b_hbm, c_hbm, raw_hbm, kx_hbm, kb_hbm, kc_hbm, rate_hbm, bias_hbm, gain_hbm,
    y, cconv, decays, incoming,
    raw_ref, kx_ref, kb_ref, kc_ref, rate_ref, bias_ref, gain_ref,
    xbuf, bbuf, cbuf, xc, bconv, aux, turned, expand, gains, falls, ends, factors, grown, btrans, prefix, window_a, window_b,
    scaled_a, scaled_b,
    run, core_got, chip_sum, got, entered, back, core_out, arrived,
    load_sem, small_sem, param_sem, tail_send, tail_recv, core_send, core_recv,
    give_send, give_recv, take_send, take_recv, last_send, last_recv,
):
    f32, bf16 = jnp.float32, jnp.bfloat16
    members = 2 * FUSED_CHIPS
    me = lax.axis_index("seq")
    chip, core = me // 2, me % 2
    partner = chip * 2 + 1 - core
    first_core = core == 0
    rows, inner = xc.shape
    wide = bconv.shape[1]
    heads = rate_ref.shape[1]
    pairs = inner // LANES
    chunks = rows // CHUNK
    half = pairs // 2
    steps = pairs // 2

    def place(i):
        m = lax.rem(chip // 2 + 1 + i // 2, half // 2)
        mine = i % 2
        owner = mine * core + (1 - mine) * (1 - core)
        return m, owner * (half // 2) + m

    def quad_lanes(i):
        return pl.ds(pl.multiple_of(place(i)[1] * QUAD, QUAD), QUAD)

    def load(i):
        lanes = quad_lanes(i)
        return pltpu.make_async_copy(
            x_hbm.at[:, lanes], xbuf.at[pl.ds(PAD, rows), lanes], load_sem.at[i]
        )

    small = [
        pltpu.make_async_copy(b_hbm, bbuf.at[pl.ds(PAD, rows)], small_sem.at[0]),
        pltpu.make_async_copy(c_hbm, cbuf.at[pl.ds(PAD, rows)], small_sem.at[1]),
    ]
    params = [
        pltpu.make_async_copy(src, dst, param_sem.at[i])
        for i, (src, dst) in enumerate((
            (rate_hbm, rate_ref), (bias_hbm, bias_ref), (gain_hbm, gain_ref), (raw_hbm, raw_ref),
            (kx_hbm, kx_ref), (kb_hbm, kb_ref), (kc_hbm, kc_ref),
        ))
    ]
    for copy in params + small[:1]:
        copy.start()
    for i in range(steps):
        load(i).start()
    small[1].start()

    barrier = pltpu.get_barrier_semaphore()
    for off in range(1, members):
        pl.semaphore_signal(
            barrier, inc=1, device_id={"seq": lax.rem(me + off, members)},
            device_id_type=pl.DeviceIdType.MESH,
        )

    def remote(src, dst, send, recv, to):
        return pltpu.make_async_remote_copy(
            src_ref=src, dst_ref=dst, send_sem=send, recv_sem=recv, device_id={"seq": to},
            device_id_type=pl.DeviceIdType.MESH,
        )

    after = lax.rem(me + 1, members)
    tails = [
        remote(h.at[pl.ds(rows - PAD, PAD)], v.at[pl.ds(0, PAD)], tail_send.at[i], tail_recv.at[i], after)
        for i, (h, v) in enumerate(((x_hbm, xbuf), (b_hbm, bbuf), (c_hbm, cbuf)))
    ]

    expand[...] = expander(heads, inner // heads, 2)
    for copy in params:
        copy.wait()
    high, middle = split_low(jnp.broadcast_to(gain_ref[...], (8, heads)))
    low = (gain_ref[...] - high.astype(f32) - middle.astype(f32)).astype(bf16)
    gains[...] = jnp.dot(
        jnp.concatenate([high, middle], axis=1), expand[...], preferred_element_type=f32
    ) + jnp.dot(
        jnp.concatenate([low, jnp.zeros_like(low)], axis=1), expand[...], preferred_element_type=f32
    )
    row = lax.broadcasted_iota(jnp.int32, (CHUNK, CHUNK), 0)
    col = lax.broadcasted_iota(jnp.int32, (CHUNK, CHUNK), 1)
    turns = jnp.concatenate([rate_ref[...], bias_ref[...], rate_ref[...], bias_ref[...]], axis=1)
    turns = jnp.broadcast_to(turns, (CHUNK, CHUNK)).T
    speed = jnp.exp(turns[:heads]) * LOG2E
    bias = turns[heads : 2 * heads]
    upper = (row <= col).astype(bf16)
    log_before = jnp.zeros((heads, CHUNK), f32)
    chunk_falls = []
    for q in range(chunks):
        span = slice(q * CHUNK, (q + 1) * CHUNK)
        shifted = raw_ref[:, span] + bias
        dt = jnp.maximum(shifted, 0.0) + jnp.log1p(jnp.exp(-jnp.abs(shifted)))
        logdec = -speed * dt
        part0 = logdec.astype(bf16)
        rest = logdec - part0.astype(f32)
        part1 = rest.astype(bf16)
        part2 = (rest - part1.astype(f32)).astype(bf16)
        sums = jnp.dot(
            jnp.concatenate([part0, part1, part2], axis=0), upper, preferred_element_type=f32
        )
        cum = sums[:heads] + sums[heads : 2 * heads] + sums[2 * heads :]
        total = jnp.broadcast_to(cum[:, CHUNK - 1 :], cum.shape)
        shift = cum - jnp.log(dt) * LOG2E
        flat = jnp.concatenate(
            [cum, shift, jnp.exp2(log_before + cum), jnp.exp2(total - shift)], axis=0
        )
        log_before = log_before + total
        stood = flat.T
        turned[q] = flat
        aux[q] = stood
        factors[span, :] = stood[:, 3 * heads :].astype(bf16)
        high, low = split_low(stood[:, 2 * heads : 3 * heads])
        grown[span, :] = jnp.concatenate([high, low], axis=1)
        chunk_falls.append(jnp.exp2(stood[CHUNK - 1 :, :heads]))
    high, low = split_low(jnp.concatenate(chunk_falls, axis=0))
    falls[...] = jnp.dot(
        jnp.concatenate([high, low], axis=1), expand[...], preferred_element_type=f32
    )
    high, low = split_low(
        jnp.broadcast_to(stood[CHUNK - 1 :, 2 * heads : 3 * heads], (8, heads))
    )
    zero = jnp.zeros_like(high)
    high = jnp.dot(jnp.concatenate([high, zero], axis=1), expand[...], preferred_element_type=f32)
    low = jnp.dot(jnp.concatenate([low, zero], axis=1), expand[...], preferred_element_type=f32)
    ends[...] = jnp.concatenate([high, low], axis=0).astype(bf16)
    pl.semaphore_wait(barrier, members - 1)

    @pl.when(me < members - 1)
    def _():
        for copy in tails:
            copy.start()

    def fill(buf, slot, at, count, lanes):
        slot[at : at + count, :] = buf[at : at + count, lanes].astype(f32)

    def convolve(taps_ref, slot, q, lanes):
        taps = 0.5 * taps_ref[:, lanes]
        count = taps.shape[0]
        at = PAD - count + 1 + q * CHUNK
        total = taps[0:1] * slot[at : at + CHUNK, :]
        for k in range(1, count):
            total = total + taps[k : k + 1] * slot[at + k : at + k + CHUNK, :]
        return (total + total * jnp.tanh(total)).astype(bf16)

    everything = slice(0, LANES)

    def small_chunk(q):
        span = slice(q * CHUNK, (q + 1) * CHUNK)
        bconv[span, :] = convolve(kb_ref, window_b.at[0], q, everything)
        cconv[span, :] = convolve(kc_ref, window_b.at[1], q, everything)

    def part_lanes(i, part):
        return pl.ds(pl.multiple_of(place(i)[1] * QUAD + part * LANES, LANES), LANES)

    def fill_chunk(i, win, q):
        for part in range(2):
            fill(xbuf, win.at[part], PAD + q * CHUNK, CHUNK, part_lanes(i, part))

    def convolve_chunk(i, win, scaled, q):
        span = slice(q * CHUNK, (q + 1) * CHUNK)
        spread = jnp.dot(
            factors[span, :], expand[:heads, quad_lanes(i)], preferred_element_type=f32
        ).astype(bf16)
        for part in range(2):
            lanes = part_lanes(i, part)
            piece = slice(part * LANES, (part + 1) * LANES)
            done = convolve(kx_ref, win.at[part], q, lanes)
            xc[span, lanes] = done
            scaled[span, piece] = done * spread[:, piece]

    small[0].wait()
    small[1].wait()
    fill(bbuf, window_b.at[0], PAD, rows, everything)
    fill(cbuf, window_b.at[1], PAD, rows, everything)
    for q in range(1, chunks):
        small_chunk(q)
    load(0).wait()
    for q in range(chunks):
        fill_chunk(0, window_a, q)
    for q in range(1, chunks):
        convolve_chunk(0, window_a, scaled_a, q)

    @pl.when(me > 0)
    def _():
        for copy in tails:
            copy.wait_recv()

    @pl.when(me == 0)
    def _():
        xbuf[0:PAD, :] = jnp.zeros((PAD, inner), bf16)
        bbuf[0:PAD, :] = jnp.zeros((PAD, wide), bf16)
        cbuf[0:PAD, :] = jnp.zeros((PAD, wide), bf16)

    fill(bbuf, window_b.at[0], 0, PAD, everything)
    fill(cbuf, window_b.at[1], 0, PAD, everything)
    small_chunk(0)
    for part in range(2):
        fill(xbuf, window_a.at[part], 0, PAD, part_lanes(0, part))
    convolve_chunk(0, window_a, scaled_a, 0)
    for q in range(chunks):
        span = slice(q * CHUNK, (q + 1) * CHUNK)
        btrans[:, span] = bconv[span, :].astype(f32).T.astype(bf16)

    def state_chunk(i, scaled, q, held):
        span = slice(q * CHUNK, (q + 1) * CHUNK)
        lanes = quad_lanes(i)
        prefix[q, :, lanes] = held.astype(bf16)
        return falls[q : q + 1, lanes] * held + jnp.dot(
            btrans[:, span], scaled[span, :], preferred_element_type=f32
        )

    def state_and_next(i, scaled, following):
        held = jnp.zeros((wide, QUAD), f32)
        if following is not None:
            win, into = following
            for part in range(2):
                fill(xbuf, win.at[part], 0, PAD, part_lanes(i + 1, part))
        for q in range(chunks):
            if following is not None:
                fill_chunk(i + 1, win, q)
                convolve_chunk(i + 1, win, into, q)
            held = state_chunk(i, scaled, q, held)
        held = held.astype(bf16)
        tip = ends[:, quad_lanes(i)]
        first = place(i)[1] * 2
        for part in range(2):
            piece = slice(part * LANES, (part + 1) * LANES)
            run[first + part, 0:wide, :] = held[:, piece]
            run[first + part, wide:, :] = tip[:, piece]

    def to_core(m):
        return remote(
            run.at[pl.ds((1 - core) * half + 2 * m, 2)], core_got.at[pl.ds(2 * m, 2)],
            core_send.at[m], core_recv.at[m], partner,
        )

    def give(other):
        return remote(
            chip_sum.at[other], got.at[chip], give_send.at[other], give_recv.at[chip],
            other * 2 + core,
        )

    def given(other):
        return remote(
            chip_sum.at[other], got.at[other], give_send.at[other], give_recv.at[other],
            other * 2 + core,
        )

    def take(other):
        return remote(
            entered.at[other], back.at[chip], take_send.at[other], take_recv.at[chip],
            other * 2 + core,
        )

    def taken(other):
        return remote(
            entered.at[other], back.at[other], take_send.at[other], take_recv.at[other],
            other * 2 + core,
        )

    def last():
        return remote(
            core_out, arrived, last_send.at[0], last_recv.at[0], partner,
        )

    def decay_of(piece):
        return piece[wide : wide + 1].astype(f32) + piece[wide + 8 : wide + 9].astype(f32)

    def add_cores(m):
        to_core(m).wait_recv()
        for part in range(2):
            j = 2 * m + part
            mine, other = run[core * half + j], core_got[j]
            lead = jnp.where(first_core, mine.astype(f32), other.astype(f32))
            trail = jnp.where(first_core, other.astype(f32), mine.astype(f32))
            fall = trail[wide : wide + 1] + trail[wide + 8 : wide + 9]
            whole = (lead[wide : wide + 1] + lead[wide + 8 : wide + 9]) * fall
            high, low = split_low(jnp.broadcast_to(whole, (8, LANES)))
            chip_sum[j, 0:wide, :] = (fall * lead[:wide] + trail[:wide]).astype(bf16)
            chip_sum[j, wide:, :] = jnp.concatenate(
                [high.astype(f32), low.astype(f32)], axis=0
            ).astype(bf16)

            @pl.when(j != chip)
            def _():
                give(j).start()

            @pl.when(j == chip)
            def _():
                got[chip] = chip_sum[chip]

    def others(act):
        for off in range(1, FUSED_CHIPS):
            act(lax.rem(chip + off, FUSED_CHIPS))

    def scan_chips():
        others(lambda k: given(k).wait_recv())
        value = jnp.zeros((wide, LANES), f32)
        for k in range(FUSED_CHIPS):
            entered[k] = value.astype(bf16)
            if k < FUSED_CHIPS - 1:
                piece = got[k]
                value = decay_of(piece) * value + piece[:wide].astype(f32)
        others(lambda k: take(k).start())
        back[chip] = entered[chip]

    def split_cores():
        others(lambda k: taken(k).wait_recv())
        for j in range(half):
            lead = jnp.where(
                first_core, run[core * half + j].astype(f32), core_got[j].astype(f32)
            )
            entering = back[j].astype(f32)
            fall = lead[wide : wide + 1] + lead[wide + 8 : wide + 9]
            later = fall * entering + lead[:wide]
            core_out[j] = jnp.where(first_core, later, entering).astype(bf16)
            incoming[core * half + j] = jnp.where(first_core, entering, later).astype(bf16)
        last().start()

    @pl.loop(0, steps // 2)
    def _(k):
        i = 2 * k
        load(i + 1).wait()
        state_and_next(i, scaled_a, (window_b, scaled_b))
        to_core(place(i)[0]).start()

        @pl.when(k < steps // 2 - 1)
        def _():
            load(i + 2).wait()
            state_and_next(i + 1, scaled_b, (window_a, scaled_a))

        @pl.when(k == steps // 2 - 1)
        def _():
            state_and_next(i + 1, scaled_b, None)

        add_cores(place(i + 1)[0])

    @pl.when(me < members - 1)
    def _():
        for copy in tails:
            copy.wait_send()

    left = lax.broadcasted_iota(jnp.int32, (CHUNK, LANES), 1) < LANES // 2

    @pl.loop(0, chunks)
    def _(q):
        at = pl.ds(pl.multiple_of(q * CHUNK, CHUNK), CHUNK)
        cc = cconv[at, :]
        gram = lax.dot_general(
            cc, bconv[at, :], (((1,), (1,)), ((), ())), preferred_element_type=f32
        )
        gram = jnp.where(row >= col, gram, 0.0).astype(bf16)
        for g in range(pairs // 2):
            wider = slice(g * QUAD, (g + 1) * QUAD)
            carried = jnp.dot(cc, prefix[q, :, wider], preferred_element_type=f32)
            decays[at, wider] = jnp.dot(grown[at, :], expand[:, wider], preferred_element_type=f32)
            for part in range(2):
                j = 2 * g + part
                lanes = slice(j * LANES, (j + 1) * LANES)
                values = xc[at, lanes]
                weights, cums = [], []
                for h in (2 * j, 2 * j + 1):
                    cum = jnp.broadcast_to(aux[q, :, h : h + 1], (CHUNK, CHUNK))
                    cums.append(cum)
                    grow = jnp.exp2(cum - turned[q, heads + h : heads + h + 1, :]).astype(bf16)
                    weights.append(gram * jnp.minimum(grow, jnp.asarray(BIG, bf16)))
                zero = jnp.zeros_like(values)
                both = jnp.concatenate(
                    [jnp.where(left, values, zero), jnp.where(left, zero, values)], axis=0
                )
                mixed = jnp.dot(jnp.concatenate(weights, axis=1), both, preferred_element_type=f32)
                decay = jnp.exp2(jnp.where(left, cums[0], cums[1]))
                y[at, lanes] = (
                    mixed + decay * carried[:, part * LANES : (part + 1) * LANES]
                    + gains[0:1, lanes] * values.astype(f32)
                )

        @pl.when(q == SCAN_AT)
        def _():
            scan_chips()

        @pl.when(q == SPLIT_AT)
        def _():
            split_cores()

    for m in range(half // 2):
        to_core(m).wait_send()
    others(lambda k: give(k).wait_send())
    others(lambda k: take(k).wait_send())
    last().wait()
    incoming[pl.ds((1 - core) * half, half)] = arrived[...]


SCAN_AT = 1
SPLIT_AT = 6


def output_kernel(y_ref, c_ref, decay_ref, inc_ref, out_hbm, held, store_sem):
    rows = held.shape[0]

    def store(r):
        at = pl.ds(pl.multiple_of(r * ROWS, ROWS), ROWS)
        return pltpu.make_async_copy(held.at[at], out_hbm.at[at], store_sem.at[r])

    @pl.loop(0, rows // ROWS)
    def _(r):
        at = pl.ds(pl.multiple_of(r * ROWS, ROWS), ROWS)
        cc = c_ref[at, :]
        for g in range(inc_ref.shape[0] // 2):
            wider = slice(g * QUAD, (g + 1) * QUAD)
            entering = jnp.concatenate([inc_ref[2 * g], inc_ref[2 * g + 1]], axis=1)
            carried = jnp.dot(cc, entering, preferred_element_type=jnp.float32)
            held[at, wider] = (y_ref[at, wider] + decay_ref[at, wider] * carried).astype(jnp.bfloat16)
        store(r).start()

    @pl.loop(0, rows // ROWS)
    def _(r):
        store(r).wait()


def fused(inner_x, input_map, output_map, raw, kernel_x, kernel_b, kernel_c, rate, bias, gain):
    rows, inner = inner_x.shape
    wide = input_map.shape[1]
    heads = rate.shape[1]
    pairs = inner // LANES
    half = pairs // 2
    chunks = rows // CHUNK
    f32, bf16 = jnp.float32, jnp.bfloat16
    far = pl.BlockSpec(memory_space=pltpu.HBM)
    near = pl.BlockSpec(memory_space=pltpu.VMEM)
    tall = wide + DECAY_ROWS
    chips = FUSED_CHIPS
    dma = pltpu.SemaphoreType.DMA
    y, cconv, decays, incoming = pl.pallas_call(
        fused_kernel,
        in_specs=[far] * 10,
        out_specs=[near] * 4,
        out_shape=[
            pltpu.VMEM((rows, inner), f32), pltpu.VMEM((rows, wide), bf16),
            pltpu.VMEM((rows, inner), f32), pltpu.VMEM((pairs, wide, LANES), bf16),
        ],
        scratch_shapes=[
            pltpu.VMEM(raw.shape, f32), pltpu.VMEM(kernel_x.shape, f32),
            pltpu.VMEM(kernel_b.shape, f32), pltpu.VMEM(kernel_c.shape, f32),
            pltpu.VMEM(rate.shape, f32), pltpu.VMEM(bias.shape, f32), pltpu.VMEM(gain.shape, f32),
            pltpu.VMEM((PAD + rows, inner), bf16), pltpu.VMEM((PAD + rows, wide), bf16),
            pltpu.VMEM((PAD + rows, wide), bf16), pltpu.VMEM((rows, inner), bf16),
            pltpu.VMEM((rows, wide), bf16), pltpu.VMEM((chunks, CHUNK, LANES), f32),
            pltpu.VMEM((chunks, LANES, CHUNK), f32), pltpu.VMEM((2 * heads, inner), bf16),
            pltpu.VMEM((8, inner), f32), pltpu.VMEM((chunks, inner), f32),
            pltpu.VMEM((DECAY_ROWS, inner), bf16), pltpu.VMEM((rows, heads), bf16),
            pltpu.VMEM((rows, 2 * heads), bf16), pltpu.VMEM((wide, rows), bf16),
            pltpu.VMEM((chunks, wide, inner), bf16), pltpu.VMEM((2, rows + PAD, LANES), f32),
            pltpu.VMEM((2, rows + PAD, LANES), f32), pltpu.VMEM((rows, QUAD), bf16),
            pltpu.VMEM((rows, QUAD), bf16),
            pltpu.VMEM((pairs, tall, LANES), bf16), pltpu.VMEM((half, tall, LANES), bf16),
            pltpu.VMEM((chips, tall, LANES), bf16), pltpu.VMEM((chips, tall, LANES), bf16),
            pltpu.VMEM((chips, wide, LANES), bf16), pltpu.VMEM((chips, wide, LANES), bf16),
            pltpu.VMEM((half, wide, LANES), bf16), pltpu.VMEM((half, wide, LANES), bf16),
            dma((pairs // 2,)), dma((2,)), dma((7,)), dma((3,)), dma((3,)), dma((half // 2,)),
            dma((half // 2,)), dma((chips,)), dma((chips,)), dma((chips,)), dma((chips,)),
            dma((1,)), dma((1,)),
        ],
        compiler_params=pltpu.CompilerParams(
            vmem_limit_bytes=FUSED_VMEM, collective_id=0, has_side_effects=True
        ),
        name="fused_mixer",
    )(inner_x, input_map, output_map, raw, kernel_x, kernel_b, kernel_c, rate, bias, gain)
    return pl.pallas_call(
        output_kernel,
        in_specs=[near] * 4,
        out_specs=pl.BlockSpec(memory_space=pl.ANY),
        out_shape=jax.ShapeDtypeStruct((rows, inner), bf16),
        scratch_shapes=[pltpu.VMEM((rows, inner), bf16), dma((rows // ROWS,))],
        compiler_params=pltpu.CompilerParams(vmem_limit_bytes=OUTPUT_VMEM),
        name="output_rows",
    )(y, cconv, decays, incoming)


FUSED_VMEM = (47 << 20) + (160 << 10)
OUTPUT_VMEM = 16 << 20


def on_device(
    inner_x, input_map, output_map, step_raw, kernel_x, kernel_b, kernel_c, log_rate, step_bias,
    skip_gain,
):
    rows, inner = inner_x.shape
    heads = log_rate.shape[0]
    members = lax.axis_size("seq")
    if members == 2 * FUSED_CHIPS and inner == members * LANES and rows % ROWS == 0:
        return fused(
            inner_x, input_map, output_map, step_raw.T, kernel_x, kernel_b, kernel_c,
            log_rate[None, :], step_bias[None, :], skip_gain[None, :],
        )
    last = jnp.concatenate([a[rows - HALO :] for a in (inner_x, input_map, output_map)], axis=1)
    tail = lax.ppermute(last, "seq", [(i, i + 1) for i in range(members - 1)])
    xconv, bc, aux, prefix, run = local_states(
        inner_x, input_map, output_map, step_raw, tail, kernel_x, kernel_b, kernel_c,
        log_rate[None, :], step_bias[None, :],
    )
    gain = jnp.repeat(skip_gain, inner // heads)[None, :]
    half = rows // CHUNK // 2
    got = exchange(regroup(run, members))
    ya = local_mix(0, half, xconv, bc, aux, prefix, gain)
    got, ya = lax.optimization_barrier((got, ya))
    back = exchange(scan_members(got))
    yb = local_mix(half, half, xconv, bc, aux, prefix, gain)
    incoming = regroup(back, inner // LANES)
    return finish(heads, ya, yb, bc, aux, incoming)


def solution(mesh):
    split = P(("groups", "seq"), None)
    return jax.shard_map(
        on_device, mesh=mesh, in_specs=(split,) * 4 + (P(),) * 6, out_specs=split, check_vma=False
    )
```

```python
import functools

import jax
import jax.numpy as jnp
from jax import lax
from jax.experimental import pallas as pl
from jax.experimental.pallas import tpu as pltpu
from jax.sharding import PartitionSpec as P

CHUNK = 128
ROWS = 256
LANES = 128
LOG2E = 1.4426950408889634
HALO = 8
VMEM_LIMIT = 60 << 20
DECAY_ROWS = 16


def split_low(value):
    high = value.astype(jnp.bfloat16)
    return high, (value - high.astype(jnp.float32)).astype(jnp.bfloat16)


def silu(value):
    half = 0.5 * value
    return half + half * jnp.tanh(half)


def expander(heads, width, parts):
    shape = (parts * heads, heads * width)
    row = lax.broadcasted_iota(jnp.int32, shape, 0) % heads
    col = lax.broadcasted_iota(jnp.int32, shape, 1) // width
    return (row == col).astype(jnp.bfloat16)


def state_kernel(
    heads, x_ref, b_ref, c_ref, raw_ref, tail_ref, kx_ref, kb_ref, kc_ref, rate_ref, bias_ref,
    xconv_ref, bc_ref, aux_ref, prefix_ref, run_ref,
    xwin, bwin, cwin, spread, scaled, expand, state, logrun,
):
    step = pl.program_id(0)
    inner = x_ref.shape[1]
    wide = b_ref.shape[1]
    pairs = inner // LANES

    @pl.when(step == 0)
    def _():
        tail = tail_ref[...].astype(jnp.float32)
        xwin[0:HALO, :] = tail[:, :inner]
        bwin[0:HALO, :] = tail[:, inner : inner + wide]
        cwin[0:HALO, :] = tail[:, inner + wide :]
        expand[...] = expander(heads, inner // heads, 2)
        state[...] = jnp.zeros_like(state)
        logrun[...] = jnp.zeros_like(logrun)

    @pl.when(step > 0)
    def _():
        xwin[0:HALO, :] = xwin[ROWS : ROWS + HALO, :]
        bwin[0:HALO, :] = bwin[ROWS : ROWS + HALO, :]
        cwin[0:HALO, :] = cwin[ROWS : ROWS + HALO, :]

    bwin[HALO:, :] = b_ref[...].astype(jnp.float32)
    cwin[HALO:, :] = c_ref[...].astype(jnp.float32)

    def small_conv(win, taps):
        count = taps.shape[0]
        total = jnp.zeros((ROWS, win.shape[1]), jnp.float32)
        for k in range(count):
            at = HALO - (count - 1) + k
            total = total + taps[k : k + 1, :] * win[at : at + ROWS, :]
        return silu(total).astype(jnp.bfloat16)

    bconv = small_conv(bwin, kb_ref)
    cconv = small_conv(cwin, kc_ref)
    bc_ref[:, :wide] = bconv
    bc_ref[:, wide:] = cconv

    shifted = raw_ref[...] + bias_ref[...]
    dt = jnp.maximum(shifted, 0.0) + jnp.log1p(jnp.exp(-jnp.abs(shifted)))
    logdec = -(jnp.exp(rate_ref[...]) * LOG2E) * dt
    part0, rest = logdec.astype(jnp.bfloat16), None
    rest = logdec - part0.astype(jnp.float32)
    part1 = rest.astype(jnp.bfloat16)
    part2 = (rest - part1.astype(jnp.float32)).astype(jnp.bfloat16)
    row = lax.broadcasted_iota(jnp.int32, (CHUNK, CHUNK), 0)
    col = lax.broadcasted_iota(jnp.int32, (CHUNK, CHUNK), 1)
    lower = (row >= col).astype(jnp.bfloat16)
    parts = jnp.concatenate([part0, part1, part2, jnp.zeros_like(part0)], axis=1)
    logdt = jnp.log(dt) * LOG2E
    totals = []
    for q in range(ROWS // CHUNK):
        span = slice(q * CHUNK, (q + 1) * CHUNK)
        sums = jnp.dot(lower, parts[span], preferred_element_type=jnp.float32)
        cum = sums[:, :heads] + sums[:, heads : 2 * heads] + sums[:, 2 * heads : 3 * heads]
        total = cum[CHUNK - 1 :, :]
        totals.append(total)
        shift = cum - logdt[span]
        run = logrun[...] + cum
        logrun[...] = logrun[...] + total
        aux_ref[span, :] = jnp.concatenate([cum, shift, run, jnp.zeros_like(run)], axis=1)
        high, low = split_low(jnp.exp2(total - shift))
        spread[span, :] = jnp.dot(
            jnp.concatenate([high, low], axis=1), expand[...], preferred_element_type=jnp.float32
        )

    @pl.loop(0, pairs)
    def _(j):
        lanes = pl.ds(pl.multiple_of(j * LANES, LANES), LANES)
        xwin[HALO:, lanes] = x_ref[:, lanes].astype(jnp.float32)
        count = kx_ref.shape[0]
        total = jnp.zeros((ROWS, LANES), jnp.float32)
        for k in range(count):
            at = HALO - (count - 1) + k
            total = total + kx_ref[k : k + 1, lanes] * xwin[at : at + ROWS, lanes]
        xc = silu(total).astype(jnp.bfloat16)
        xconv_ref[:, lanes] = xc
        scaled[:, lanes] = (xc.astype(jnp.float32) * spread[:, lanes]).astype(jnp.bfloat16)

    btrans = bconv.astype(jnp.float32).T.astype(jnp.bfloat16)
    for q in range(ROWS // CHUNK):
        span = slice(q * CHUNK, (q + 1) * CHUNK)
        prefix_ref[q] = state[...].astype(jnp.bfloat16)
        factor = jnp.broadcast_to(jnp.exp2(totals[q]), (8, heads))
        high, low = split_low(factor)
        decay = jnp.dot(
            jnp.concatenate([high, low], axis=1), expand[...], preferred_element_type=jnp.float32
        )[0:1, :]
        state[...] = decay * state[...] + jnp.dot(
            btrans[:, span], scaled[span, :], preferred_element_type=jnp.float32
        )

    @pl.when(step == pl.num_programs(0) - 1)
    def _():
        high, low = split_low(jnp.broadcast_to(jnp.exp2(logrun[...]), (8, heads)))
        zero = jnp.zeros_like(high)
        high = jnp.dot(jnp.concatenate([high, zero], axis=1), expand[...], preferred_element_type=jnp.float32)
        low = jnp.dot(jnp.concatenate([low, zero], axis=1), expand[...], preferred_element_type=jnp.float32)
        both = jnp.concatenate([high, low], axis=0).astype(jnp.bfloat16)
        for j in range(pairs):
            lanes = slice(j * LANES, (j + 1) * LANES)
            run_ref[j, 0 : state.shape[0], :] = state[:, lanes].astype(jnp.bfloat16)
            run_ref[j, state.shape[0] :, :] = both[:, lanes]


def local_states(x, b, c, raw, tail, kx, kb, kc, rate, bias):
    rows, inner = x.shape
    wide = b.shape[1]
    heads = raw.shape[1]
    pairs = inner // LANES
    whole = lambda a: pl.BlockSpec(a.shape, lambda i: (0,) * a.ndim)
    block = lambda w: pl.BlockSpec((ROWS, w), lambda i: (i, 0))
    per = ROWS // CHUNK
    f32, bf16 = jnp.float32, jnp.bfloat16
    return pl.pallas_call(
        functools.partial(state_kernel, heads),
        grid=(rows // ROWS,),
        in_specs=[block(inner), block(wide), block(wide), block(heads), whole(tail), whole(kx),
                  whole(kb), whole(kc), whole(rate), whole(bias)],
        out_specs=[
            block(inner), block(2 * wide), block(LANES),
            pl.BlockSpec((per, wide, inner), lambda i: (i, 0, 0)),
            pl.BlockSpec((pairs, wide + DECAY_ROWS, LANES), lambda i: (0, 0, 0)),
        ],
        out_shape=[
            jax.ShapeDtypeStruct((rows, inner), bf16),
            jax.ShapeDtypeStruct((rows, 2 * wide), bf16),
            jax.ShapeDtypeStruct((rows, LANES), f32),
            jax.ShapeDtypeStruct((rows // CHUNK, wide, inner), bf16),
            jax.ShapeDtypeStruct((pairs, wide + DECAY_ROWS, LANES), bf16),
        ],
        scratch_shapes=[
            pltpu.VMEM((ROWS + HALO, inner), f32), pltpu.VMEM((ROWS + HALO, wide), f32),
            pltpu.VMEM((ROWS + HALO, wide), f32), pltpu.VMEM((ROWS, inner), f32),
            pltpu.VMEM((ROWS, inner), bf16), pltpu.VMEM((2 * heads, inner), bf16),
            pltpu.VMEM((wide, inner), f32), pltpu.VMEM((1, heads), f32),
        ],
        compiler_params=pltpu.CompilerParams(vmem_limit_bytes=VMEM_LIMIT),
        cost_estimate=pl.CostEstimate(flops=2 * 10**9, bytes_accessed=12 << 20, transcendentals=1 << 21),
        name="local_states",
    )(x, b, c, raw, tail, kx, kb, kc, rate, bias)


def inner_kernel(heads, xconv_ref, bc_ref, aux_ref, prefix_ref, gain_ref, y_ref):
    wide = bc_ref.shape[1] // 2
    pairs = xconv_ref.shape[1] // LANES
    aux = aux_ref[...]
    turned = aux.T
    bconv, cconv = bc_ref[:, :wide], bc_ref[:, wide:]
    row = lax.broadcasted_iota(jnp.int32, (CHUNK, CHUNK), 0)
    col = lax.broadcasted_iota(jnp.int32, (CHUNK, CHUNK), 1)
    gram = lax.dot_general(cconv, bconv, (((1,), (1,)), ((), ())), preferred_element_type=jnp.float32)
    gram = jnp.where(row >= col, gram, 0.0)
    left = lax.broadcasted_iota(jnp.int32, (CHUNK, LANES), 1) < LANES // 2
    for j in range(pairs):
        lanes = slice(j * LANES, (j + 1) * LANES)
        xc = xconv_ref[:, lanes]
        weights = []
        cums = []
        for h in (2 * j, 2 * j + 1):
            cum = jnp.broadcast_to(aux[:, h : h + 1], (CHUNK, CHUNK))
            cums.append(cum)
            power = jnp.minimum(cum - turned[heads + h : heads + h + 1, :], 126.0)
            weights.append((gram * jnp.exp2(power)).astype(jnp.bfloat16))
        zero = jnp.zeros_like(xc)
        both = jnp.concatenate([jnp.where(left, xc, zero), jnp.where(left, zero, xc)], axis=0)
        inner = jnp.dot(jnp.concatenate(weights, axis=1), both, preferred_element_type=jnp.float32)
        carried = jnp.dot(cconv, prefix_ref[0, :, lanes], preferred_element_type=jnp.float32)
        decay = jnp.exp2(jnp.where(left, cums[0], cums[1]))
        y_ref[:, lanes] = inner + decay * carried + gain_ref[:, lanes] * xc.astype(jnp.float32)


def local_mix(first, count, xconv, bc, aux, prefix, gain):
    inner = xconv.shape[1]
    heads = gain.shape[1] // 64
    wide = bc.shape[1] // 2
    block = lambda w: pl.BlockSpec((CHUNK, w), lambda i: (i + first, 0))
    return pl.pallas_call(
        functools.partial(inner_kernel, heads),
        grid=(count,),
        in_specs=[block(inner), block(2 * wide), block(LANES),
                  pl.BlockSpec((1, wide, inner), lambda i: (i + first, 0, 0)),
                  pl.BlockSpec((1, inner), lambda i: (0, 0))],
        out_specs=pl.BlockSpec((CHUNK, inner), lambda i: (i, 0)),
        out_shape=jax.ShapeDtypeStruct((count * CHUNK, inner), jnp.float32),
        compiler_params=pltpu.CompilerParams(vmem_limit_bytes=VMEM_LIMIT),
        cost_estimate=pl.CostEstimate(flops=10**10, bytes_accessed=24 << 20, transcendentals=1 << 22),
        name="local_mix",
    )(xconv, bc, aux, prefix, gain)


def scan_kernel(got_ref, out_ref):
    members, rows, width = out_ref.shape
    entering = jnp.zeros((rows, width), jnp.float32)
    for k in range(members):
        out_ref[k] = entering.astype(jnp.bfloat16)
        decay = got_ref[k, rows : rows + 1, :].astype(jnp.float32) + got_ref[
            k, rows + 8 : rows + 9, :
        ].astype(jnp.float32)
        entering = decay * entering + got_ref[k, 0:rows, :].astype(jnp.float32)


def scan_members(got):
    members, rows, width = got.shape
    return pl.pallas_call(
        scan_kernel,
        out_shape=jax.ShapeDtypeStruct((members, rows - DECAY_ROWS, width), jnp.bfloat16),
        compiler_params=pltpu.CompilerParams(vmem_limit_bytes=VMEM_LIMIT),
        name="scan_members",
    )(got)


def finish_kernel(heads, ya_ref, yb_ref, bc_ref, aux_ref, inc_ref, out_ref, expand):
    wide = bc_ref.shape[1] // 2
    pairs = out_ref.shape[1] // LANES

    @pl.when(pl.program_id(0) == 0)
    def _():
        expand[...] = expander(heads, out_ref.shape[1] // heads, 2)

    high, low = split_low(jnp.exp2(aux_ref[:, 2 * heads : 3 * heads]))
    factors = jnp.concatenate([high, low], axis=1)
    cconv = bc_ref[:, wide:]
    early = pl.program_id(0) < pl.num_programs(0) // 2

    def emit(y_ref):
        for j in range(pairs):
            lanes = slice(j * LANES, (j + 1) * LANES)
            decay = jnp.dot(factors, expand[:, lanes], preferred_element_type=jnp.float32)
            carried = jnp.dot(cconv, inc_ref[j], preferred_element_type=jnp.float32)
            out_ref[:, lanes] = (y_ref[:, lanes] + decay * carried).astype(jnp.bfloat16)

    @pl.when(early)
    def _():
        emit(ya_ref)

    @pl.when(jnp.logical_not(early))
    def _():
        emit(yb_ref)


def finish(heads, ya, yb, bc, aux, inc):
    rows, inner = bc.shape[0], ya.shape[1]
    wide = bc.shape[1] // 2
    steps = rows // CHUNK
    half = steps // 2
    block = lambda w: pl.BlockSpec((CHUNK, w), lambda i: (i, 0))
    return pl.pallas_call(
        functools.partial(finish_kernel, heads),
        grid=(steps,),
        in_specs=[
            pl.BlockSpec((CHUNK, inner), lambda i: (jnp.minimum(i, half - 1), 0)),
            pl.BlockSpec((CHUNK, inner), lambda i: (jnp.maximum(i - half, 0), 0)),
            block(2 * wide), block(LANES), pl.BlockSpec(inc.shape, lambda i: (0, 0, 0)),
        ],
        out_specs=block(inner),
        out_shape=jax.ShapeDtypeStruct((rows, inner), jnp.bfloat16),
        scratch_shapes=[pltpu.VMEM((2 * heads, inner), jnp.bfloat16)],
        compiler_params=pltpu.CompilerParams(vmem_limit_bytes=VMEM_LIMIT),
        name="finish",
    )(ya, yb, bc, aux, inc)


def exchange(x):
    return lax.all_to_all(x, "seq", split_axis=0, concat_axis=0, tiled=True)


def regroup(x, count):
    groups, rows, width = x.shape
    if groups == count:
        return x
    flat = x.transpose(1, 0, 2).reshape(rows, groups * width)
    return flat.reshape(rows, count, groups * width // count).transpose(1, 0, 2)


FUSED_CHIPS = 8
PAD = 16
QUAD = 2 * LANES
BIG = 1e38


def fused_kernel(
    x_hbm, b_hbm, c_hbm, raw_hbm, kx_hbm, kb_hbm, kc_hbm, rate_hbm, bias_hbm, gain_hbm,
    y, cconv, decays, incoming,
    raw_ref, kx_ref, kb_ref, kc_ref, rate_ref, bias_ref, gain_ref,
    xbuf, bbuf, cbuf, xc, bconv, aux, turned, expand, gains, falls, ends, factors, growth, btrans, prefix, window_a, window_b,
    scaled_a, scaled_b,
    run, core_got, chip_sum, got, entered, back, core_out, arrived,
    load_sem, small_sem, param_sem, tail_send, tail_recv, core_send, core_recv,
    give_send, give_recv, take_send, take_recv, last_send, last_recv,
):
    f32, bf16 = jnp.float32, jnp.bfloat16
    members = 2 * FUSED_CHIPS
    me = lax.axis_index("seq")
    chip, core = me // 2, me % 2
    partner = chip * 2 + 1 - core
    first_core = core == 0
    rows, inner = xc.shape
    wide = bconv.shape[1]
    heads = rate_ref.shape[1]
    pairs = inner // LANES
    chunks = rows // CHUNK
    half = pairs // 2
    steps = pairs // 2

    def place(i):
        m = lax.rem(chip // 2 + 1 + i // 2, half // 2)
        mine = i % 2
        owner = mine * core + (1 - mine) * (1 - core)
        return m, owner * (half // 2) + m

    def quad_lanes(i):
        return pl.ds(pl.multiple_of(place(i)[1] * QUAD, QUAD), QUAD)

    def load(i):
        lanes = quad_lanes(i)
        return pltpu.make_async_copy(
            x_hbm.at[:, lanes], xbuf.at[pl.ds(PAD, rows), lanes], load_sem.at[i]
        )

    small = [
        pltpu.make_async_copy(b_hbm, bbuf.at[pl.ds(PAD, rows)], small_sem.at[0]),
        pltpu.make_async_copy(c_hbm, cbuf.at[pl.ds(PAD, rows)], small_sem.at[1]),
    ]
    params = [
        pltpu.make_async_copy(src, dst, param_sem.at[i])
        for i, (src, dst) in enumerate((
            (rate_hbm, rate_ref), (bias_hbm, bias_ref), (gain_hbm, gain_ref), (raw_hbm, raw_ref),
            (kx_hbm, kx_ref), (kb_hbm, kb_ref), (kc_hbm, kc_ref),
        ))
    ]
    for copy in params + small[:1]:
        copy.start()
    for i in range(steps):
        load(i).start()
    small[1].start()

    barrier = pltpu.get_barrier_semaphore()
    for off in range(1, members):
        pl.semaphore_signal(
            barrier, inc=1, device_id={"seq": lax.rem(me + off, members)},
            device_id_type=pl.DeviceIdType.MESH,
        )

    def remote(src, dst, send, recv, to):
        return pltpu.make_async_remote_copy(
            src_ref=src, dst_ref=dst, send_sem=send, recv_sem=recv, device_id={"seq": to},
            device_id_type=pl.DeviceIdType.MESH,
        )

    after = lax.rem(me + 1, members)
    tails = [
        remote(h.at[pl.ds(rows - PAD, PAD)], v.at[pl.ds(0, PAD)], tail_send.at[i], tail_recv.at[i], after)
        for i, (h, v) in enumerate(((x_hbm, xbuf), (b_hbm, bbuf), (c_hbm, cbuf)))
    ]

    expand[...] = expander(heads, inner // heads, 2)
    for copy in params:
        copy.wait()
    high, middle = split_low(jnp.broadcast_to(gain_ref[...], (8, heads)))
    low = (gain_ref[...] - high.astype(f32) - middle.astype(f32)).astype(bf16)
    gains[...] = jnp.dot(
        jnp.concatenate([high, middle], axis=1), expand[...], preferred_element_type=f32
    ) + jnp.dot(
        jnp.concatenate([low, jnp.zeros_like(low)], axis=1), expand[...], preferred_element_type=f32
    )
    row = lax.broadcasted_iota(jnp.int32, (CHUNK, CHUNK), 0)
    col = lax.broadcasted_iota(jnp.int32, (CHUNK, CHUNK), 1)
    turns = jnp.concatenate([rate_ref[...], bias_ref[...], rate_ref[...], bias_ref[...]], axis=1)
    turns = jnp.broadcast_to(turns, (CHUNK, CHUNK)).T
    speed = jnp.exp(turns[:heads]) * LOG2E
    bias = turns[heads : 2 * heads]
    upper = (row <= col).astype(bf16)
    pl.semaphore_wait(barrier, members - 1)

    @pl.when(me < members - 1)
    def _():
        for copy in tails:
            copy.start()

    chunk_falls, chunk_growth = [], []
    before = jnp.zeros((1, heads), f32)
    for q in range(chunks):
        span = slice(q * CHUNK, (q + 1) * CHUNK)
        shifted = raw_ref[:, span] + bias
        dt = jnp.maximum(shifted, 0.0) + jnp.log1p(jnp.exp(-jnp.abs(shifted)))
        logdec = -speed * dt
        part0 = logdec.astype(bf16)
        rest = logdec - part0.astype(f32)
        part1 = rest.astype(bf16)
        part2 = (rest - part1.astype(f32)).astype(bf16)
        sums = jnp.dot(
            jnp.concatenate([part0, part1, part2], axis=0), upper, preferred_element_type=f32
        )
        cum = sums[:heads] + sums[heads : 2 * heads] + sums[2 * heads :]
        total = jnp.broadcast_to(cum[:, CHUNK - 1 :], cum.shape)
        shift = cum - jnp.log(dt) * LOG2E
        flat = jnp.concatenate(
            [cum, shift, cum, jnp.exp2(total - shift)], axis=0
        )
        stood = flat.T
        turned[q] = flat
        aux[q] = stood
        factors[span, :] = stood[:, 3 * heads :].astype(bf16)
        chunk_growth.append(jnp.exp2(before))
        before = before + stood[CHUNK - 1 :, :heads]
        chunk_falls.append(jnp.exp2(stood[CHUNK - 1 :, :heads]))
    high, low = split_low(jnp.concatenate(chunk_falls, axis=0))
    falls[...] = jnp.dot(
        jnp.concatenate([high, low], axis=1), expand[...], preferred_element_type=f32
    )
    high, low = split_low(jnp.concatenate(chunk_growth, axis=0))
    growth[...] = jnp.dot(
        jnp.concatenate([high, low], axis=1), expand[...], preferred_element_type=f32
    )
    high, low = split_low(jnp.broadcast_to(jnp.exp2(before), (8, heads)))
    zero = jnp.zeros_like(high)
    high = jnp.dot(jnp.concatenate([high, zero], axis=1), expand[...], preferred_element_type=f32)
    low = jnp.dot(jnp.concatenate([low, zero], axis=1), expand[...], preferred_element_type=f32)
    ends[...] = jnp.concatenate([high, low], axis=0).astype(bf16)
    def fill(buf, slot, at, count, lanes):
        slot[at : at + count, :] = buf[at : at + count, lanes].astype(f32)

    def convolve(taps_ref, slot, q, lanes):
        taps = 0.5 * taps_ref[:, lanes]
        count = taps.shape[0]
        at = PAD - count + 1 + q * CHUNK
        total = taps[0:1] * slot[at : at + CHUNK, :]
        for k in range(1, count):
            total = total + taps[k : k + 1] * slot[at + k : at + k + CHUNK, :]
        return total + total * jnp.tanh(total)

    everything = slice(0, LANES)

    def small_chunk(q):
        span = slice(q * CHUNK, (q + 1) * CHUNK)
        bconv[span, :] = convolve(kb_ref, window_b.at[0], q, everything).astype(bf16)
        cconv[span, :] = convolve(kc_ref, window_b.at[1], q, everything).astype(bf16)

    def part_lanes(i, part):
        return pl.ds(pl.multiple_of(place(i)[1] * QUAD + part * LANES, LANES), LANES)

    def fill_chunk(i, win, q):
        for part in range(2):
            fill(xbuf, win.at[part], PAD + q * CHUNK, CHUNK, part_lanes(i, part))

    def convolve_chunk(i, win, scaled, q):
        span = slice(q * CHUNK, (q + 1) * CHUNK)
        spread = jnp.dot(
            factors[span, :], expand[:heads, quad_lanes(i)], preferred_element_type=f32
        )
        for part in range(2):
            lanes = part_lanes(i, part)
            piece = slice(part * LANES, (part + 1) * LANES)
            done = convolve(kx_ref, win.at[part], q, lanes)
            xc[span, lanes] = done.astype(bf16)
            scaled[span, piece] = (done * spread[:, piece]).astype(bf16)

    small[0].wait()
    small[1].wait()
    fill(bbuf, window_b.at[0], PAD, rows, everything)
    fill(cbuf, window_b.at[1], PAD, rows, everything)
    for q in range(1, chunks):
        small_chunk(q)
    load(0).wait()
    for q in range(chunks):
        fill_chunk(0, window_a, q)
    for q in range(1, chunks):
        convolve_chunk(0, window_a, scaled_a, q)

    @pl.when(me > 0)
    def _():
        for copy in tails:
            copy.wait_recv()

    @pl.when(me == 0)
    def _():
        xbuf[0:PAD, :] = jnp.zeros((PAD, inner), bf16)
        bbuf[0:PAD, :] = jnp.zeros((PAD, wide), bf16)
        cbuf[0:PAD, :] = jnp.zeros((PAD, wide), bf16)

    fill(bbuf, window_b.at[0], 0, PAD, everything)
    fill(cbuf, window_b.at[1], 0, PAD, everything)
    small_chunk(0)
    for part in range(2):
        fill(xbuf, window_a.at[part], 0, PAD, part_lanes(0, part))
    convolve_chunk(0, window_a, scaled_a, 0)
    for q in range(chunks):
        span = slice(q * CHUNK, (q + 1) * CHUNK)
        btrans[:, span] = bconv[span, :].astype(f32).T.astype(bf16)

    def state_chunk(i, scaled, q, held):
        span = slice(q * CHUNK, (q + 1) * CHUNK)
        lanes = quad_lanes(i)
        prefix[q, :, lanes] = held.astype(bf16)
        return falls[q : q + 1, lanes] * held + jnp.dot(
            btrans[:, span], scaled[span, :], preferred_element_type=f32
        )

    def state_and_next(i, scaled, following):
        held = jnp.zeros((wide, QUAD), f32)
        if following is not None:
            win, into = following
            for part in range(2):
                fill(xbuf, win.at[part], 0, PAD, part_lanes(i + 1, part))
        for q in range(chunks):
            if following is not None:
                fill_chunk(i + 1, win, q)
                convolve_chunk(i + 1, win, into, q)
            held = state_chunk(i, scaled, q, held)
        held = held.astype(bf16)
        tip = ends[:, quad_lanes(i)]
        first = place(i)[1] * 2
        for part in range(2):
            piece = slice(part * LANES, (part + 1) * LANES)
            run[first + part, 0:wide, :] = held[:, piece]
            run[first + part, wide:, :] = tip[:, piece]

    def to_core(m):
        return remote(
            run.at[pl.ds((1 - core) * half + 2 * m, 2)], core_got.at[pl.ds(2 * m, 2)],
            core_send.at[m], core_recv.at[m], partner,
        )

    def give(other):
        return remote(
            chip_sum.at[other], got.at[chip], give_send.at[other], give_recv.at[chip],
            other * 2 + core,
        )

    def given(other):
        return remote(
            chip_sum.at[other], got.at[other], give_send.at[other], give_recv.at[other],
            other * 2 + core,
        )

    def take(other):
        return remote(
            entered.at[other], back.at[chip], take_send.at[other], take_recv.at[chip],
            other * 2 + core,
        )

    def taken(other):
        return remote(
            entered.at[other], back.at[other], take_send.at[other], take_recv.at[other],
            other * 2 + core,
        )

    def last():
        return remote(
            core_out, arrived, last_send.at[0], last_recv.at[0], partner,
        )

    def decay_of(piece):
        return piece[wide : wide + 1].astype(f32) + piece[wide + 8 : wide + 9].astype(f32)

    def add_cores(m):
        to_core(m).wait_recv()
        for part in range(2):
            j = 2 * m + part
            mine, other = run[core * half + j], core_got[j]
            lead = jnp.where(first_core, mine.astype(f32), other.astype(f32))
            trail = jnp.where(first_core, other.astype(f32), mine.astype(f32))
            fall = trail[wide : wide + 1] + trail[wide + 8 : wide + 9]
            whole = (lead[wide : wide + 1] + lead[wide + 8 : wide + 9]) * fall
            high, low = split_low(jnp.broadcast_to(whole, (8, LANES)))
            chip_sum[j, 0:wide, :] = (fall * lead[:wide] + trail[:wide]).astype(bf16)
            chip_sum[j, wide:, :] = jnp.concatenate(
                [high.astype(f32), low.astype(f32)], axis=0
            ).astype(bf16)

            @pl.when(j != chip)
            def _():
                give(j).start()

            @pl.when(j == chip)
            def _():
                got[chip] = chip_sum[chip]

    def others(act):
        for off in range(1, FUSED_CHIPS):
            act(lax.rem(chip + off, FUSED_CHIPS))

    def scan_chips():
        others(lambda k: given(k).wait_recv())
        value = jnp.zeros((wide, LANES), f32)
        for k in range(FUSED_CHIPS):
            entered[k] = value.astype(bf16)
            if k < FUSED_CHIPS - 1:
                piece = got[k]
                value = decay_of(piece) * value + piece[:wide].astype(f32)
        others(lambda k: take(k).start())
        back[chip] = entered[chip]

    def split_cores():
        others(lambda k: taken(k).wait_recv())
        for j in range(half):
            lead = jnp.where(
                first_core, run[core * half + j].astype(f32), core_got[j].astype(f32)
            )
            entering = back[j].astype(f32)
            fall = lead[wide : wide + 1] + lead[wide + 8 : wide + 9]
            later = fall * entering + lead[:wide]
            core_out[j] = jnp.where(first_core, later, entering).astype(bf16)
            incoming[core * half + j] = jnp.where(first_core, entering, later).astype(bf16)
        last().start()

    @pl.loop(0, steps // 2)
    def _(k):
        i = 2 * k
        load(i + 1).wait()
        state_and_next(i, scaled_a, (window_b, scaled_b))
        to_core(place(i)[0]).start()

        @pl.when(k < steps // 2 - 1)
        def _():
            load(i + 2).wait()
            state_and_next(i + 1, scaled_b, (window_a, scaled_a))

        @pl.when(k == steps // 2 - 1)
        def _():
            state_and_next(i + 1, scaled_b, None)

        add_cores(place(i + 1)[0])

    @pl.when(me < members - 1)
    def _():
        for copy in tails:
            copy.wait_send()

    left = lax.broadcasted_iota(jnp.int32, (CHUNK, LANES), 1) < LANES // 2

    @pl.loop(0, chunks)
    def _(q):
        at = pl.ds(pl.multiple_of(q * CHUNK, CHUNK), CHUNK)
        cc = cconv[at, :]
        gram = lax.dot_general(
            cc, bconv[at, :], (((1,), (1,)), ((), ())), preferred_element_type=f32
        )
        gram = jnp.where(row >= col, gram, 0.0).astype(bf16)
        grow_row = growth[pl.ds(q, 1), :]
        for g in range(pairs // 2):
            wider = slice(g * QUAD, (g + 1) * QUAD)
            carried = jnp.dot(cc, prefix[q, :, wider], preferred_element_type=f32)
            for part in range(2):
                j = 2 * g + part
                lanes = slice(j * LANES, (j + 1) * LANES)
                values = xc[at, lanes]
                weights, cums = [], []
                for h in (2 * j, 2 * j + 1):
                    cum = jnp.broadcast_to(aux[q, :, h : h + 1], (CHUNK, CHUNK))
                    cums.append(cum)
                    grow = jnp.exp2(cum - turned[q, heads + h : heads + h + 1, :]).astype(bf16)
                    weights.append(gram * jnp.minimum(grow, jnp.asarray(BIG, bf16)))
                zero = jnp.zeros_like(values)
                both = jnp.concatenate(
                    [jnp.where(left, values, zero), jnp.where(left, zero, values)], axis=0
                )
                mixed = jnp.dot(jnp.concatenate(weights, axis=1), both, preferred_element_type=f32)
                decay = jnp.exp2(jnp.where(left, cums[0], cums[1]))
                y[at, lanes] = (
                    mixed + decay * carried[:, part * LANES : (part + 1) * LANES]
                    + gains[0:1, lanes] * values.astype(f32)
                )
                decays[at, lanes] = decay * grow_row[:, lanes]

        @pl.when(q == SCAN_AT)
        def _():
            scan_chips()

        @pl.when(q == SPLIT_AT)
        def _():
            split_cores()

    for m in range(half // 2):
        to_core(m).wait_send()
    others(lambda k: give(k).wait_send())
    others(lambda k: take(k).wait_send())
    last().wait()
    incoming[pl.ds((1 - core) * half, half)] = arrived[...]


SCAN_AT = 1
SPLIT_AT = 6


def output_kernel(y_ref, c_ref, decay_ref, inc_ref, out_hbm, held, store_sem):
    chunks = held.shape[0] // CHUNK

    def store(q):
        at = pl.ds(q * CHUNK, CHUNK)
        return pltpu.make_async_copy(held.at[at], out_hbm.at[at], store_sem.at[q])

    for q in range(chunks):
        at = slice(q * CHUNK, (q + 1) * CHUNK)
        cc = c_ref[at, :]
        for g in range(inc_ref.shape[0] // 2):
            wider = slice(g * QUAD, (g + 1) * QUAD)
            entering = jnp.concatenate([inc_ref[2 * g], inc_ref[2 * g + 1]], axis=1)
            carried = jnp.dot(cc, entering, preferred_element_type=jnp.float32)
            held[at, wider] = (y_ref[at, wider] + decay_ref[at, wider] * carried).astype(jnp.bfloat16)
        store(q).start()
    for q in range(chunks):
        store(q).wait()


def fused(inner_x, input_map, output_map, raw, kernel_x, kernel_b, kernel_c, rate, bias, gain):
    rows, inner = inner_x.shape
    wide = input_map.shape[1]
    heads = rate.shape[1]
    pairs = inner // LANES
    half = pairs // 2
    chunks = rows // CHUNK
    f32, bf16 = jnp.float32, jnp.bfloat16
    far = pl.BlockSpec(memory_space=pltpu.HBM)
    near = pl.BlockSpec(memory_space=pltpu.VMEM)
    tall = wide + DECAY_ROWS
    chips = FUSED_CHIPS
    dma = pltpu.SemaphoreType.DMA
    y, cconv, decays, incoming = pl.pallas_call(
        fused_kernel,
        in_specs=[far] * 10,
        out_specs=[near] * 4,
        out_shape=[
            pltpu.VMEM((rows, inner), f32), pltpu.VMEM((rows, wide), bf16),
            pltpu.VMEM((rows, inner), f32), pltpu.VMEM((pairs, wide, LANES), bf16),
        ],
        scratch_shapes=[
            pltpu.VMEM(raw.shape, f32), pltpu.VMEM(kernel_x.shape, f32),
            pltpu.VMEM(kernel_b.shape, f32), pltpu.VMEM(kernel_c.shape, f32),
            pltpu.VMEM(rate.shape, f32), pltpu.VMEM(bias.shape, f32), pltpu.VMEM(gain.shape, f32),
            pltpu.VMEM((PAD + rows, inner), bf16), pltpu.VMEM((PAD + rows, wide), bf16),
            pltpu.VMEM((PAD + rows, wide), bf16), pltpu.VMEM((rows, inner), bf16),
            pltpu.VMEM((rows, wide), bf16), pltpu.VMEM((chunks, CHUNK, LANES), f32),
            pltpu.VMEM((chunks, LANES, CHUNK), f32), pltpu.VMEM((2 * heads, inner), bf16),
            pltpu.VMEM((8, inner), f32), pltpu.VMEM((chunks, inner), f32),
            pltpu.VMEM((DECAY_ROWS, inner), bf16), pltpu.VMEM((rows, heads), bf16),
            pltpu.VMEM((chunks, inner), f32), pltpu.VMEM((wide, rows), bf16),
            pltpu.VMEM((chunks, wide, inner), bf16), pltpu.VMEM((2, rows + PAD, LANES), f32),
            pltpu.VMEM((2, rows + PAD, LANES), f32), pltpu.VMEM((rows, QUAD), bf16),
            pltpu.VMEM((rows, QUAD), bf16),
            pltpu.VMEM((pairs, tall, LANES), bf16), pltpu.VMEM((half, tall, LANES), bf16),
            pltpu.VMEM((chips, tall, LANES), bf16), pltpu.VMEM((chips, tall, LANES), bf16),
            pltpu.VMEM((chips, wide, LANES), bf16), pltpu.VMEM((chips, wide, LANES), bf16),
            pltpu.VMEM((half, wide, LANES), bf16), pltpu.VMEM((half, wide, LANES), bf16),
            dma((pairs // 2,)), dma((2,)), dma((7,)), dma((3,)), dma((3,)), dma((half // 2,)),
            dma((half // 2,)), dma((chips,)), dma((chips,)), dma((chips,)), dma((chips,)),
            dma((1,)), dma((1,)),
        ],
        compiler_params=pltpu.CompilerParams(
            vmem_limit_bytes=FUSED_VMEM, collective_id=0, has_side_effects=True
        ),
        name="fused_mixer",
    )(inner_x, input_map, output_map, raw, kernel_x, kernel_b, kernel_c, rate, bias, gain)
    return pl.pallas_call(
        output_kernel,
        in_specs=[near] * 4,
        out_specs=pl.BlockSpec(memory_space=pl.ANY),
        out_shape=jax.ShapeDtypeStruct((rows, inner), bf16),
        scratch_shapes=[pltpu.VMEM((rows, inner), bf16), dma((chunks,))],
        compiler_params=pltpu.CompilerParams(vmem_limit_bytes=OUTPUT_VMEM),
        name="output_rows",
    )(y, cconv, decays, incoming)


FUSED_VMEM = (47 << 20) + (160 << 10)
OUTPUT_VMEM = 16 << 20


def on_device(
    inner_x, input_map, output_map, step_raw, kernel_x, kernel_b, kernel_c, log_rate, step_bias,
    skip_gain,
):
    rows, inner = inner_x.shape
    heads = log_rate.shape[0]
    members = lax.axis_size("seq")
    if members == 2 * FUSED_CHIPS and inner == members * LANES and rows % ROWS == 0:
        return fused(
            inner_x, input_map, output_map, step_raw.T, kernel_x, kernel_b, kernel_c,
            log_rate[None, :], step_bias[None, :], skip_gain[None, :],
        )
    last = jnp.concatenate([a[rows - HALO :] for a in (inner_x, input_map, output_map)], axis=1)
    tail = lax.ppermute(last, "seq", [(i, i + 1) for i in range(members - 1)])
    xconv, bc, aux, prefix, run = local_states(
        inner_x, input_map, output_map, step_raw, tail, kernel_x, kernel_b, kernel_c,
        log_rate[None, :], step_bias[None, :],
    )
    gain = jnp.repeat(skip_gain, inner // heads)[None, :]
    half = rows // CHUNK // 2
    got = exchange(regroup(run, members))
    ya = local_mix(0, half, xconv, bc, aux, prefix, gain)
    got, ya = lax.optimization_barrier((got, ya))
    back = exchange(scan_members(got))
    yb = local_mix(half, half, xconv, bc, aux, prefix, gain)
    incoming = regroup(back, inner // LANES)
    return finish(heads, ya, yb, bc, aux, incoming)


def solution(mesh):
    split = P(("groups", "seq"), None)
    return jax.shard_map(
        on_device, mesh=mesh, in_specs=(split,) * 4 + (P(),) * 6, out_specs=split, check_vma=False
    )
```

```python
import functools

import jax
import jax.numpy as jnp
from jax import lax
from jax.experimental import pallas as pl
from jax.experimental.pallas import tpu as pltpu
from jax.sharding import PartitionSpec as P

CHUNK = 128
ROWS = 256
LANES = 128
LOG2E = 1.4426950408889634
HALO = 8
VMEM_LIMIT = 60 << 20
DECAY_ROWS = 16


def split_low(value):
    high = value.astype(jnp.bfloat16)
    return high, (value - high.astype(jnp.float32)).astype(jnp.bfloat16)


def silu(value):
    half = 0.5 * value
    return half + half * jnp.tanh(half)


def expander(heads, width, parts):
    shape = (parts * heads, heads * width)
    row = lax.broadcasted_iota(jnp.int32, shape, 0) % heads
    col = lax.broadcasted_iota(jnp.int32, shape, 1) // width
    return (row == col).astype(jnp.bfloat16)


def state_kernel(
    heads, x_ref, b_ref, c_ref, raw_ref, tail_ref, kx_ref, kb_ref, kc_ref, rate_ref, bias_ref,
    xconv_ref, bc_ref, aux_ref, prefix_ref, run_ref,
    xwin, bwin, cwin, spread, scaled, expand, state, logrun,
):
    step = pl.program_id(0)
    inner = x_ref.shape[1]
    wide = b_ref.shape[1]
    pairs = inner // LANES

    @pl.when(step == 0)
    def _():
        tail = tail_ref[...].astype(jnp.float32)
        xwin[0:HALO, :] = tail[:, :inner]
        bwin[0:HALO, :] = tail[:, inner : inner + wide]
        cwin[0:HALO, :] = tail[:, inner + wide :]
        expand[...] = expander(heads, inner // heads, 2)
        state[...] = jnp.zeros_like(state)
        logrun[...] = jnp.zeros_like(logrun)

    @pl.when(step > 0)
    def _():
        xwin[0:HALO, :] = xwin[ROWS : ROWS + HALO, :]
        bwin[0:HALO, :] = bwin[ROWS : ROWS + HALO, :]
        cwin[0:HALO, :] = cwin[ROWS : ROWS + HALO, :]

    bwin[HALO:, :] = b_ref[...].astype(jnp.float32)
    cwin[HALO:, :] = c_ref[...].astype(jnp.float32)

    def small_conv(win, taps):
        count = taps.shape[0]
        total = jnp.zeros((ROWS, win.shape[1]), jnp.float32)
        for k in range(count):
            at = HALO - (count - 1) + k
            total = total + taps[k : k + 1, :] * win[at : at + ROWS, :]
        return silu(total).astype(jnp.bfloat16)

    bconv = small_conv(bwin, kb_ref)
    cconv = small_conv(cwin, kc_ref)
    bc_ref[:, :wide] = bconv
    bc_ref[:, wide:] = cconv

    shifted = raw_ref[...] + bias_ref[...]
    dt = jnp.maximum(shifted, 0.0) + jnp.log1p(jnp.exp(-jnp.abs(shifted)))
    logdec = -(jnp.exp(rate_ref[...]) * LOG2E) * dt
    part0, rest = logdec.astype(jnp.bfloat16), None
    rest = logdec - part0.astype(jnp.float32)
    part1 = rest.astype(jnp.bfloat16)
    part2 = (rest - part1.astype(jnp.float32)).astype(jnp.bfloat16)
    row = lax.broadcasted_iota(jnp.int32, (CHUNK, CHUNK), 0)
    col = lax.broadcasted_iota(jnp.int32, (CHUNK, CHUNK), 1)
    lower = (row >= col).astype(jnp.bfloat16)
    parts = jnp.concatenate([part0, part1, part2, jnp.zeros_like(part0)], axis=1)
    logdt = jnp.log(dt) * LOG2E
    totals = []
    for q in range(ROWS // CHUNK):
        span = slice(q * CHUNK, (q + 1) * CHUNK)
        sums = jnp.dot(lower, parts[span], preferred_element_type=jnp.float32)
        cum = sums[:, :heads] + sums[:, heads : 2 * heads] + sums[:, 2 * heads : 3 * heads]
        total = cum[CHUNK - 1 :, :]
        totals.append(total)
        shift = cum - logdt[span]
        run = logrun[...] + cum
        logrun[...] = logrun[...] + total
        aux_ref[span, :] = jnp.concatenate([cum, shift, run, jnp.zeros_like(run)], axis=1)
        high, low = split_low(jnp.exp2(total - shift))
        spread[span, :] = jnp.dot(
            jnp.concatenate([high, low], axis=1), expand[...], preferred_element_type=jnp.float32
        )

    @pl.loop(0, pairs)
    def _(j):
        lanes = pl.ds(pl.multiple_of(j * LANES, LANES), LANES)
        xwin[HALO:, lanes] = x_ref[:, lanes].astype(jnp.float32)
        count = kx_ref.shape[0]
        total = jnp.zeros((ROWS, LANES), jnp.float32)
        for k in range(count):
            at = HALO - (count - 1) + k
            total = total + kx_ref[k : k + 1, lanes] * xwin[at : at + ROWS, lanes]
        xc = silu(total).astype(jnp.bfloat16)
        xconv_ref[:, lanes] = xc
        scaled[:, lanes] = (xc.astype(jnp.float32) * spread[:, lanes]).astype(jnp.bfloat16)

    btrans = bconv.astype(jnp.float32).T.astype(jnp.bfloat16)
    for q in range(ROWS // CHUNK):
        span = slice(q * CHUNK, (q + 1) * CHUNK)
        prefix_ref[q] = state[...].astype(jnp.bfloat16)
        factor = jnp.broadcast_to(jnp.exp2(totals[q]), (8, heads))
        high, low = split_low(factor)
        decay = jnp.dot(
            jnp.concatenate([high, low], axis=1), expand[...], preferred_element_type=jnp.float32
        )[0:1, :]
        state[...] = decay * state[...] + jnp.dot(
            btrans[:, span], scaled[span, :], preferred_element_type=jnp.float32
        )

    @pl.when(step == pl.num_programs(0) - 1)
    def _():
        high, low = split_low(jnp.broadcast_to(jnp.exp2(logrun[...]), (8, heads)))
        zero = jnp.zeros_like(high)
        high = jnp.dot(jnp.concatenate([high, zero], axis=1), expand[...], preferred_element_type=jnp.float32)
        low = jnp.dot(jnp.concatenate([low, zero], axis=1), expand[...], preferred_element_type=jnp.float32)
        both = jnp.concatenate([high, low], axis=0).astype(jnp.bfloat16)
        for j in range(pairs):
            lanes = slice(j * LANES, (j + 1) * LANES)
            run_ref[j, 0 : state.shape[0], :] = state[:, lanes].astype(jnp.bfloat16)
            run_ref[j, state.shape[0] :, :] = both[:, lanes]


def local_states(x, b, c, raw, tail, kx, kb, kc, rate, bias):
    rows, inner = x.shape
    wide = b.shape[1]
    heads = raw.shape[1]
    pairs = inner // LANES
    whole = lambda a: pl.BlockSpec(a.shape, lambda i: (0,) * a.ndim)
    block = lambda w: pl.BlockSpec((ROWS, w), lambda i: (i, 0))
    per = ROWS // CHUNK
    f32, bf16 = jnp.float32, jnp.bfloat16
    return pl.pallas_call(
        functools.partial(state_kernel, heads),
        grid=(rows // ROWS,),
        in_specs=[block(inner), block(wide), block(wide), block(heads), whole(tail), whole(kx),
                  whole(kb), whole(kc), whole(rate), whole(bias)],
        out_specs=[
            block(inner), block(2 * wide), block(LANES),
            pl.BlockSpec((per, wide, inner), lambda i: (i, 0, 0)),
            pl.BlockSpec((pairs, wide + DECAY_ROWS, LANES), lambda i: (0, 0, 0)),
        ],
        out_shape=[
            jax.ShapeDtypeStruct((rows, inner), bf16),
            jax.ShapeDtypeStruct((rows, 2 * wide), bf16),
            jax.ShapeDtypeStruct((rows, LANES), f32),
            jax.ShapeDtypeStruct((rows // CHUNK, wide, inner), bf16),
            jax.ShapeDtypeStruct((pairs, wide + DECAY_ROWS, LANES), bf16),
        ],
        scratch_shapes=[
            pltpu.VMEM((ROWS + HALO, inner), f32), pltpu.VMEM((ROWS + HALO, wide), f32),
            pltpu.VMEM((ROWS + HALO, wide), f32), pltpu.VMEM((ROWS, inner), f32),
            pltpu.VMEM((ROWS, inner), bf16), pltpu.VMEM((2 * heads, inner), bf16),
            pltpu.VMEM((wide, inner), f32), pltpu.VMEM((1, heads), f32),
        ],
        compiler_params=pltpu.CompilerParams(vmem_limit_bytes=VMEM_LIMIT),
        cost_estimate=pl.CostEstimate(flops=2 * 10**9, bytes_accessed=12 << 20, transcendentals=1 << 21),
        name="local_states",
    )(x, b, c, raw, tail, kx, kb, kc, rate, bias)


def inner_kernel(heads, xconv_ref, bc_ref, aux_ref, prefix_ref, gain_ref, y_ref):
    wide = bc_ref.shape[1] // 2
    pairs = xconv_ref.shape[1] // LANES
    aux = aux_ref[...]
    turned = aux.T
    bconv, cconv = bc_ref[:, :wide], bc_ref[:, wide:]
    row = lax.broadcasted_iota(jnp.int32, (CHUNK, CHUNK), 0)
    col = lax.broadcasted_iota(jnp.int32, (CHUNK, CHUNK), 1)
    gram = lax.dot_general(cconv, bconv, (((1,), (1,)), ((), ())), preferred_element_type=jnp.float32)
    gram = jnp.where(row >= col, gram, 0.0)
    left = lax.broadcasted_iota(jnp.int32, (CHUNK, LANES), 1) < LANES // 2
    for j in range(pairs):
        lanes = slice(j * LANES, (j + 1) * LANES)
        xc = xconv_ref[:, lanes]
        weights = []
        cums = []
        for h in (2 * j, 2 * j + 1):
            cum = jnp.broadcast_to(aux[:, h : h + 1], (CHUNK, CHUNK))
            cums.append(cum)
            power = jnp.minimum(cum - turned[heads + h : heads + h + 1, :], 126.0)
            weights.append((gram * jnp.exp2(power)).astype(jnp.bfloat16))
        zero = jnp.zeros_like(xc)
        both = jnp.concatenate([jnp.where(left, xc, zero), jnp.where(left, zero, xc)], axis=0)
        inner = jnp.dot(jnp.concatenate(weights, axis=1), both, preferred_element_type=jnp.float32)
        carried = jnp.dot(cconv, prefix_ref[0, :, lanes], preferred_element_type=jnp.float32)
        decay = jnp.exp2(jnp.where(left, cums[0], cums[1]))
        y_ref[:, lanes] = inner + decay * carried + gain_ref[:, lanes] * xc.astype(jnp.float32)


def local_mix(first, count, xconv, bc, aux, prefix, gain):
    inner = xconv.shape[1]
    heads = gain.shape[1] // 64
    wide = bc.shape[1] // 2
    block = lambda w: pl.BlockSpec((CHUNK, w), lambda i: (i + first, 0))
    return pl.pallas_call(
        functools.partial(inner_kernel, heads),
        grid=(count,),
        in_specs=[block(inner), block(2 * wide), block(LANES),
                  pl.BlockSpec((1, wide, inner), lambda i: (i + first, 0, 0)),
                  pl.BlockSpec((1, inner), lambda i: (0, 0))],
        out_specs=pl.BlockSpec((CHUNK, inner), lambda i: (i, 0)),
        out_shape=jax.ShapeDtypeStruct((count * CHUNK, inner), jnp.float32),
        compiler_params=pltpu.CompilerParams(vmem_limit_bytes=VMEM_LIMIT),
        cost_estimate=pl.CostEstimate(flops=10**10, bytes_accessed=24 << 20, transcendentals=1 << 22),
        name="local_mix",
    )(xconv, bc, aux, prefix, gain)


def scan_kernel(got_ref, out_ref):
    members, rows, width = out_ref.shape
    entering = jnp.zeros((rows, width), jnp.float32)
    for k in range(members):
        out_ref[k] = entering.astype(jnp.bfloat16)
        decay = got_ref[k, rows : rows + 1, :].astype(jnp.float32) + got_ref[
            k, rows + 8 : rows + 9, :
        ].astype(jnp.float32)
        entering = decay * entering + got_ref[k, 0:rows, :].astype(jnp.float32)


def scan_members(got):
    members, rows, width = got.shape
    return pl.pallas_call(
        scan_kernel,
        out_shape=jax.ShapeDtypeStruct((members, rows - DECAY_ROWS, width), jnp.bfloat16),
        compiler_params=pltpu.CompilerParams(vmem_limit_bytes=VMEM_LIMIT),
        name="scan_members",
    )(got)


def finish_kernel(heads, ya_ref, yb_ref, bc_ref, aux_ref, inc_ref, out_ref, expand):
    wide = bc_ref.shape[1] // 2
    pairs = out_ref.shape[1] // LANES

    @pl.when(pl.program_id(0) == 0)
    def _():
        expand[...] = expander(heads, out_ref.shape[1] // heads, 2)

    high, low = split_low(jnp.exp2(aux_ref[:, 2 * heads : 3 * heads]))
    factors = jnp.concatenate([high, low], axis=1)
    cconv = bc_ref[:, wide:]
    early = pl.program_id(0) < pl.num_programs(0) // 2

    def emit(y_ref):
        for j in range(pairs):
            lanes = slice(j * LANES, (j + 1) * LANES)
            decay = jnp.dot(factors, expand[:, lanes], preferred_element_type=jnp.float32)
            carried = jnp.dot(cconv, inc_ref[j], preferred_element_type=jnp.float32)
            out_ref[:, lanes] = (y_ref[:, lanes] + decay * carried).astype(jnp.bfloat16)

    @pl.when(early)
    def _():
        emit(ya_ref)

    @pl.when(jnp.logical_not(early))
    def _():
        emit(yb_ref)


def finish(heads, ya, yb, bc, aux, inc):
    rows, inner = bc.shape[0], ya.shape[1]
    wide = bc.shape[1] // 2
    steps = rows // CHUNK
    half = steps // 2
    block = lambda w: pl.BlockSpec((CHUNK, w), lambda i: (i, 0))
    return pl.pallas_call(
        functools.partial(finish_kernel, heads),
        grid=(steps,),
        in_specs=[
            pl.BlockSpec((CHUNK, inner), lambda i: (jnp.minimum(i, half - 1), 0)),
            pl.BlockSpec((CHUNK, inner), lambda i: (jnp.maximum(i - half, 0), 0)),
            block(2 * wide), block(LANES), pl.BlockSpec(inc.shape, lambda i: (0, 0, 0)),
        ],
        out_specs=block(inner),
        out_shape=jax.ShapeDtypeStruct((rows, inner), jnp.bfloat16),
        scratch_shapes=[pltpu.VMEM((2 * heads, inner), jnp.bfloat16)],
        compiler_params=pltpu.CompilerParams(vmem_limit_bytes=VMEM_LIMIT),
        name="finish",
    )(ya, yb, bc, aux, inc)


def exchange(x):
    return lax.all_to_all(x, "seq", split_axis=0, concat_axis=0, tiled=True)


def regroup(x, count):
    groups, rows, width = x.shape
    if groups == count:
        return x
    flat = x.transpose(1, 0, 2).reshape(rows, groups * width)
    return flat.reshape(rows, count, groups * width // count).transpose(1, 0, 2)


FUSED_CHIPS = 8
PAD = 16
QUAD = 2 * LANES
BIG = 1e38


def fused_kernel(
    x_hbm, b_hbm, c_hbm, raw_hbm, kx_hbm, kb_hbm, kc_hbm, rate_hbm, bias_hbm, gain_hbm,
    y, cconv, decays, incoming,
    raw_ref, kx_ref, kb_ref, kc_ref, rate_ref, bias_ref, gain_ref,
    xbuf, bbuf, cbuf, xc, bconv, aux, turned, expand, gains, falls, ends, factors, growth, btrans, prefix, window_a, window_b,
    scaled_a, scaled_b,
    run, core_got, chip_sum, got, entered, back, core_out, arrived,
    load_sem, small_sem, param_sem, tail_send, tail_recv, core_send, core_recv,
    give_send, give_recv, take_send, take_recv, last_send, last_recv,
):
    f32, bf16 = jnp.float32, jnp.bfloat16
    members = 2 * FUSED_CHIPS
    me = lax.axis_index("seq")
    chip, core = me // 2, me % 2
    partner = chip * 2 + 1 - core
    first_core = core == 0
    rows, inner = xc.shape
    wide = bconv.shape[1]
    heads = rate_ref.shape[1]
    pairs = inner // LANES
    chunks = rows // CHUNK
    half = pairs // 2
    steps = pairs // 2

    after = lax.rem(me + 1, members)

    def place(i, at=None):
        who = me if at is None else at
        m = lax.rem(who // 4 + 1 + i // 2, half // 2)
        mine = i % 2
        owner = mine * (who % 2) + (1 - mine) * (1 - who % 2)
        return m, owner * (half // 2) + m

    def quad_lanes(i):
        return pl.ds(pl.multiple_of(place(i)[1] * QUAD, QUAD), QUAD)

    def load(i):
        lanes = quad_lanes(i)
        return pltpu.make_async_copy(
            x_hbm.at[:, lanes], xbuf.at[pl.ds(PAD, rows), lanes], load_sem.at[i]
        )

    small = [
        pltpu.make_async_copy(b_hbm, bbuf.at[pl.ds(PAD, rows)], small_sem.at[0]),
        pltpu.make_async_copy(c_hbm, cbuf.at[pl.ds(PAD, rows)], small_sem.at[1]),
    ]
    params = [
        pltpu.make_async_copy(src, dst, param_sem.at[i])
        for i, (src, dst) in enumerate((
            (rate_hbm, rate_ref), (bias_hbm, bias_ref), (gain_hbm, gain_ref), (raw_hbm, raw_ref),
            (kx_hbm, kx_ref), (kb_hbm, kb_ref), (kc_hbm, kc_ref),
        ))
    ]
    for copy in params + small[:1]:
        copy.start()
    for i in range(steps):
        load(i).start()
    small[1].start()

    barrier = pltpu.get_barrier_semaphore()
    for off in range(1, members):
        pl.semaphore_signal(
            barrier, inc=1, device_id={"seq": lax.rem(me + off, members)},
            device_id_type=pl.DeviceIdType.MESH,
        )

    def remote(src, dst, send, recv, to):
        return pltpu.make_async_remote_copy(
            src_ref=src, dst_ref=dst, send_sem=send, recv_sem=recv, device_id={"seq": to},
            device_id_type=pl.DeviceIdType.MESH,
        )

    def x_tail(i, at):
        lanes = pl.ds(pl.multiple_of(place(i, at)[1] * QUAD, QUAD), QUAD)
        return remote(
            x_hbm.at[pl.ds(rows - PAD, PAD), lanes], xbuf.at[pl.ds(0, PAD), lanes],
            tail_send.at[i], tail_recv.at[i], after,
        )

    small_tails = [
        remote(
            h.at[pl.ds(rows - PAD, PAD)], v.at[pl.ds(0, PAD)], tail_send.at[steps + k],
            tail_recv.at[steps + k], after,
        )
        for k, (h, v) in enumerate(((b_hbm, bbuf), (c_hbm, cbuf)))
    ]

    expand[...] = expander(heads, inner // heads, 2)
    pl.semaphore_wait(barrier, members - 1)

    @pl.when(me < members - 1)
    def _():
        small_tails[0].start()
        for i in range(steps):
            x_tail(i, after).start()
        small_tails[1].start()

    for copy in params:
        copy.wait()
    high, middle = split_low(jnp.broadcast_to(gain_ref[...], (8, heads)))
    low = (gain_ref[...] - high.astype(f32) - middle.astype(f32)).astype(bf16)
    gains[...] = jnp.dot(
        jnp.concatenate([high, middle], axis=1), expand[...], preferred_element_type=f32
    ) + jnp.dot(
        jnp.concatenate([low, jnp.zeros_like(low)], axis=1), expand[...], preferred_element_type=f32
    )
    row = lax.broadcasted_iota(jnp.int32, (CHUNK, CHUNK), 0)
    col = lax.broadcasted_iota(jnp.int32, (CHUNK, CHUNK), 1)
    turns = jnp.concatenate([rate_ref[...], bias_ref[...], rate_ref[...], bias_ref[...]], axis=1)
    turns = jnp.broadcast_to(turns, (CHUNK, CHUNK)).T
    speed = jnp.exp(turns[:heads]) * LOG2E
    bias = turns[heads : 2 * heads]
    upper = (row <= col).astype(bf16)
    chunk_falls, chunk_growth = [], []
    before = jnp.zeros((1, heads), f32)
    for q in range(chunks):
        span = slice(q * CHUNK, (q + 1) * CHUNK)
        shifted = raw_ref[:, span] + bias
        dt = jnp.maximum(shifted, 0.0) + jnp.log1p(jnp.exp(-jnp.abs(shifted)))
        logdec = -speed * dt
        part0 = logdec.astype(bf16)
        rest = logdec - part0.astype(f32)
        part1 = rest.astype(bf16)
        part2 = (rest - part1.astype(f32)).astype(bf16)
        sums = jnp.dot(
            jnp.concatenate([part0, part1, part2], axis=0), upper, preferred_element_type=f32
        )
        cum = sums[:heads] + sums[heads : 2 * heads] + sums[2 * heads :]
        total = jnp.broadcast_to(cum[:, CHUNK - 1 :], cum.shape)
        shift = cum - jnp.log(dt) * LOG2E
        flat = jnp.concatenate(
            [cum, shift, cum, jnp.exp2(total - shift)], axis=0
        )
        stood = flat.T
        turned[q] = flat
        aux[q] = stood
        factors[span, :] = stood[:, 3 * heads :].astype(bf16)
        chunk_growth.append(jnp.exp2(before))
        before = before + stood[CHUNK - 1 :, :heads]
        chunk_falls.append(jnp.exp2(stood[CHUNK - 1 :, :heads]))
    high, low = split_low(jnp.concatenate(chunk_falls, axis=0))
    falls[...] = jnp.dot(
        jnp.concatenate([high, low], axis=1), expand[...], preferred_element_type=f32
    )
    high, low = split_low(jnp.concatenate(chunk_growth, axis=0))
    growth[...] = jnp.dot(
        jnp.concatenate([high, low], axis=1), expand[...], preferred_element_type=f32
    )
    high, low = split_low(jnp.broadcast_to(jnp.exp2(before), (8, heads)))
    zero = jnp.zeros_like(high)
    high = jnp.dot(jnp.concatenate([high, zero], axis=1), expand[...], preferred_element_type=f32)
    low = jnp.dot(jnp.concatenate([low, zero], axis=1), expand[...], preferred_element_type=f32)
    ends[...] = jnp.concatenate([high, low], axis=0).astype(bf16)
    def fill(buf, slot, at, count, lanes):
        slot[at : at + count, :] = buf[at : at + count, lanes].astype(f32)

    def convolve(taps_ref, slot, q, lanes):
        taps = 0.5 * taps_ref[:, lanes]
        count = taps.shape[0]
        at = PAD - count + 1 + q * CHUNK
        total = taps[0:1] * slot[at : at + CHUNK, :]
        for k in range(1, count):
            total = total + taps[k : k + 1] * slot[at + k : at + k + CHUNK, :]
        return total + total * jnp.tanh(total)

    everything = slice(0, LANES)

    def small_chunk(q):
        span = slice(q * CHUNK, (q + 1) * CHUNK)
        bconv[span, :] = convolve(kb_ref, window_b.at[0], q, everything).astype(bf16)

    def part_lanes(i, part):
        return pl.ds(pl.multiple_of(place(i)[1] * QUAD + part * LANES, LANES), LANES)

    def fill_chunk(i, win, q):
        for part in range(2):
            fill(xbuf, win.at[part], PAD + q * CHUNK, CHUNK, part_lanes(i, part))

    def convolve_chunk(i, win, scaled, q):
        span = slice(q * CHUNK, (q + 1) * CHUNK)
        spread = jnp.dot(
            factors[span, :], expand[:heads, quad_lanes(i)], preferred_element_type=f32
        )
        for part in range(2):
            lanes = part_lanes(i, part)
            piece = slice(part * LANES, (part + 1) * LANES)
            done = convolve(kx_ref, win.at[part], q, lanes)
            xc[span, lanes] = done.astype(bf16)
            scaled[span, piece] = (done * spread[:, piece]).astype(bf16)

    small[0].wait()
    fill(bbuf, window_b.at[0], PAD, rows, everything)
    for q in range(1, chunks):
        small_chunk(q)
    load(0).wait()
    for q in range(chunks):
        fill_chunk(0, window_a, q)
    for q in range(1, chunks):
        convolve_chunk(0, window_a, scaled_a, q)

    def tail_here(copy):
        @pl.when(me > 0)
        def _():
            copy.wait_recv()

    tail_here(small_tails[0])
    tail_here(x_tail(0, me))

    @pl.when(me == 0)
    def _():
        xbuf[0:PAD, :] = jnp.zeros((PAD, inner), bf16)
        bbuf[0:PAD, :] = jnp.zeros((PAD, wide), bf16)
        cbuf[0:PAD, :] = jnp.zeros((PAD, wide), bf16)

    fill(bbuf, window_b.at[0], 0, PAD, everything)
    small_chunk(0)
    for part in range(2):
        fill(xbuf, window_a.at[part], 0, PAD, part_lanes(0, part))
    convolve_chunk(0, window_a, scaled_a, 0)
    for q in range(chunks):
        span = slice(q * CHUNK, (q + 1) * CHUNK)
        btrans[:, span] = bconv[span, :].astype(f32).T.astype(bf16)

    def state_chunk(i, scaled, q, held):
        span = slice(q * CHUNK, (q + 1) * CHUNK)
        lanes = quad_lanes(i)
        prefix[q, :, lanes] = held.astype(bf16)
        return falls[q : q + 1, lanes] * held + jnp.dot(
            btrans[:, span], scaled[span, :], preferred_element_type=f32
        )

    def state_and_next(i, scaled, following):
        held = jnp.zeros((wide, QUAD), f32)
        if following is not None:
            win, into = following
            for part in range(2):
                fill(xbuf, win.at[part], 0, PAD, part_lanes(i + 1, part))
        for q in range(chunks):
            if following is not None:
                fill_chunk(i + 1, win, q)
                convolve_chunk(i + 1, win, into, q)
            held = state_chunk(i, scaled, q, held)
        held = held.astype(bf16)
        tip = ends[:, quad_lanes(i)]
        first = place(i)[1] * 2
        for part in range(2):
            piece = slice(part * LANES, (part + 1) * LANES)
            run[first + part, 0:wide, :] = held[:, piece]
            run[first + part, wide:, :] = tip[:, piece]

    def to_core(m):
        return remote(
            run.at[pl.ds((1 - core) * half + 2 * m, 2)], core_got.at[pl.ds(2 * m, 2)],
            core_send.at[m], core_recv.at[m], partner,
        )

    def give(other):
        return remote(
            chip_sum.at[other], got.at[chip], give_send.at[other], give_recv.at[chip],
            other * 2 + core,
        )

    def given(other):
        return remote(
            chip_sum.at[other], got.at[other], give_send.at[other], give_recv.at[other],
            other * 2 + core,
        )

    def take(other):
        return remote(
            entered.at[other], back.at[chip], take_send.at[other], take_recv.at[chip],
            other * 2 + core,
        )

    def taken(other):
        return remote(
            entered.at[other], back.at[other], take_send.at[other], take_recv.at[other],
            other * 2 + core,
        )

    def last():
        return remote(
            core_out, arrived, last_send.at[0], last_recv.at[0], partner,
        )

    def decay_of(piece):
        return piece[wide : wide + 1].astype(f32) + piece[wide + 8 : wide + 9].astype(f32)

    def add_cores(m):
        to_core(m).wait_recv()
        for part in range(2):
            j = 2 * m + part
            mine, other = run[core * half + j], core_got[j]
            lead = jnp.where(first_core, mine.astype(f32), other.astype(f32))
            trail = jnp.where(first_core, other.astype(f32), mine.astype(f32))
            fall = trail[wide : wide + 1] + trail[wide + 8 : wide + 9]
            whole = (lead[wide : wide + 1] + lead[wide + 8 : wide + 9]) * fall
            high, low = split_low(jnp.broadcast_to(whole, (8, LANES)))
            chip_sum[j, 0:wide, :] = (fall * lead[:wide] + trail[:wide]).astype(bf16)
            chip_sum[j, wide:, :] = jnp.concatenate(
                [high.astype(f32), low.astype(f32)], axis=0
            ).astype(bf16)

            @pl.when(j != chip)
            def _():
                give(j).start()

            @pl.when(j == chip)
            def _():
                got[chip] = chip_sum[chip]

    def others(act):
        for off in range(1, FUSED_CHIPS):
            act(lax.rem(chip + off, FUSED_CHIPS))

    def scan_chips():
        others(lambda k: given(k).wait_recv())
        value = jnp.zeros((wide, LANES), f32)
        for k in range(FUSED_CHIPS):
            entered[k] = value.astype(bf16)
            if k < FUSED_CHIPS - 1:
                piece = got[k]
                value = decay_of(piece) * value + piece[:wide].astype(f32)
        others(lambda k: take(k).start())
        back[chip] = entered[chip]

    def split_cores():
        others(lambda k: taken(k).wait_recv())
        for j in range(half):
            lead = jnp.where(
                first_core, run[core * half + j].astype(f32), core_got[j].astype(f32)
            )
            entering = back[j].astype(f32)
            fall = lead[wide : wide + 1] + lead[wide + 8 : wide + 9]
            later = fall * entering + lead[:wide]
            core_out[j] = jnp.where(first_core, later, entering).astype(bf16)
            incoming[core * half + j] = jnp.where(first_core, entering, later).astype(bf16)
        last().start()

    @pl.loop(0, steps // 2)
    def _(k):
        i = 2 * k
        load(i + 1).wait()
        tail_here(x_tail(i + 1, me))
        state_and_next(i, scaled_a, (window_b, scaled_b))
        to_core(place(i)[0]).start()

        @pl.when(k < steps // 2 - 1)
        def _():
            load(i + 2).wait()
            tail_here(x_tail(i + 2, me))
            state_and_next(i + 1, scaled_b, (window_a, scaled_a))

        @pl.when(k == steps // 2 - 1)
        def _():
            state_and_next(i + 1, scaled_b, None)

        add_cores(place(i + 1)[0])

    @pl.when(me < members - 1)
    def _():
        for i in range(steps):
            x_tail(i, after).wait_send()
        for copy in small_tails:
            copy.wait_send()

    small[1].wait()
    tail_here(small_tails[1])
    fill(cbuf, window_b.at[1], 0, PAD + rows, everything)
    for q in range(chunks):
        span = slice(q * CHUNK, (q + 1) * CHUNK)
        cconv[span, :] = convolve(kc_ref, window_b.at[1], q, everything).astype(bf16)
    left = lax.broadcasted_iota(jnp.int32, (CHUNK, LANES), 1) < LANES // 2

    @pl.loop(0, chunks)
    def _(q):
        at = pl.ds(pl.multiple_of(q * CHUNK, CHUNK), CHUNK)
        cc = cconv[at, :]
        gram = lax.dot_general(
            cc, bconv[at, :], (((1,), (1,)), ((), ())), preferred_element_type=f32
        )
        gram = jnp.where(row >= col, gram, 0.0).astype(bf16)
        grow_row = growth[pl.ds(q, 1), :]
        for g in range(pairs // 2):
            wider = slice(g * QUAD, (g + 1) * QUAD)
            carried = jnp.dot(cc, prefix[q, :, wider], preferred_element_type=f32)
            for part in range(2):
                j = 2 * g + part
                lanes = slice(j * LANES, (j + 1) * LANES)
                values = xc[at, lanes]
                weights, cums = [], []
                for h in (2 * j, 2 * j + 1):
                    cum = jnp.broadcast_to(aux[q, :, h : h + 1], (CHUNK, CHUNK))
                    cums.append(cum)
                    grow = jnp.exp2(cum - turned[q, heads + h : heads + h + 1, :]).astype(bf16)
                    weights.append(gram * jnp.minimum(grow, jnp.asarray(BIG, bf16)))
                zero = jnp.zeros_like(values)
                both = jnp.concatenate(
                    [jnp.where(left, values, zero), jnp.where(left, zero, values)], axis=0
                )
                mixed = jnp.dot(jnp.concatenate(weights, axis=1), both, preferred_element_type=f32)
                decay = jnp.exp2(jnp.where(left, cums[0], cums[1]))
                y[at, lanes] = (
                    mixed + decay * carried[:, part * LANES : (part + 1) * LANES]
                    + gains[0:1, lanes] * values.astype(f32)
                )
                decays[at, lanes] = decay * grow_row[:, lanes]

        @pl.when(q == SCAN_AT)
        def _():
            scan_chips()

        @pl.when(q == SPLIT_AT)
        def _():
            split_cores()

    for m in range(half // 2):
        to_core(m).wait_send()
    others(lambda k: give(k).wait_send())
    others(lambda k: take(k).wait_send())
    last().wait()
    incoming[pl.ds((1 - core) * half, half)] = arrived[...]


SCAN_AT = 1
SPLIT_AT = 6


def output_kernel(y_ref, c_ref, decay_ref, inc_ref, out_hbm, held, store_sem):
    chunks = held.shape[0] // CHUNK

    def store(q):
        at = pl.ds(q * CHUNK, CHUNK)
        return pltpu.make_async_copy(held.at[at], out_hbm.at[at], store_sem.at[q])

    for q in range(chunks):
        at = slice(q * CHUNK, (q + 1) * CHUNK)
        cc = c_ref[at, :]
        for g in range(inc_ref.shape[0] // 2):
            wider = slice(g * QUAD, (g + 1) * QUAD)
            entering = jnp.concatenate([inc_ref[2 * g], inc_ref[2 * g + 1]], axis=1)
            carried = jnp.dot(cc, entering, preferred_element_type=jnp.float32)
            held[at, wider] = (y_ref[at, wider] + decay_ref[at, wider] * carried).astype(jnp.bfloat16)
        store(q).start()
    for q in range(chunks):
        store(q).wait()


def fused(inner_x, input_map, output_map, raw, kernel_x, kernel_b, kernel_c, rate, bias, gain):
    rows, inner = inner_x.shape
    wide = input_map.shape[1]
    heads = rate.shape[1]
    pairs = inner // LANES
    half = pairs // 2
    chunks = rows // CHUNK
    f32, bf16 = jnp.float32, jnp.bfloat16
    far = pl.BlockSpec(memory_space=pltpu.HBM)
    near = pl.BlockSpec(memory_space=pltpu.VMEM)
    tall = wide + DECAY_ROWS
    chips = FUSED_CHIPS
    dma = pltpu.SemaphoreType.DMA
    y, cconv, decays, incoming = pl.pallas_call(
        fused_kernel,
        in_specs=[far] * 10,
        out_specs=[near] * 4,
        out_shape=[
            pltpu.VMEM((rows, inner), f32), pltpu.VMEM((rows, wide), bf16),
            pltpu.VMEM((rows, inner), f32), pltpu.VMEM((pairs, wide, LANES), bf16),
        ],
        scratch_shapes=[
            pltpu.VMEM(raw.shape, f32), pltpu.VMEM(kernel_x.shape, f32),
            pltpu.VMEM(kernel_b.shape, f32), pltpu.VMEM(kernel_c.shape, f32),
            pltpu.VMEM(rate.shape, f32), pltpu.VMEM(bias.shape, f32), pltpu.VMEM(gain.shape, f32),
            pltpu.VMEM((PAD + rows, inner), bf16), pltpu.VMEM((PAD + rows, wide), bf16),
            pltpu.VMEM((PAD + rows, wide), bf16), pltpu.VMEM((rows, inner), bf16),
            pltpu.VMEM((rows, wide), bf16), pltpu.VMEM((chunks, CHUNK, LANES), f32),
            pltpu.VMEM((chunks, LANES, CHUNK), f32), pltpu.VMEM((2 * heads, inner), bf16),
            pltpu.VMEM((8, inner), f32), pltpu.VMEM((chunks, inner), f32),
            pltpu.VMEM((DECAY_ROWS, inner), bf16), pltpu.VMEM((rows, heads), bf16),
            pltpu.VMEM((chunks, inner), f32), pltpu.VMEM((wide, rows), bf16),
            pltpu.VMEM((chunks, wide, inner), bf16), pltpu.VMEM((2, rows + PAD, LANES), f32),
            pltpu.VMEM((2, rows + PAD, LANES), f32), pltpu.VMEM((rows, QUAD), bf16),
            pltpu.VMEM((rows, QUAD), bf16),
            pltpu.VMEM((pairs, tall, LANES), bf16), pltpu.VMEM((half, tall, LANES), bf16),
            pltpu.VMEM((chips, tall, LANES), bf16), pltpu.VMEM((chips, tall, LANES), bf16),
            pltpu.VMEM((chips, wide, LANES), bf16), pltpu.VMEM((chips, wide, LANES), bf16),
            pltpu.VMEM((half, wide, LANES), bf16), pltpu.VMEM((half, wide, LANES), bf16),
            dma((pairs // 2,)), dma((2,)), dma((7,)), dma((pairs // 2 + 2,)),
            dma((pairs // 2 + 2,)), dma((half // 2,)),
            dma((half // 2,)), dma((chips,)), dma((chips,)), dma((chips,)), dma((chips,)),
            dma((1,)), dma((1,)),
        ],
        compiler_params=pltpu.CompilerParams(
            vmem_limit_bytes=FUSED_VMEM, collective_id=0, has_side_effects=True
        ),
        name="fused_mixer",
    )(inner_x, input_map, output_map, raw, kernel_x, kernel_b, kernel_c, rate, bias, gain)
    return pl.pallas_call(
        output_kernel,
        in_specs=[near] * 4,
        out_specs=pl.BlockSpec(memory_space=pl.ANY),
        out_shape=jax.ShapeDtypeStruct((rows, inner), bf16),
        scratch_shapes=[pltpu.VMEM((rows, inner), bf16), dma((chunks,))],
        compiler_params=pltpu.CompilerParams(vmem_limit_bytes=OUTPUT_VMEM),
        name="output_rows",
    )(y, cconv, decays, incoming)


FUSED_VMEM = (47 << 20) + (160 << 10)
OUTPUT_VMEM = 16 << 20


def on_device(
    inner_x, input_map, output_map, step_raw, kernel_x, kernel_b, kernel_c, log_rate, step_bias,
    skip_gain,
):
    rows, inner = inner_x.shape
    heads = log_rate.shape[0]
    members = lax.axis_size("seq")
    if members == 2 * FUSED_CHIPS and inner == members * LANES and rows % ROWS == 0:
        return fused(
            inner_x, input_map, output_map, step_raw.T, kernel_x, kernel_b, kernel_c,
            log_rate[None, :], step_bias[None, :], skip_gain[None, :],
        )
    last = jnp.concatenate([a[rows - HALO :] for a in (inner_x, input_map, output_map)], axis=1)
    tail = lax.ppermute(last, "seq", [(i, i + 1) for i in range(members - 1)])
    xconv, bc, aux, prefix, run = local_states(
        inner_x, input_map, output_map, step_raw, tail, kernel_x, kernel_b, kernel_c,
        log_rate[None, :], step_bias[None, :],
    )
    gain = jnp.repeat(skip_gain, inner // heads)[None, :]
    half = rows // CHUNK // 2
    got = exchange(regroup(run, members))
    ya = local_mix(0, half, xconv, bc, aux, prefix, gain)
    got, ya = lax.optimization_barrier((got, ya))
    back = exchange(scan_members(got))
    yb = local_mix(half, half, xconv, bc, aux, prefix, gain)
    incoming = regroup(back, inner // LANES)
    return finish(heads, ya, yb, bc, aux, incoming)


def solution(mesh):
    split = P(("groups", "seq"), None)
    return jax.shard_map(
        on_device, mesh=mesh, in_specs=(split,) * 4 + (P(),) * 6, out_specs=split, check_vma=False
    )
```

```python
import functools

import jax
import jax.numpy as jnp
from jax import lax
from jax.experimental import pallas as pl
from jax.experimental.pallas import tpu as pltpu
from jax.sharding import PartitionSpec as P

CHUNK = 128
ROWS = 256
LANES = 128
LOG2E = 1.4426950408889634
HALO = 8
VMEM_LIMIT = 60 << 20
DECAY_ROWS = 16


def split_low(value):
    high = value.astype(jnp.bfloat16)
    return high, (value - high.astype(jnp.float32)).astype(jnp.bfloat16)


def silu(value):
    half = 0.5 * value
    return half + half * jnp.tanh(half)


def expander(heads, width, parts):
    shape = (parts * heads, heads * width)
    row = lax.broadcasted_iota(jnp.int32, shape, 0) % heads
    col = lax.broadcasted_iota(jnp.int32, shape, 1) // width
    return (row == col).astype(jnp.bfloat16)


def state_kernel(
    heads, x_ref, b_ref, c_ref, raw_ref, tail_ref, kx_ref, kb_ref, kc_ref, rate_ref, bias_ref,
    xconv_ref, bc_ref, aux_ref, prefix_ref, run_ref,
    xwin, bwin, cwin, spread, scaled, expand, state, logrun,
):
    step = pl.program_id(0)
    inner = x_ref.shape[1]
    wide = b_ref.shape[1]
    pairs = inner // LANES

    @pl.when(step == 0)
    def _():
        tail = tail_ref[...].astype(jnp.float32)
        xwin[0:HALO, :] = tail[:, :inner]
        bwin[0:HALO, :] = tail[:, inner : inner + wide]
        cwin[0:HALO, :] = tail[:, inner + wide :]
        expand[...] = expander(heads, inner // heads, 2)
        state[...] = jnp.zeros_like(state)
        logrun[...] = jnp.zeros_like(logrun)

    @pl.when(step > 0)
    def _():
        xwin[0:HALO, :] = xwin[ROWS : ROWS + HALO, :]
        bwin[0:HALO, :] = bwin[ROWS : ROWS + HALO, :]
        cwin[0:HALO, :] = cwin[ROWS : ROWS + HALO, :]

    bwin[HALO:, :] = b_ref[...].astype(jnp.float32)
    cwin[HALO:, :] = c_ref[...].astype(jnp.float32)

    def small_conv(win, taps):
        count = taps.shape[0]
        total = jnp.zeros((ROWS, win.shape[1]), jnp.float32)
        for k in range(count):
            at = HALO - (count - 1) + k
            total = total + taps[k : k + 1, :] * win[at : at + ROWS, :]
        return silu(total).astype(jnp.bfloat16)

    bconv = small_conv(bwin, kb_ref)
    cconv = small_conv(cwin, kc_ref)
    bc_ref[:, :wide] = bconv
    bc_ref[:, wide:] = cconv

    shifted = raw_ref[...] + bias_ref[...]
    dt = jnp.maximum(shifted, 0.0) + jnp.log1p(jnp.exp(-jnp.abs(shifted)))
    logdec = -(jnp.exp(rate_ref[...]) * LOG2E) * dt
    part0, rest = logdec.astype(jnp.bfloat16), None
    rest = logdec - part0.astype(jnp.float32)
    part1 = rest.astype(jnp.bfloat16)
    part2 = (rest - part1.astype(jnp.float32)).astype(jnp.bfloat16)
    row = lax.broadcasted_iota(jnp.int32, (CHUNK, CHUNK), 0)
    col = lax.broadcasted_iota(jnp.int32, (CHUNK, CHUNK), 1)
    lower = (row >= col).astype(jnp.bfloat16)
    parts = jnp.concatenate([part0, part1, part2, jnp.zeros_like(part0)], axis=1)
    logdt = jnp.log(dt) * LOG2E
    totals = []
    for q in range(ROWS // CHUNK):
        span = slice(q * CHUNK, (q + 1) * CHUNK)
        sums = jnp.dot(lower, parts[span], preferred_element_type=jnp.float32)
        cum = sums[:, :heads] + sums[:, heads : 2 * heads] + sums[:, 2 * heads : 3 * heads]
        total = cum[CHUNK - 1 :, :]
        totals.append(total)
        shift = cum - logdt[span]
        run = logrun[...] + cum
        logrun[...] = logrun[...] + total
        aux_ref[span, :] = jnp.concatenate([cum, shift, run, jnp.zeros_like(run)], axis=1)
        high, low = split_low(jnp.exp2(total - shift))
        spread[span, :] = jnp.dot(
            jnp.concatenate([high, low], axis=1), expand[...], preferred_element_type=jnp.float32
        )

    @pl.loop(0, pairs)
    def _(j):
        lanes = pl.ds(pl.multiple_of(j * LANES, LANES), LANES)
        xwin[HALO:, lanes] = x_ref[:, lanes].astype(jnp.float32)
        count = kx_ref.shape[0]
        total = jnp.zeros((ROWS, LANES), jnp.float32)
        for k in range(count):
            at = HALO - (count - 1) + k
            total = total + kx_ref[k : k + 1, lanes] * xwin[at : at + ROWS, lanes]
        xc = silu(total).astype(jnp.bfloat16)
        xconv_ref[:, lanes] = xc
        scaled[:, lanes] = (xc.astype(jnp.float32) * spread[:, lanes]).astype(jnp.bfloat16)

    btrans = bconv.astype(jnp.float32).T.astype(jnp.bfloat16)
    for q in range(ROWS // CHUNK):
        span = slice(q * CHUNK, (q + 1) * CHUNK)
        prefix_ref[q] = state[...].astype(jnp.bfloat16)
        factor = jnp.broadcast_to(jnp.exp2(totals[q]), (8, heads))
        high, low = split_low(factor)
        decay = jnp.dot(
            jnp.concatenate([high, low], axis=1), expand[...], preferred_element_type=jnp.float32
        )[0:1, :]
        state[...] = decay * state[...] + jnp.dot(
            btrans[:, span], scaled[span, :], preferred_element_type=jnp.float32
        )

    @pl.when(step == pl.num_programs(0) - 1)
    def _():
        high, low = split_low(jnp.broadcast_to(jnp.exp2(logrun[...]), (8, heads)))
        zero = jnp.zeros_like(high)
        high = jnp.dot(jnp.concatenate([high, zero], axis=1), expand[...], preferred_element_type=jnp.float32)
        low = jnp.dot(jnp.concatenate([low, zero], axis=1), expand[...], preferred_element_type=jnp.float32)
        both = jnp.concatenate([high, low], axis=0).astype(jnp.bfloat16)
        for j in range(pairs):
            lanes = slice(j * LANES, (j + 1) * LANES)
            run_ref[j, 0 : state.shape[0], :] = state[:, lanes].astype(jnp.bfloat16)
            run_ref[j, state.shape[0] :, :] = both[:, lanes]


def local_states(x, b, c, raw, tail, kx, kb, kc, rate, bias):
    rows, inner = x.shape
    wide = b.shape[1]
    heads = raw.shape[1]
    pairs = inner // LANES
    whole = lambda a: pl.BlockSpec(a.shape, lambda i: (0,) * a.ndim)
    block = lambda w: pl.BlockSpec((ROWS, w), lambda i: (i, 0))
    per = ROWS // CHUNK
    f32, bf16 = jnp.float32, jnp.bfloat16
    return pl.pallas_call(
        functools.partial(state_kernel, heads),
        grid=(rows // ROWS,),
        in_specs=[block(inner), block(wide), block(wide), block(heads), whole(tail), whole(kx),
                  whole(kb), whole(kc), whole(rate), whole(bias)],
        out_specs=[
            block(inner), block(2 * wide), block(LANES),
            pl.BlockSpec((per, wide, inner), lambda i: (i, 0, 0)),
            pl.BlockSpec((pairs, wide + DECAY_ROWS, LANES), lambda i: (0, 0, 0)),
        ],
        out_shape=[
            jax.ShapeDtypeStruct((rows, inner), bf16),
            jax.ShapeDtypeStruct((rows, 2 * wide), bf16),
            jax.ShapeDtypeStruct((rows, LANES), f32),
            jax.ShapeDtypeStruct((rows // CHUNK, wide, inner), bf16),
            jax.ShapeDtypeStruct((pairs, wide + DECAY_ROWS, LANES), bf16),
        ],
        scratch_shapes=[
            pltpu.VMEM((ROWS + HALO, inner), f32), pltpu.VMEM((ROWS + HALO, wide), f32),
            pltpu.VMEM((ROWS + HALO, wide), f32), pltpu.VMEM((ROWS, inner), f32),
            pltpu.VMEM((ROWS, inner), bf16), pltpu.VMEM((2 * heads, inner), bf16),
            pltpu.VMEM((wide, inner), f32), pltpu.VMEM((1, heads), f32),
        ],
        compiler_params=pltpu.CompilerParams(vmem_limit_bytes=VMEM_LIMIT),
        cost_estimate=pl.CostEstimate(flops=2 * 10**9, bytes_accessed=12 << 20, transcendentals=1 << 21),
        name="local_states",
    )(x, b, c, raw, tail, kx, kb, kc, rate, bias)


def inner_kernel(heads, xconv_ref, bc_ref, aux_ref, prefix_ref, gain_ref, y_ref):
    wide = bc_ref.shape[1] // 2
    pairs = xconv_ref.shape[1] // LANES
    aux = aux_ref[...]
    turned = aux.T
    bconv, cconv = bc_ref[:, :wide], bc_ref[:, wide:]
    row = lax.broadcasted_iota(jnp.int32, (CHUNK, CHUNK), 0)
    col = lax.broadcasted_iota(jnp.int32, (CHUNK, CHUNK), 1)
    gram = lax.dot_general(cconv, bconv, (((1,), (1,)), ((), ())), preferred_element_type=jnp.float32)
    gram = jnp.where(row >= col, gram, 0.0)
    left = lax.broadcasted_iota(jnp.int32, (CHUNK, LANES), 1) < LANES // 2
    for j in range(pairs):
        lanes = slice(j * LANES, (j + 1) * LANES)
        xc = xconv_ref[:, lanes]
        weights = []
        cums = []
        for h in (2 * j, 2 * j + 1):
            cum = jnp.broadcast_to(aux[:, h : h + 1], (CHUNK, CHUNK))
            cums.append(cum)
            power = jnp.minimum(cum - turned[heads + h : heads + h + 1, :], 126.0)
            weights.append((gram * jnp.exp2(power)).astype(jnp.bfloat16))
        zero = jnp.zeros_like(xc)
        both = jnp.concatenate([jnp.where(left, xc, zero), jnp.where(left, zero, xc)], axis=0)
        inner = jnp.dot(jnp.concatenate(weights, axis=1), both, preferred_element_type=jnp.float32)
        carried = jnp.dot(cconv, prefix_ref[0, :, lanes], preferred_element_type=jnp.float32)
        decay = jnp.exp2(jnp.where(left, cums[0], cums[1]))
        y_ref[:, lanes] = inner + decay * carried + gain_ref[:, lanes] * xc.astype(jnp.float32)


def local_mix(first, count, xconv, bc, aux, prefix, gain):
    inner = xconv.shape[1]
    heads = gain.shape[1] // 64
    wide = bc.shape[1] // 2
    block = lambda w: pl.BlockSpec((CHUNK, w), lambda i: (i + first, 0))
    return pl.pallas_call(
        functools.partial(inner_kernel, heads),
        grid=(count,),
        in_specs=[block(inner), block(2 * wide), block(LANES),
                  pl.BlockSpec((1, wide, inner), lambda i: (i + first, 0, 0)),
                  pl.BlockSpec((1, inner), lambda i: (0, 0))],
        out_specs=pl.BlockSpec((CHUNK, inner), lambda i: (i, 0)),
        out_shape=jax.ShapeDtypeStruct((count * CHUNK, inner), jnp.float32),
        compiler_params=pltpu.CompilerParams(vmem_limit_bytes=VMEM_LIMIT),
        cost_estimate=pl.CostEstimate(flops=10**10, bytes_accessed=24 << 20, transcendentals=1 << 22),
        name="local_mix",
    )(xconv, bc, aux, prefix, gain)


def scan_kernel(got_ref, out_ref):
    members, rows, width = out_ref.shape
    entering = jnp.zeros((rows, width), jnp.float32)
    for k in range(members):
        out_ref[k] = entering.astype(jnp.bfloat16)
        decay = got_ref[k, rows : rows + 1, :].astype(jnp.float32) + got_ref[
            k, rows + 8 : rows + 9, :
        ].astype(jnp.float32)
        entering = decay * entering + got_ref[k, 0:rows, :].astype(jnp.float32)


def scan_members(got):
    members, rows, width = got.shape
    return pl.pallas_call(
        scan_kernel,
        out_shape=jax.ShapeDtypeStruct((members, rows - DECAY_ROWS, width), jnp.bfloat16),
        compiler_params=pltpu.CompilerParams(vmem_limit_bytes=VMEM_LIMIT),
        name="scan_members",
    )(got)


def finish_kernel(heads, ya_ref, yb_ref, bc_ref, aux_ref, inc_ref, out_ref, expand):
    wide = bc_ref.shape[1] // 2
    pairs = out_ref.shape[1] // LANES

    @pl.when(pl.program_id(0) == 0)
    def _():
        expand[...] = expander(heads, out_ref.shape[1] // heads, 2)

    high, low = split_low(jnp.exp2(aux_ref[:, 2 * heads : 3 * heads]))
    factors = jnp.concatenate([high, low], axis=1)
    cconv = bc_ref[:, wide:]
    early = pl.program_id(0) < pl.num_programs(0) // 2

    def emit(y_ref):
        for j in range(pairs):
            lanes = slice(j * LANES, (j + 1) * LANES)
            decay = jnp.dot(factors, expand[:, lanes], preferred_element_type=jnp.float32)
            carried = jnp.dot(cconv, inc_ref[j], preferred_element_type=jnp.float32)
            out_ref[:, lanes] = (y_ref[:, lanes] + decay * carried).astype(jnp.bfloat16)

    @pl.when(early)
    def _():
        emit(ya_ref)

    @pl.when(jnp.logical_not(early))
    def _():
        emit(yb_ref)


def finish(heads, ya, yb, bc, aux, inc):
    rows, inner = bc.shape[0], ya.shape[1]
    wide = bc.shape[1] // 2
    steps = rows // CHUNK
    half = steps // 2
    block = lambda w: pl.BlockSpec((CHUNK, w), lambda i: (i, 0))
    return pl.pallas_call(
        functools.partial(finish_kernel, heads),
        grid=(steps,),
        in_specs=[
            pl.BlockSpec((CHUNK, inner), lambda i: (jnp.minimum(i, half - 1), 0)),
            pl.BlockSpec((CHUNK, inner), lambda i: (jnp.maximum(i - half, 0), 0)),
            block(2 * wide), block(LANES), pl.BlockSpec(inc.shape, lambda i: (0, 0, 0)),
        ],
        out_specs=block(inner),
        out_shape=jax.ShapeDtypeStruct((rows, inner), jnp.bfloat16),
        scratch_shapes=[pltpu.VMEM((2 * heads, inner), jnp.bfloat16)],
        compiler_params=pltpu.CompilerParams(vmem_limit_bytes=VMEM_LIMIT),
        name="finish",
    )(ya, yb, bc, aux, inc)


def exchange(x):
    return lax.all_to_all(x, "seq", split_axis=0, concat_axis=0, tiled=True)


def regroup(x, count):
    groups, rows, width = x.shape
    if groups == count:
        return x
    flat = x.transpose(1, 0, 2).reshape(rows, groups * width)
    return flat.reshape(rows, count, groups * width // count).transpose(1, 0, 2)


FUSED_CHIPS = 8
PAD = 16
QUAD = 2 * LANES
BIG = 1e38


def fused_kernel(
    x_hbm, b_hbm, c_hbm, raw_hbm, kx_hbm, kb_hbm, kc_hbm, rate_hbm, bias_hbm, gain_hbm,
    y, cconv, decays, incoming,
    raw_ref, kx_ref, kb_ref, kc_ref, rate_ref, bias_ref, gain_ref,
    xbuf, bbuf, cbuf, xc, bconv, aux, turned, expand, gains, falls, ends, factors, growth, btrans, prefix, window_a, window_b,
    scaled_a, scaled_b,
    run, core_got, chip_sum, got, entered, back, core_out, arrived,
    load_sem, small_sem, param_sem, tail_send, tail_recv, core_send, core_recv,
    give_send, give_recv, take_send, take_recv, last_send, last_recv,
):
    f32, bf16 = jnp.float32, jnp.bfloat16
    members = 2 * FUSED_CHIPS
    me = lax.axis_index("seq")
    chip, core = me // 2, me % 2
    partner = chip * 2 + 1 - core
    first_core = core == 0
    rows, inner = xc.shape
    wide = bconv.shape[1]
    heads = rate_ref.shape[1]
    pairs = inner // LANES
    chunks = rows // CHUNK
    half = pairs // 2
    steps = pairs // 2

    after = lax.rem(me + 1, members)

    def place(i, at=None):
        who = me if at is None else at
        m = lax.rem(who // 4 + 1 + i // 2, half // 2)
        mine = i % 2
        owner = mine * (who % 2) + (1 - mine) * (1 - who % 2)
        return m, owner * (half // 2) + m

    def quad_lanes(i):
        return pl.ds(pl.multiple_of(place(i)[1] * QUAD, QUAD), QUAD)

    def load(i):
        lanes = quad_lanes(i)
        return pltpu.make_async_copy(
            x_hbm.at[:, lanes], xbuf.at[pl.ds(PAD, rows), lanes], load_sem.at[i]
        )

    small = [
        pltpu.make_async_copy(b_hbm, bbuf.at[pl.ds(PAD, rows)], small_sem.at[0]),
        pltpu.make_async_copy(c_hbm, cbuf.at[pl.ds(PAD, rows)], small_sem.at[1]),
    ]
    params = [
        pltpu.make_async_copy(src, dst, param_sem.at[i])
        for i, (src, dst) in enumerate((
            (rate_hbm, rate_ref), (bias_hbm, bias_ref), (gain_hbm, gain_ref), (raw_hbm, raw_ref),
            (kx_hbm, kx_ref), (kb_hbm, kb_ref), (kc_hbm, kc_ref),
        ))
    ]
    for copy in params + small[:1]:
        copy.start()
    for i in range(steps):
        load(i).start()
    small[1].start()

    barrier = pltpu.get_barrier_semaphore()
    for off in range(1, members):
        pl.semaphore_signal(
            barrier, inc=1, device_id={"seq": lax.rem(me + off, members)},
            device_id_type=pl.DeviceIdType.MESH,
        )

    def remote(src, dst, send, recv, to):
        return pltpu.make_async_remote_copy(
            src_ref=src, dst_ref=dst, send_sem=send, recv_sem=recv, device_id={"seq": to},
            device_id_type=pl.DeviceIdType.MESH,
        )

    def x_tail(i, at):
        lanes = pl.ds(pl.multiple_of(place(i, at)[1] * QUAD, QUAD), QUAD)
        return remote(
            x_hbm.at[pl.ds(rows - PAD, PAD), lanes], xbuf.at[pl.ds(0, PAD), lanes],
            tail_send.at[i], tail_recv.at[i], after,
        )

    small_tails = [
        remote(
            h.at[pl.ds(rows - PAD, PAD)], v.at[pl.ds(0, PAD)], tail_send.at[steps + k],
            tail_recv.at[steps + k], after,
        )
        for k, (h, v) in enumerate(((b_hbm, bbuf), (c_hbm, cbuf)))
    ]

    expand[...] = expander(heads, inner // heads, 2)
    pl.semaphore_wait(barrier, members - 1)

    @pl.when(me < members - 1)
    def _():
        small_tails[0].start()
        for i in range(steps):
            x_tail(i, after).start()
        small_tails[1].start()

    for copy in params:
        copy.wait()
    high, middle = split_low(jnp.broadcast_to(gain_ref[...], (8, heads)))
    low = (gain_ref[...] - high.astype(f32) - middle.astype(f32)).astype(bf16)
    gains[...] = jnp.dot(
        jnp.concatenate([high, middle], axis=1), expand[...], preferred_element_type=f32
    ) + jnp.dot(
        jnp.concatenate([low, jnp.zeros_like(low)], axis=1), expand[...], preferred_element_type=f32
    )
    row = lax.broadcasted_iota(jnp.int32, (CHUNK, CHUNK), 0)
    col = lax.broadcasted_iota(jnp.int32, (CHUNK, CHUNK), 1)
    turns = jnp.concatenate([rate_ref[...], bias_ref[...], rate_ref[...], bias_ref[...]], axis=1)
    turns = jnp.broadcast_to(turns, (CHUNK, CHUNK)).T
    speed = jnp.exp(turns[:heads]) * LOG2E
    bias = turns[heads : 2 * heads]
    upper = (row <= col).astype(bf16)
    chunk_falls, chunk_growth = [], []
    before = jnp.zeros((1, heads), f32)
    for q in range(chunks):
        span = slice(q * CHUNK, (q + 1) * CHUNK)
        shifted = raw_ref[:, span] + bias
        dt = jnp.maximum(shifted, 0.0) + jnp.log1p(jnp.exp(-jnp.abs(shifted)))
        logdec = -speed * dt
        part0 = logdec.astype(bf16)
        rest = logdec - part0.astype(f32)
        part1 = rest.astype(bf16)
        part2 = (rest - part1.astype(f32)).astype(bf16)
        sums = jnp.dot(
            jnp.concatenate([part0, part1, part2], axis=0), upper, preferred_element_type=f32
        )
        cum = sums[:heads] + sums[heads : 2 * heads] + sums[2 * heads :]
        total = jnp.broadcast_to(cum[:, CHUNK - 1 :], cum.shape)
        shift = cum - jnp.log(dt) * LOG2E
        flat = jnp.concatenate(
            [cum, shift, cum, jnp.exp2(total - shift)], axis=0
        )
        stood = flat.T
        turned[q] = flat
        aux[q] = stood
        factors[span, :] = stood[:, 3 * heads :].astype(bf16)
        chunk_growth.append(jnp.exp2(before))
        before = before + stood[CHUNK - 1 :, :heads]
        chunk_falls.append(jnp.exp2(stood[CHUNK - 1 :, :heads]))
    high, low = split_low(jnp.concatenate(chunk_falls, axis=0))
    falls[...] = jnp.dot(
        jnp.concatenate([high, low], axis=1), expand[...], preferred_element_type=f32
    )
    high, low = split_low(jnp.concatenate(chunk_growth, axis=0))
    growth[...] = jnp.dot(
        jnp.concatenate([high, low], axis=1), expand[...], preferred_element_type=f32
    )
    high, low = split_low(jnp.broadcast_to(jnp.exp2(before), (8, heads)))
    zero = jnp.zeros_like(high)
    high = jnp.dot(jnp.concatenate([high, zero], axis=1), expand[...], preferred_element_type=f32)
    low = jnp.dot(jnp.concatenate([low, zero], axis=1), expand[...], preferred_element_type=f32)
    ends[...] = jnp.concatenate([high, low], axis=0).astype(bf16)
    def fill(buf, slot, at, count, lanes):
        slot[at : at + count, :] = buf[at : at + count, lanes].astype(f32)

    def convolve(taps_ref, slot, q, lanes):
        taps = 0.5 * taps_ref[:, lanes]
        count = taps.shape[0]
        at = PAD - count + 1 + q * CHUNK
        total = taps[0:1] * slot[at : at + CHUNK, :]
        for k in range(1, count):
            total = total + taps[k : k + 1] * slot[at + k : at + k + CHUNK, :]
        return total + total * jnp.tanh(total)

    everything = slice(0, LANES)

    def small_chunk(q):
        span = slice(q * CHUNK, (q + 1) * CHUNK)
        bconv[span, :] = convolve(kb_ref, window_b.at[0], q, everything).astype(bf16)

    def part_lanes(i, part):
        return pl.ds(pl.multiple_of(place(i)[1] * QUAD + part * LANES, LANES), LANES)

    def fill_chunk(i, win, q):
        for part in range(2):
            fill(xbuf, win.at[part], PAD + q * CHUNK, CHUNK, part_lanes(i, part))

    def convolve_chunk(i, win, scaled, q):
        span = slice(q * CHUNK, (q + 1) * CHUNK)
        spread = jnp.dot(
            factors[span, :], expand[:heads, quad_lanes(i)], preferred_element_type=f32
        )
        for part in range(2):
            lanes = part_lanes(i, part)
            piece = slice(part * LANES, (part + 1) * LANES)
            done = convolve(kx_ref, win.at[part], q, lanes)
            xc[span, lanes] = done.astype(bf16)
            scaled[span, piece] = (done * spread[:, piece]).astype(bf16)

    small[0].wait()
    fill(bbuf, window_b.at[0], PAD, rows, everything)
    for q in range(1, chunks):
        small_chunk(q)
    load(0).wait()
    for q in range(chunks):
        fill_chunk(0, window_a, q)
    for q in range(1, chunks):
        convolve_chunk(0, window_a, scaled_a, q)

    def tail_here(copy):
        @pl.when(me > 0)
        def _():
            copy.wait_recv()

    tail_here(small_tails[0])
    tail_here(x_tail(0, me))

    @pl.when(me == 0)
    def _():
        xbuf[0:PAD, :] = jnp.zeros((PAD, inner), bf16)
        bbuf[0:PAD, :] = jnp.zeros((PAD, wide), bf16)
        cbuf[0:PAD, :] = jnp.zeros((PAD, wide), bf16)

    fill(bbuf, window_b.at[0], 0, PAD, everything)
    small_chunk(0)
    for part in range(2):
        fill(xbuf, window_a.at[part], 0, PAD, part_lanes(0, part))
    convolve_chunk(0, window_a, scaled_a, 0)
    for q in range(chunks):
        span = slice(q * CHUNK, (q + 1) * CHUNK)
        btrans[:, span] = bconv[span, :].astype(f32).T.astype(bf16)

    def state_chunk(i, scaled, q, held):
        span = slice(q * CHUNK, (q + 1) * CHUNK)
        lanes = quad_lanes(i)
        prefix[q, :, lanes] = held.astype(bf16)
        return falls[q : q + 1, lanes] * held + jnp.dot(
            btrans[:, span], scaled[span, :], preferred_element_type=f32
        )

    def state_and_next(i, scaled, following):
        held = jnp.zeros((wide, QUAD), f32)
        if following is not None:
            win, into = following
            for part in range(2):
                fill(xbuf, win.at[part], 0, PAD, part_lanes(i + 1, part))
        for q in range(chunks):
            if following is not None:
                fill_chunk(i + 1, win, q)
                convolve_chunk(i + 1, win, into, q)
            held = state_chunk(i, scaled, q, held)
        held = held.astype(bf16)
        tip = ends[:, quad_lanes(i)]
        first = place(i)[1] * 2
        for part in range(2):
            piece = slice(part * LANES, (part + 1) * LANES)
            run[first + part, 0:wide, :] = held[:, piece]
            run[first + part, wide:, :] = tip[:, piece]

    def to_core(m):
        return remote(
            run.at[pl.ds((1 - core) * half + 2 * m, 2)], core_got.at[pl.ds(2 * m, 2)],
            core_send.at[m], core_recv.at[m], partner,
        )

    def give(other):
        return remote(
            chip_sum.at[other], got.at[chip], give_send.at[other], give_recv.at[chip],
            other * 2 + core,
        )

    def given(other):
        return remote(
            chip_sum.at[other], got.at[other], give_send.at[other], give_recv.at[other],
            other * 2 + core,
        )

    def take(other):
        return remote(
            entered.at[other], back.at[chip], take_send.at[other], take_recv.at[chip],
            other * 2 + core,
        )

    def taken(other):
        return remote(
            entered.at[other], back.at[other], take_send.at[other], take_recv.at[other],
            other * 2 + core,
        )

    def last(part):
        span = pl.ds(part * (half // 2), half // 2)
        return remote(
            core_out.at[span], arrived.at[span], last_send.at[part], last_recv.at[part], partner,
        )

    def decay_of(piece):
        return piece[wide : wide + 1].astype(f32) + piece[wide + 8 : wide + 9].astype(f32)

    def add_cores(m):
        to_core(m).wait_recv()
        for part in range(2):
            j = 2 * m + part
            mine, other = run[core * half + j], core_got[j]
            lead = jnp.where(first_core, mine.astype(f32), other.astype(f32))
            trail = jnp.where(first_core, other.astype(f32), mine.astype(f32))
            fall = trail[wide : wide + 1] + trail[wide + 8 : wide + 9]
            whole = (lead[wide : wide + 1] + lead[wide + 8 : wide + 9]) * fall
            high, low = split_low(jnp.broadcast_to(whole, (8, LANES)))
            chip_sum[j, 0:wide, :] = (fall * lead[:wide] + trail[:wide]).astype(bf16)
            chip_sum[j, wide:, :] = jnp.concatenate(
                [high.astype(f32), low.astype(f32)], axis=0
            ).astype(bf16)

            @pl.when(j != chip)
            def _():
                give(j).start()

            @pl.when(j == chip)
            def _():
                got[chip] = chip_sum[chip]

    def others(act):
        for off in range(1, FUSED_CHIPS):
            act(lax.rem(chip + off, FUSED_CHIPS))

    def scan_chips():
        others(lambda k: given(k).wait_recv())
        value = jnp.zeros((wide, LANES), f32)
        for k in range(FUSED_CHIPS):
            entered[k] = value.astype(bf16)
            if k < FUSED_CHIPS - 1:
                piece = got[k]
                value = decay_of(piece) * value + piece[:wide].astype(f32)
        others(lambda k: take(k).start())
        back[chip] = entered[chip]

    def split_cores():
        others(lambda k: taken(k).wait_recv())
        for j in range(half):
            lead = jnp.where(
                first_core, run[core * half + j].astype(f32), core_got[j].astype(f32)
            )
            entering = back[j].astype(f32)
            fall = lead[wide : wide + 1] + lead[wide + 8 : wide + 9]
            later = fall * entering + lead[:wide]
            core_out[j] = jnp.where(first_core, later, entering).astype(bf16)
            incoming[core * half + j] = jnp.where(first_core, entering, later).astype(bf16)
            if j % (half // 2) == half // 2 - 1:
                last(j // (half // 2)).start()

    @pl.loop(0, steps // 2)
    def _(k):
        i = 2 * k
        load(i + 1).wait()
        tail_here(x_tail(i + 1, me))
        state_and_next(i, scaled_a, (window_b, scaled_b))
        to_core(place(i)[0]).start()

        @pl.when(k < steps // 2 - 1)
        def _():
            load(i + 2).wait()
            tail_here(x_tail(i + 2, me))
            state_and_next(i + 1, scaled_b, (window_a, scaled_a))

        @pl.when(k == steps // 2 - 1)
        def _():
            state_and_next(i + 1, scaled_b, None)

        add_cores(place(i + 1)[0])

    @pl.when(me < members - 1)
    def _():
        for i in range(steps):
            x_tail(i, after).wait_send()
        for copy in small_tails:
            copy.wait_send()

    small[1].wait()
    tail_here(small_tails[1])
    fill(cbuf, window_b.at[1], 0, PAD + rows, everything)
    for q in range(chunks):
        span = slice(q * CHUNK, (q + 1) * CHUNK)
        cconv[span, :] = convolve(kc_ref, window_b.at[1], q, everything).astype(bf16)
    left = lax.broadcasted_iota(jnp.int32, (CHUNK, LANES), 1) < LANES // 2

    @pl.loop(0, chunks)
    def _(q):
        at = pl.ds(pl.multiple_of(q * CHUNK, CHUNK), CHUNK)
        cc = cconv[at, :]
        gram = lax.dot_general(
            cc, bconv[at, :], (((1,), (1,)), ((), ())), preferred_element_type=f32
        )
        gram = jnp.where(row >= col, gram, 0.0).astype(bf16)
        grow_row = growth[pl.ds(q, 1), :]
        for g in range(pairs // 2):
            wider = slice(g * QUAD, (g + 1) * QUAD)
            carried = jnp.dot(cc, prefix[q, :, wider], preferred_element_type=f32)
            for part in range(2):
                j = 2 * g + part
                lanes = slice(j * LANES, (j + 1) * LANES)
                values = xc[at, lanes]
                weights, cums = [], []
                for h in (2 * j, 2 * j + 1):
                    cum = jnp.broadcast_to(aux[q, :, h : h + 1], (CHUNK, CHUNK))
                    cums.append(cum)
                    grow = jnp.exp2(cum - turned[q, heads + h : heads + h + 1, :]).astype(bf16)
                    weights.append(gram * jnp.minimum(grow, jnp.asarray(BIG, bf16)))
                zero = jnp.zeros_like(values)
                both = jnp.concatenate(
                    [jnp.where(left, values, zero), jnp.where(left, zero, values)], axis=0
                )
                mixed = jnp.dot(jnp.concatenate(weights, axis=1), both, preferred_element_type=f32)
                decay = jnp.exp2(jnp.where(left, cums[0], cums[1]))
                y[at, lanes] = (
                    mixed + decay * carried[:, part * LANES : (part + 1) * LANES]
                    + gains[0:1, lanes] * values.astype(f32)
                )
                decays[at, lanes] = decay * grow_row[:, lanes]

        @pl.when(q == SCAN_AT)
        def _():
            scan_chips()

        @pl.when(q == SPLIT_AT)
        def _():
            split_cores()

    for m in range(half // 2):
        to_core(m).wait_send()
    others(lambda k: give(k).wait_send())
    others(lambda k: take(k).wait_send())
    for part in range(2):
        last(part).wait()
        span = pl.ds(part * (half // 2), half // 2)
        incoming[pl.ds((1 - core) * half + part * (half // 2), half // 2)] = arrived[span]


SCAN_AT = 1
SPLIT_AT = 6


def output_kernel(y_ref, c_ref, decay_ref, inc_ref, out_hbm, held, store_sem):
    chunks = held.shape[0] // CHUNK

    def store(q):
        at = pl.ds(q * CHUNK, CHUNK)
        return pltpu.make_async_copy(held.at[at], out_hbm.at[at], store_sem.at[q])

    for q in range(chunks):
        at = slice(q * CHUNK, (q + 1) * CHUNK)
        cc = c_ref[at, :]
        for g in range(inc_ref.shape[0] // 2):
            wider = slice(g * QUAD, (g + 1) * QUAD)
            entering = jnp.concatenate([inc_ref[2 * g], inc_ref[2 * g + 1]], axis=1)
            carried = jnp.dot(cc, entering, preferred_element_type=jnp.float32)
            held[at, wider] = (y_ref[at, wider] + decay_ref[at, wider] * carried).astype(jnp.bfloat16)
        store(q).start()
    for q in range(chunks):
        store(q).wait()


def fused(inner_x, input_map, output_map, raw, kernel_x, kernel_b, kernel_c, rate, bias, gain):
    rows, inner = inner_x.shape
    wide = input_map.shape[1]
    heads = rate.shape[1]
    pairs = inner // LANES
    half = pairs // 2
    chunks = rows // CHUNK
    f32, bf16 = jnp.float32, jnp.bfloat16
    far = pl.BlockSpec(memory_space=pltpu.HBM)
    near = pl.BlockSpec(memory_space=pltpu.VMEM)
    tall = wide + DECAY_ROWS
    chips = FUSED_CHIPS
    dma = pltpu.SemaphoreType.DMA
    y, cconv, decays, incoming = pl.pallas_call(
        fused_kernel,
        in_specs=[far] * 10,
        out_specs=[near] * 4,
        out_shape=[
            pltpu.VMEM((rows, inner), f32), pltpu.VMEM((rows, wide), bf16),
            pltpu.VMEM((rows, inner), f32), pltpu.VMEM((pairs, wide, LANES), bf16),
        ],
        scratch_shapes=[
            pltpu.VMEM(raw.shape, f32), pltpu.VMEM(kernel_x.shape, f32),
            pltpu.VMEM(kernel_b.shape, f32), pltpu.VMEM(kernel_c.shape, f32),
            pltpu.VMEM(rate.shape, f32), pltpu.VMEM(bias.shape, f32), pltpu.VMEM(gain.shape, f32),
            pltpu.VMEM((PAD + rows, inner), bf16), pltpu.VMEM((PAD + rows, wide), bf16),
            pltpu.VMEM((PAD + rows, wide), bf16), pltpu.VMEM((rows, inner), bf16),
            pltpu.VMEM((rows, wide), bf16), pltpu.VMEM((chunks, CHUNK, LANES), f32),
            pltpu.VMEM((chunks, LANES, CHUNK), f32), pltpu.VMEM((2 * heads, inner), bf16),
            pltpu.VMEM((8, inner), f32), pltpu.VMEM((chunks, inner), f32),
            pltpu.VMEM((DECAY_ROWS, inner), bf16), pltpu.VMEM((rows, heads), bf16),
            pltpu.VMEM((chunks, inner), f32), pltpu.VMEM((wide, rows), bf16),
            pltpu.VMEM((chunks, wide, inner), bf16), pltpu.VMEM((2, rows + PAD, LANES), f32),
            pltpu.VMEM((2, rows + PAD, LANES), f32), pltpu.VMEM((rows, QUAD), bf16),
            pltpu.VMEM((rows, QUAD), bf16),
            pltpu.VMEM((pairs, tall, LANES), bf16), pltpu.VMEM((half, tall, LANES), bf16),
            pltpu.VMEM((chips, tall, LANES), bf16), pltpu.VMEM((chips, tall, LANES), bf16),
            pltpu.VMEM((chips, wide, LANES), bf16), pltpu.VMEM((chips, wide, LANES), bf16),
            pltpu.VMEM((half, wide, LANES), bf16), pltpu.VMEM((half, wide, LANES), bf16),
            dma((pairs // 2,)), dma((2,)), dma((7,)), dma((pairs // 2 + 2,)),
            dma((pairs // 2 + 2,)), dma((half // 2,)),
            dma((half // 2,)), dma((chips,)), dma((chips,)), dma((chips,)), dma((chips,)),
            dma((2,)), dma((2,)),
        ],
        compiler_params=pltpu.CompilerParams(
            vmem_limit_bytes=FUSED_VMEM, collective_id=0, has_side_effects=True
        ),
        name="fused_mixer",
    )(inner_x, input_map, output_map, raw, kernel_x, kernel_b, kernel_c, rate, bias, gain)
    return pl.pallas_call(
        output_kernel,
        in_specs=[near] * 4,
        out_specs=pl.BlockSpec(memory_space=pl.ANY),
        out_shape=jax.ShapeDtypeStruct((rows, inner), bf16),
        scratch_shapes=[pltpu.VMEM((rows, inner), bf16), dma((chunks,))],
        compiler_params=pltpu.CompilerParams(vmem_limit_bytes=OUTPUT_VMEM),
        name="output_rows",
    )(y, cconv, decays, incoming)


FUSED_VMEM = (47 << 20) + (160 << 10)
OUTPUT_VMEM = 16 << 20


def on_device(
    inner_x, input_map, output_map, step_raw, kernel_x, kernel_b, kernel_c, log_rate, step_bias,
    skip_gain,
):
    rows, inner = inner_x.shape
    heads = log_rate.shape[0]
    members = lax.axis_size("seq")
    if members == 2 * FUSED_CHIPS and inner == members * LANES and rows % ROWS == 0:
        return fused(
            inner_x, input_map, output_map, step_raw.T, kernel_x, kernel_b, kernel_c,
            log_rate[None, :], step_bias[None, :], skip_gain[None, :],
        )
    last = jnp.concatenate([a[rows - HALO :] for a in (inner_x, input_map, output_map)], axis=1)
    tail = lax.ppermute(last, "seq", [(i, i + 1) for i in range(members - 1)])
    xconv, bc, aux, prefix, run = local_states(
        inner_x, input_map, output_map, step_raw, tail, kernel_x, kernel_b, kernel_c,
        log_rate[None, :], step_bias[None, :],
    )
    gain = jnp.repeat(skip_gain, inner // heads)[None, :]
    half = rows // CHUNK // 2
    got = exchange(regroup(run, members))
    ya = local_mix(0, half, xconv, bc, aux, prefix, gain)
    got, ya = lax.optimization_barrier((got, ya))
    back = exchange(scan_members(got))
    yb = local_mix(half, half, xconv, bc, aux, prefix, gain)
    incoming = regroup(back, inner // LANES)
    return finish(heads, ya, yb, bc, aux, incoming)


def solution(mesh):
    split = P(("groups", "seq"), None)
    return jax.shard_map(
        on_device, mesh=mesh, in_specs=(split,) * 4 + (P(),) * 6, out_specs=split, check_vma=False
    )
```

```python
import functools

import jax
import jax.numpy as jnp
from jax import lax
from jax.experimental import pallas as pl
from jax.experimental.pallas import tpu as pltpu
from jax.sharding import PartitionSpec as P

CHUNK = 128
ROWS = 256
LANES = 128
LOG2E = 1.4426950408889634
HALO = 8
VMEM_LIMIT = 60 << 20
DECAY_ROWS = 16


def split_low(value):
    high = value.astype(jnp.bfloat16)
    return high, (value - high.astype(jnp.float32)).astype(jnp.bfloat16)


def silu(value):
    half = 0.5 * value
    return half + half * jnp.tanh(half)


def expander(heads, width, parts):
    shape = (parts * heads, heads * width)
    row = lax.broadcasted_iota(jnp.int32, shape, 0) % heads
    col = lax.broadcasted_iota(jnp.int32, shape, 1) // width
    return (row == col).astype(jnp.bfloat16)


def state_kernel(
    heads, x_ref, b_ref, c_ref, raw_ref, tail_ref, kx_ref, kb_ref, kc_ref, rate_ref, bias_ref,
    xconv_ref, bc_ref, aux_ref, prefix_ref, run_ref,
    xwin, bwin, cwin, spread, scaled, expand, state, logrun,
):
    step = pl.program_id(0)
    inner = x_ref.shape[1]
    wide = b_ref.shape[1]
    pairs = inner // LANES

    @pl.when(step == 0)
    def _():
        tail = tail_ref[...].astype(jnp.float32)
        xwin[0:HALO, :] = tail[:, :inner]
        bwin[0:HALO, :] = tail[:, inner : inner + wide]
        cwin[0:HALO, :] = tail[:, inner + wide :]
        expand[...] = expander(heads, inner // heads, 2)
        state[...] = jnp.zeros_like(state)
        logrun[...] = jnp.zeros_like(logrun)

    @pl.when(step > 0)
    def _():
        xwin[0:HALO, :] = xwin[ROWS : ROWS + HALO, :]
        bwin[0:HALO, :] = bwin[ROWS : ROWS + HALO, :]
        cwin[0:HALO, :] = cwin[ROWS : ROWS + HALO, :]

    bwin[HALO:, :] = b_ref[...].astype(jnp.float32)
    cwin[HALO:, :] = c_ref[...].astype(jnp.float32)

    def small_conv(win, taps):
        count = taps.shape[0]
        total = jnp.zeros((ROWS, win.shape[1]), jnp.float32)
        for k in range(count):
            at = HALO - (count - 1) + k
            total = total + taps[k : k + 1, :] * win[at : at + ROWS, :]
        return silu(total).astype(jnp.bfloat16)

    bconv = small_conv(bwin, kb_ref)
    cconv = small_conv(cwin, kc_ref)
    bc_ref[:, :wide] = bconv
    bc_ref[:, wide:] = cconv

    shifted = raw_ref[...] + bias_ref[...]
    dt = jnp.maximum(shifted, 0.0) + jnp.log1p(jnp.exp(-jnp.abs(shifted)))
    logdec = -(jnp.exp(rate_ref[...]) * LOG2E) * dt
    part0, rest = logdec.astype(jnp.bfloat16), None
    rest = logdec - part0.astype(jnp.float32)
    part1 = rest.astype(jnp.bfloat16)
    part2 = (rest - part1.astype(jnp.float32)).astype(jnp.bfloat16)
    row = lax.broadcasted_iota(jnp.int32, (CHUNK, CHUNK), 0)
    col = lax.broadcasted_iota(jnp.int32, (CHUNK, CHUNK), 1)
    lower = (row >= col).astype(jnp.bfloat16)
    parts = jnp.concatenate([part0, part1, part2, jnp.zeros_like(part0)], axis=1)
    logdt = jnp.log(dt) * LOG2E
    totals = []
    for q in range(ROWS // CHUNK):
        span = slice(q * CHUNK, (q + 1) * CHUNK)
        sums = jnp.dot(lower, parts[span], preferred_element_type=jnp.float32)
        cum = sums[:, :heads] + sums[:, heads : 2 * heads] + sums[:, 2 * heads : 3 * heads]
        total = cum[CHUNK - 1 :, :]
        totals.append(total)
        shift = cum - logdt[span]
        run = logrun[...] + cum
        logrun[...] = logrun[...] + total
        aux_ref[span, :] = jnp.concatenate([cum, shift, run, jnp.zeros_like(run)], axis=1)
        high, low = split_low(jnp.exp2(total - shift))
        spread[span, :] = jnp.dot(
            jnp.concatenate([high, low], axis=1), expand[...], preferred_element_type=jnp.float32
        )

    @pl.loop(0, pairs)
    def _(j):
        lanes = pl.ds(pl.multiple_of(j * LANES, LANES), LANES)
        xwin[HALO:, lanes] = x_ref[:, lanes].astype(jnp.float32)
        count = kx_ref.shape[0]
        total = jnp.zeros((ROWS, LANES), jnp.float32)
        for k in range(count):
            at = HALO - (count - 1) + k
            total = total + kx_ref[k : k + 1, lanes] * xwin[at : at + ROWS, lanes]
        xc = silu(total).astype(jnp.bfloat16)
        xconv_ref[:, lanes] = xc
        scaled[:, lanes] = (xc.astype(jnp.float32) * spread[:, lanes]).astype(jnp.bfloat16)

    btrans = bconv.astype(jnp.float32).T.astype(jnp.bfloat16)
    for q in range(ROWS // CHUNK):
        span = slice(q * CHUNK, (q + 1) * CHUNK)
        prefix_ref[q] = state[...].astype(jnp.bfloat16)
        factor = jnp.broadcast_to(jnp.exp2(totals[q]), (8, heads))
        high, low = split_low(factor)
        decay = jnp.dot(
            jnp.concatenate([high, low], axis=1), expand[...], preferred_element_type=jnp.float32
        )[0:1, :]
        state[...] = decay * state[...] + jnp.dot(
            btrans[:, span], scaled[span, :], preferred_element_type=jnp.float32
        )

    @pl.when(step == pl.num_programs(0) - 1)
    def _():
        high, low = split_low(jnp.broadcast_to(jnp.exp2(logrun[...]), (8, heads)))
        zero = jnp.zeros_like(high)
        high = jnp.dot(jnp.concatenate([high, zero], axis=1), expand[...], preferred_element_type=jnp.float32)
        low = jnp.dot(jnp.concatenate([low, zero], axis=1), expand[...], preferred_element_type=jnp.float32)
        both = jnp.concatenate([high, low], axis=0).astype(jnp.bfloat16)
        for j in range(pairs):
            lanes = slice(j * LANES, (j + 1) * LANES)
            run_ref[j, 0 : state.shape[0], :] = state[:, lanes].astype(jnp.bfloat16)
            run_ref[j, state.shape[0] :, :] = both[:, lanes]


def local_states(x, b, c, raw, tail, kx, kb, kc, rate, bias):
    rows, inner = x.shape
    wide = b.shape[1]
    heads = raw.shape[1]
    pairs = inner // LANES
    whole = lambda a: pl.BlockSpec(a.shape, lambda i: (0,) * a.ndim)
    block = lambda w: pl.BlockSpec((ROWS, w), lambda i: (i, 0))
    per = ROWS // CHUNK
    f32, bf16 = jnp.float32, jnp.bfloat16
    return pl.pallas_call(
        functools.partial(state_kernel, heads),
        grid=(rows // ROWS,),
        in_specs=[block(inner), block(wide), block(wide), block(heads), whole(tail), whole(kx),
                  whole(kb), whole(kc), whole(rate), whole(bias)],
        out_specs=[
            block(inner), block(2 * wide), block(LANES),
            pl.BlockSpec((per, wide, inner), lambda i: (i, 0, 0)),
            pl.BlockSpec((pairs, wide + DECAY_ROWS, LANES), lambda i: (0, 0, 0)),
        ],
        out_shape=[
            jax.ShapeDtypeStruct((rows, inner), bf16),
            jax.ShapeDtypeStruct((rows, 2 * wide), bf16),
            jax.ShapeDtypeStruct((rows, LANES), f32),
            jax.ShapeDtypeStruct((rows // CHUNK, wide, inner), bf16),
            jax.ShapeDtypeStruct((pairs, wide + DECAY_ROWS, LANES), bf16),
        ],
        scratch_shapes=[
            pltpu.VMEM((ROWS + HALO, inner), f32), pltpu.VMEM((ROWS + HALO, wide), f32),
            pltpu.VMEM((ROWS + HALO, wide), f32), pltpu.VMEM((ROWS, inner), f32),
            pltpu.VMEM((ROWS, inner), bf16), pltpu.VMEM((2 * heads, inner), bf16),
            pltpu.VMEM((wide, inner), f32), pltpu.VMEM((1, heads), f32),
        ],
        compiler_params=pltpu.CompilerParams(vmem_limit_bytes=VMEM_LIMIT),
        cost_estimate=pl.CostEstimate(flops=2 * 10**9, bytes_accessed=12 << 20, transcendentals=1 << 21),
        name="local_states",
    )(x, b, c, raw, tail, kx, kb, kc, rate, bias)


def inner_kernel(heads, xconv_ref, bc_ref, aux_ref, prefix_ref, gain_ref, y_ref):
    wide = bc_ref.shape[1] // 2
    pairs = xconv_ref.shape[1] // LANES
    aux = aux_ref[...]
    turned = aux.T
    bconv, cconv = bc_ref[:, :wide], bc_ref[:, wide:]
    row = lax.broadcasted_iota(jnp.int32, (CHUNK, CHUNK), 0)
    col = lax.broadcasted_iota(jnp.int32, (CHUNK, CHUNK), 1)
    gram = lax.dot_general(cconv, bconv, (((1,), (1,)), ((), ())), preferred_element_type=jnp.float32)
    gram = jnp.where(row >= col, gram, 0.0)
    left = lax.broadcasted_iota(jnp.int32, (CHUNK, LANES), 1) < LANES // 2
    for j in range(pairs):
        lanes = slice(j * LANES, (j + 1) * LANES)
        xc = xconv_ref[:, lanes]
        weights = []
        cums = []
        for h in (2 * j, 2 * j + 1):
            cum = jnp.broadcast_to(aux[:, h : h + 1], (CHUNK, CHUNK))
            cums.append(cum)
            power = jnp.minimum(cum - turned[heads + h : heads + h + 1, :], 126.0)
            weights.append((gram * jnp.exp2(power)).astype(jnp.bfloat16))
        zero = jnp.zeros_like(xc)
        both = jnp.concatenate([jnp.where(left, xc, zero), jnp.where(left, zero, xc)], axis=0)
        inner = jnp.dot(jnp.concatenate(weights, axis=1), both, preferred_element_type=jnp.float32)
        carried = jnp.dot(cconv, prefix_ref[0, :, lanes], preferred_element_type=jnp.float32)
        decay = jnp.exp2(jnp.where(left, cums[0], cums[1]))
        y_ref[:, lanes] = inner + decay * carried + gain_ref[:, lanes] * xc.astype(jnp.float32)


def local_mix(first, count, xconv, bc, aux, prefix, gain):
    inner = xconv.shape[1]
    heads = gain.shape[1] // 64
    wide = bc.shape[1] // 2
    block = lambda w: pl.BlockSpec((CHUNK, w), lambda i: (i + first, 0))
    return pl.pallas_call(
        functools.partial(inner_kernel, heads),
        grid=(count,),
        in_specs=[block(inner), block(2 * wide), block(LANES),
                  pl.BlockSpec((1, wide, inner), lambda i: (i + first, 0, 0)),
                  pl.BlockSpec((1, inner), lambda i: (0, 0))],
        out_specs=pl.BlockSpec((CHUNK, inner), lambda i: (i, 0)),
        out_shape=jax.ShapeDtypeStruct((count * CHUNK, inner), jnp.float32),
        compiler_params=pltpu.CompilerParams(vmem_limit_bytes=VMEM_LIMIT),
        cost_estimate=pl.CostEstimate(flops=10**10, bytes_accessed=24 << 20, transcendentals=1 << 22),
        name="local_mix",
    )(xconv, bc, aux, prefix, gain)


def scan_kernel(got_ref, out_ref):
    members, rows, width = out_ref.shape
    entering = jnp.zeros((rows, width), jnp.float32)
    for k in range(members):
        out_ref[k] = entering.astype(jnp.bfloat16)
        decay = got_ref[k, rows : rows + 1, :].astype(jnp.float32) + got_ref[
            k, rows + 8 : rows + 9, :
        ].astype(jnp.float32)
        entering = decay * entering + got_ref[k, 0:rows, :].astype(jnp.float32)


def scan_members(got):
    members, rows, width = got.shape
    return pl.pallas_call(
        scan_kernel,
        out_shape=jax.ShapeDtypeStruct((members, rows - DECAY_ROWS, width), jnp.bfloat16),
        compiler_params=pltpu.CompilerParams(vmem_limit_bytes=VMEM_LIMIT),
        name="scan_members",
    )(got)


def finish_kernel(heads, ya_ref, yb_ref, bc_ref, aux_ref, inc_ref, out_ref, expand):
    wide = bc_ref.shape[1] // 2
    pairs = out_ref.shape[1] // LANES

    @pl.when(pl.program_id(0) == 0)
    def _():
        expand[...] = expander(heads, out_ref.shape[1] // heads, 2)

    high, low = split_low(jnp.exp2(aux_ref[:, 2 * heads : 3 * heads]))
    factors = jnp.concatenate([high, low], axis=1)
    cconv = bc_ref[:, wide:]
    early = pl.program_id(0) < pl.num_programs(0) // 2

    def emit(y_ref):
        for j in range(pairs):
            lanes = slice(j * LANES, (j + 1) * LANES)
            decay = jnp.dot(factors, expand[:, lanes], preferred_element_type=jnp.float32)
            carried = jnp.dot(cconv, inc_ref[j], preferred_element_type=jnp.float32)
            out_ref[:, lanes] = (y_ref[:, lanes] + decay * carried).astype(jnp.bfloat16)

    @pl.when(early)
    def _():
        emit(ya_ref)

    @pl.when(jnp.logical_not(early))
    def _():
        emit(yb_ref)


def finish(heads, ya, yb, bc, aux, inc):
    rows, inner = bc.shape[0], ya.shape[1]
    wide = bc.shape[1] // 2
    steps = rows // CHUNK
    half = steps // 2
    block = lambda w: pl.BlockSpec((CHUNK, w), lambda i: (i, 0))
    return pl.pallas_call(
        functools.partial(finish_kernel, heads),
        grid=(steps,),
        in_specs=[
            pl.BlockSpec((CHUNK, inner), lambda i: (jnp.minimum(i, half - 1), 0)),
            pl.BlockSpec((CHUNK, inner), lambda i: (jnp.maximum(i - half, 0), 0)),
            block(2 * wide), block(LANES), pl.BlockSpec(inc.shape, lambda i: (0, 0, 0)),
        ],
        out_specs=block(inner),
        out_shape=jax.ShapeDtypeStruct((rows, inner), jnp.bfloat16),
        scratch_shapes=[pltpu.VMEM((2 * heads, inner), jnp.bfloat16)],
        compiler_params=pltpu.CompilerParams(vmem_limit_bytes=VMEM_LIMIT),
        name="finish",
    )(ya, yb, bc, aux, inc)


def exchange(x):
    return lax.all_to_all(x, "seq", split_axis=0, concat_axis=0, tiled=True)


def regroup(x, count):
    groups, rows, width = x.shape
    if groups == count:
        return x
    flat = x.transpose(1, 0, 2).reshape(rows, groups * width)
    return flat.reshape(rows, count, groups * width // count).transpose(1, 0, 2)


FUSED_CHIPS = 8
PAD = 16
QUAD = 2 * LANES
BIG = 1e38


def fused_kernel(
    x_hbm, b_hbm, c_hbm, raw_hbm, kx_hbm, kb_hbm, kc_hbm, rate_hbm, bias_hbm, gain_hbm,
    y, cconv, decays, incoming,
    raw_ref, kx_ref, kb_ref, kc_ref, rate_ref, bias_ref, gain_ref,
    xbuf, bbuf, cbuf, xc, bconv, aux, turned, expand, gains, falls, ends, factors, growth, btrans, prefix, window_a, window_b,
    scaled_a, scaled_b,
    run, core_got, chip_sum, got, entered, back, core_out, arrived,
    load_sem, small_sem, param_sem, tail_send, tail_recv, core_send, core_recv,
    give_send, give_recv, take_send, take_recv, last_send, last_recv,
):
    f32, bf16 = jnp.float32, jnp.bfloat16
    members = 2 * FUSED_CHIPS
    me = lax.axis_index("seq")
    chip, core = me // 2, me % 2
    partner = chip * 2 + 1 - core
    first_core = core == 0
    rows, inner = xc.shape
    wide = bconv.shape[1]
    heads = rate_ref.shape[1]
    pairs = inner // LANES
    chunks = rows // CHUNK
    half = pairs // 2
    steps = pairs // 2

    after = lax.rem(me + 1, members)

    def place(i, at=None):
        who = me if at is None else at
        m = lax.rem(who // 4 + 1 + i // 2, half // 2)
        mine = i % 2
        owner = mine * (who % 2) + (1 - mine) * (1 - who % 2)
        return m, owner * (half // 2) + m

    def quad_lanes(i):
        return pl.ds(pl.multiple_of(place(i)[1] * QUAD, QUAD), QUAD)

    def load(i):
        lanes = quad_lanes(i)
        return pltpu.make_async_copy(
            x_hbm.at[:, lanes], xbuf.at[pl.ds(PAD, rows), lanes], load_sem.at[i]
        )

    small = [
        pltpu.make_async_copy(b_hbm, bbuf.at[pl.ds(PAD, rows)], small_sem.at[0]),
        pltpu.make_async_copy(c_hbm, cbuf.at[pl.ds(PAD, rows)], small_sem.at[1]),
    ]
    params = [
        pltpu.make_async_copy(src, dst, param_sem.at[i])
        for i, (src, dst) in enumerate((
            (rate_hbm, rate_ref), (bias_hbm, bias_ref), (gain_hbm, gain_ref), (raw_hbm, raw_ref),
            (kx_hbm, kx_ref), (kb_hbm, kb_ref), (kc_hbm, kc_ref),
        ))
    ]
    for copy in params + small[:1]:
        copy.start()
    for i in range(steps):
        load(i).start()
    small[1].start()

    barrier = pltpu.get_barrier_semaphore()
    for off in range(1, members):
        pl.semaphore_signal(
            barrier, inc=1, device_id={"seq": lax.rem(me + off, members)},
            device_id_type=pl.DeviceIdType.MESH,
        )

    def remote(src, dst, send, recv, to):
        return pltpu.make_async_remote_copy(
            src_ref=src, dst_ref=dst, send_sem=send, recv_sem=recv, device_id={"seq": to},
            device_id_type=pl.DeviceIdType.MESH,
        )

    def x_tail(i, at):
        lanes = pl.ds(pl.multiple_of(place(i, at)[1] * QUAD, QUAD), QUAD)
        return remote(
            x_hbm.at[pl.ds(rows - PAD, PAD), lanes], xbuf.at[pl.ds(0, PAD), lanes],
            tail_send.at[i], tail_recv.at[i], after,
        )

    small_tails = [
        remote(
            h.at[pl.ds(rows - PAD, PAD)], v.at[pl.ds(0, PAD)], tail_send.at[steps + k],
            tail_recv.at[steps + k], after,
        )
        for k, (h, v) in enumerate(((b_hbm, bbuf), (c_hbm, cbuf)))
    ]

    expand[...] = expander(heads, inner // heads, 2)
    pl.semaphore_wait(barrier, members - 1)

    @pl.when(me < members - 1)
    def _():
        small_tails[0].start()
        for i in range(steps):
            x_tail(i, after).start()
        small_tails[1].start()

    for copy in params:
        copy.wait()
    high, middle = split_low(jnp.broadcast_to(gain_ref[...], (8, heads)))
    low = (gain_ref[...] - high.astype(f32) - middle.astype(f32)).astype(bf16)
    gains[...] = jnp.dot(
        jnp.concatenate([high, middle], axis=1), expand[...], preferred_element_type=f32
    ) + jnp.dot(
        jnp.concatenate([low, jnp.zeros_like(low)], axis=1), expand[...], preferred_element_type=f32
    )
    row = lax.broadcasted_iota(jnp.int32, (CHUNK, CHUNK), 0)
    col = lax.broadcasted_iota(jnp.int32, (CHUNK, CHUNK), 1)
    turns = jnp.concatenate([rate_ref[...], bias_ref[...], rate_ref[...], bias_ref[...]], axis=1)
    turns = jnp.broadcast_to(turns, (CHUNK, CHUNK)).T
    speed = jnp.exp(turns[:heads]) * LOG2E
    bias = turns[heads : 2 * heads]
    upper = (row <= col).astype(bf16)
    chunk_falls, chunk_growth = [], []
    before = jnp.zeros((1, heads), f32)
    for q in range(chunks):
        span = slice(q * CHUNK, (q + 1) * CHUNK)
        shifted = raw_ref[:, span] + bias
        dt = jnp.maximum(shifted, 0.0) + jnp.log1p(jnp.exp(-jnp.abs(shifted)))
        logdec = -speed * dt
        part0 = logdec.astype(bf16)
        rest = logdec - part0.astype(f32)
        part1 = rest.astype(bf16)
        part2 = (rest - part1.astype(f32)).astype(bf16)
        sums = jnp.dot(
            jnp.concatenate([part0, part1, part2], axis=0), upper, preferred_element_type=f32
        )
        cum = sums[:heads] + sums[heads : 2 * heads] + sums[2 * heads :]
        total = jnp.broadcast_to(cum[:, CHUNK - 1 :], cum.shape)
        shift = cum - jnp.log(dt) * LOG2E
        flat = jnp.concatenate(
            [cum, shift, cum, jnp.exp2(total - shift)], axis=0
        )
        stood = flat.T
        turned[q] = flat
        aux[q] = stood
        factors[span, :] = stood[:, 3 * heads :].astype(bf16)
        chunk_growth.append(jnp.exp2(before))
        before = before + stood[CHUNK - 1 :, :heads]
        chunk_falls.append(jnp.exp2(stood[CHUNK - 1 :, :heads]))
    high, low = split_low(jnp.concatenate(chunk_falls, axis=0))
    falls[...] = jnp.dot(
        jnp.concatenate([high, low], axis=1), expand[...], preferred_element_type=f32
    )
    high, low = split_low(jnp.concatenate(chunk_growth, axis=0))
    growth[...] = jnp.dot(
        jnp.concatenate([high, low], axis=1), expand[...], preferred_element_type=f32
    )
    high, low = split_low(jnp.broadcast_to(jnp.exp2(before), (8, heads)))
    zero = jnp.zeros_like(high)
    high = jnp.dot(jnp.concatenate([high, zero], axis=1), expand[...], preferred_element_type=f32)
    low = jnp.dot(jnp.concatenate([low, zero], axis=1), expand[...], preferred_element_type=f32)
    ends[...] = jnp.concatenate([high, low], axis=0).astype(bf16)
    def fill(buf, slot, at, count, lanes):
        slot[at : at + count, :] = buf[at : at + count, lanes].astype(f32)

    def convolve(taps_ref, slot, q, lanes):
        taps = 0.5 * taps_ref[:, lanes]
        count = taps.shape[0]
        at = PAD - count + 1 + q * CHUNK
        total = taps[0:1] * slot[at : at + CHUNK, :]
        for k in range(1, count):
            total = total + taps[k : k + 1] * slot[at + k : at + k + CHUNK, :]
        return total + total * jnp.tanh(total)

    everything = slice(0, LANES)

    def small_chunk(q):
        span = slice(q * CHUNK, (q + 1) * CHUNK)
        bconv[span, :] = convolve(kb_ref, window_b.at[0], q, everything).astype(bf16)

    def part_lanes(i, part):
        return pl.ds(pl.multiple_of(place(i)[1] * QUAD + part * LANES, LANES), LANES)

    def fill_chunk(i, win, q):
        for part in range(2):
            fill(xbuf, win.at[part], PAD + q * CHUNK, CHUNK, part_lanes(i, part))

    def convolve_chunk(i, win, scaled, q):
        span = slice(q * CHUNK, (q + 1) * CHUNK)
        spread = jnp.dot(
            factors[span, :], expand[:heads, quad_lanes(i)], preferred_element_type=f32
        )
        for part in range(2):
            lanes = part_lanes(i, part)
            piece = slice(part * LANES, (part + 1) * LANES)
            done = convolve(kx_ref, win.at[part], q, lanes)
            xc[span, lanes] = done.astype(bf16)
            scaled[span, piece] = (done * spread[:, piece]).astype(bf16)

    small[0].wait()
    fill(bbuf, window_b.at[0], PAD, rows, everything)
    for q in range(1, chunks):
        small_chunk(q)
    load(0).wait()
    for q in range(chunks):
        fill_chunk(0, window_a, q)
    for q in range(1, chunks):
        convolve_chunk(0, window_a, scaled_a, q)

    def tail_here(copy):
        @pl.when(me > 0)
        def _():
            copy.wait_recv()

    tail_here(small_tails[0])
    tail_here(x_tail(0, me))

    @pl.when(me == 0)
    def _():
        xbuf[0:PAD, :] = jnp.zeros((PAD, inner), bf16)
        bbuf[0:PAD, :] = jnp.zeros((PAD, wide), bf16)
        cbuf[0:PAD, :] = jnp.zeros((PAD, wide), bf16)

    fill(bbuf, window_b.at[0], 0, PAD, everything)
    small_chunk(0)
    for part in range(2):
        fill(xbuf, window_a.at[part], 0, PAD, part_lanes(0, part))
    convolve_chunk(0, window_a, scaled_a, 0)
    for q in range(chunks):
        span = slice(q * CHUNK, (q + 1) * CHUNK)
        btrans[:, span] = bconv[span, :].astype(f32).T.astype(bf16)

    def state_chunk(i, scaled, q, held):
        span = slice(q * CHUNK, (q + 1) * CHUNK)
        lanes = quad_lanes(i)
        prefix[q, :, lanes] = held.astype(bf16)
        return falls[q : q + 1, lanes] * held + jnp.dot(
            btrans[:, span], scaled[span, :], preferred_element_type=f32
        )

    def state_and_next(i, scaled, following):
        held = jnp.zeros((wide, QUAD), f32)
        if following is not None:
            win, into = following
            for part in range(2):
                fill(xbuf, win.at[part], 0, PAD, part_lanes(i + 1, part))
        for q in range(chunks):
            if following is not None:
                fill_chunk(i + 1, win, q)
                convolve_chunk(i + 1, win, into, q)
            held = state_chunk(i, scaled, q, held)
        held = held.astype(bf16)
        tip = ends[:, quad_lanes(i)]
        first = place(i)[1] * 2
        for part in range(2):
            piece = slice(part * LANES, (part + 1) * LANES)
            run[first + part, 0:wide, :] = held[:, piece]
            run[first + part, wide:, :] = tip[:, piece]

    def to_core(m):
        return remote(
            run.at[pl.ds((1 - core) * half + 2 * m, 2)], core_got.at[pl.ds(2 * m, 2)],
            core_send.at[m], core_recv.at[m], partner,
        )

    def give(other):
        return remote(
            chip_sum.at[other], got.at[chip], give_send.at[other], give_recv.at[chip],
            other * 2 + core,
        )

    def given(other):
        return remote(
            chip_sum.at[other], got.at[other], give_send.at[other], give_recv.at[other],
            other * 2 + core,
        )

    def take(other):
        return remote(
            entered.at[other], back.at[chip], take_send.at[other], take_recv.at[chip],
            other * 2 + core,
        )

    def taken(other):
        return remote(
            entered.at[other], back.at[other], take_send.at[other], take_recv.at[other],
            other * 2 + core,
        )

    def last(part):
        span = pl.ds(part * (half // 2), half // 2)
        return remote(
            core_out.at[span], arrived.at[span], last_send.at[part], last_recv.at[part], partner,
        )

    def decay_of(piece):
        return piece[wide : wide + 1].astype(f32) + piece[wide + 8 : wide + 9].astype(f32)

    def add_cores(m):
        to_core(m).wait_recv()
        for part in range(2):
            j = 2 * m + part
            mine, other = run[core * half + j], core_got[j]
            lead = jnp.where(first_core, mine.astype(f32), other.astype(f32))
            trail = jnp.where(first_core, other.astype(f32), mine.astype(f32))
            fall = trail[wide : wide + 1] + trail[wide + 8 : wide + 9]
            whole = (lead[wide : wide + 1] + lead[wide + 8 : wide + 9]) * fall
            high, low = split_low(jnp.broadcast_to(whole, (8, LANES)))
            chip_sum[j, 0:wide, :] = (fall * lead[:wide] + trail[:wide]).astype(bf16)
            chip_sum[j, wide:, :] = jnp.concatenate(
                [high.astype(f32), low.astype(f32)], axis=0
            ).astype(bf16)

            @pl.when(j != chip)
            def _():
                give(j).start()

            @pl.when(j == chip)
            def _():
                got[chip] = chip_sum[chip]

    def others(act):
        for off in range(1, FUSED_CHIPS):
            act(lax.rem(chip + off, FUSED_CHIPS))

    def scan_chips():
        others(lambda k: given(k).wait_recv())
        value = jnp.zeros((wide, LANES), f32)
        for k in range(FUSED_CHIPS):
            entered[k] = value.astype(bf16)
            if k < FUSED_CHIPS - 1:
                piece = got[k]
                value = decay_of(piece) * value + piece[:wide].astype(f32)
        others(lambda k: take(k).start())
        back[chip] = entered[chip]

    def split_cores():
        for j in range(half):

            @pl.when(j != chip)
            def _():
                taken(j).wait_recv()

            lead = jnp.where(
                first_core, run[core * half + j].astype(f32), core_got[j].astype(f32)
            )
            entering = back[j].astype(f32)
            fall = lead[wide : wide + 1] + lead[wide + 8 : wide + 9]
            later = fall * entering + lead[:wide]
            core_out[j] = jnp.where(first_core, later, entering).astype(bf16)
            incoming[core * half + j] = jnp.where(first_core, entering, later).astype(bf16)
            if j % (half // 2) == half // 2 - 1:
                last(j // (half // 2)).start()

    @pl.loop(0, steps // 2)
    def _(k):
        i = 2 * k
        load(i + 1).wait()
        tail_here(x_tail(i + 1, me))
        state_and_next(i, scaled_a, (window_b, scaled_b))
        to_core(place(i)[0]).start()

        @pl.when(k < steps // 2 - 1)
        def _():
            load(i + 2).wait()
            tail_here(x_tail(i + 2, me))
            state_and_next(i + 1, scaled_b, (window_a, scaled_a))

        @pl.when(k == steps // 2 - 1)
        def _():
            state_and_next(i + 1, scaled_b, None)

        add_cores(place(i + 1)[0])

    @pl.when(me < members - 1)
    def _():
        for i in range(steps):
            x_tail(i, after).wait_send()
        for copy in small_tails:
            copy.wait_send()

    small[1].wait()
    tail_here(small_tails[1])
    fill(cbuf, window_b.at[1], 0, PAD + rows, everything)
    for q in range(chunks):
        span = slice(q * CHUNK, (q + 1) * CHUNK)
        cconv[span, :] = convolve(kc_ref, window_b.at[1], q, everything).astype(bf16)
    left = lax.broadcasted_iota(jnp.int32, (CHUNK, LANES), 1) < LANES // 2

    @pl.loop(0, chunks)
    def _(q):
        at = pl.ds(pl.multiple_of(q * CHUNK, CHUNK), CHUNK)
        cc = cconv[at, :]
        gram = lax.dot_general(
            cc, bconv[at, :], (((1,), (1,)), ((), ())), preferred_element_type=f32
        )
        gram = jnp.where(row >= col, gram, 0.0).astype(bf16)
        grow_row = growth[pl.ds(q, 1), :]
        for g in range(pairs // 2):
            wider = slice(g * QUAD, (g + 1) * QUAD)
            carried = jnp.dot(cc, prefix[q, :, wider], preferred_element_type=f32)
            for part in range(2):
                j = 2 * g + part
                lanes = slice(j * LANES, (j + 1) * LANES)
                values = xc[at, lanes]
                weights, cums = [], []
                for h in (2 * j, 2 * j + 1):
                    cum = jnp.broadcast_to(aux[q, :, h : h + 1], (CHUNK, CHUNK))
                    cums.append(cum)
                    grow = jnp.exp2(cum - turned[q, heads + h : heads + h + 1, :]).astype(bf16)
                    weights.append(gram * jnp.minimum(grow, jnp.asarray(BIG, bf16)))
                zero = jnp.zeros_like(values)
                both = jnp.concatenate(
                    [jnp.where(left, values, zero), jnp.where(left, zero, values)], axis=0
                )
                mixed = jnp.dot(jnp.concatenate(weights, axis=1), both, preferred_element_type=f32)
                decay = jnp.exp2(jnp.where(left, cums[0], cums[1]))
                y[at, lanes] = (
                    mixed + decay * carried[:, part * LANES : (part + 1) * LANES]
                    + gains[0:1, lanes] * values.astype(f32)
                )
                decays[at, lanes] = decay * grow_row[:, lanes]

        @pl.when(q == SCAN_AT)
        def _():
            scan_chips()

        @pl.when(q == SPLIT_AT)
        def _():
            split_cores()

    for m in range(half // 2):
        to_core(m).wait_send()
    others(lambda k: give(k).wait_send())
    others(lambda k: take(k).wait_send())
    for part in range(2):
        last(part).wait()
        span = pl.ds(part * (half // 2), half // 2)
        incoming[pl.ds((1 - core) * half + part * (half // 2), half // 2)] = arrived[span]


SCAN_AT = 1
SPLIT_AT = 6


def output_kernel(y_ref, c_ref, decay_ref, inc_ref, out_hbm, held, store_sem):
    chunks = held.shape[0] // CHUNK

    def store(q):
        at = pl.ds(q * CHUNK, CHUNK)
        return pltpu.make_async_copy(held.at[at], out_hbm.at[at], store_sem.at[q])

    for q in range(chunks):
        at = slice(q * CHUNK, (q + 1) * CHUNK)
        cc = c_ref[at, :]
        for g in range(inc_ref.shape[0] // 2):
            wider = slice(g * QUAD, (g + 1) * QUAD)
            entering = jnp.concatenate([inc_ref[2 * g], inc_ref[2 * g + 1]], axis=1)
            carried = jnp.dot(cc, entering, preferred_element_type=jnp.float32)
            held[at, wider] = (y_ref[at, wider] + decay_ref[at, wider] * carried).astype(jnp.bfloat16)
        store(q).start()
    for q in range(chunks):
        store(q).wait()


def fused(inner_x, input_map, output_map, raw, kernel_x, kernel_b, kernel_c, rate, bias, gain):
    rows, inner = inner_x.shape
    wide = input_map.shape[1]
    heads = rate.shape[1]
    pairs = inner // LANES
    half = pairs // 2
    chunks = rows // CHUNK
    f32, bf16 = jnp.float32, jnp.bfloat16
    far = pl.BlockSpec(memory_space=pltpu.HBM)
    near = pl.BlockSpec(memory_space=pltpu.VMEM)
    tall = wide + DECAY_ROWS
    chips = FUSED_CHIPS
    dma = pltpu.SemaphoreType.DMA
    y, cconv, decays, incoming = pl.pallas_call(
        fused_kernel,
        in_specs=[far] * 10,
        out_specs=[near] * 4,
        out_shape=[
            pltpu.VMEM((rows, inner), f32), pltpu.VMEM((rows, wide), bf16),
            pltpu.VMEM((rows, inner), f32), pltpu.VMEM((pairs, wide, LANES), bf16),
        ],
        scratch_shapes=[
            pltpu.VMEM(raw.shape, f32), pltpu.VMEM(kernel_x.shape, f32),
            pltpu.VMEM(kernel_b.shape, f32), pltpu.VMEM(kernel_c.shape, f32),
            pltpu.VMEM(rate.shape, f32), pltpu.VMEM(bias.shape, f32), pltpu.VMEM(gain.shape, f32),
            pltpu.VMEM((PAD + rows, inner), bf16), pltpu.VMEM((PAD + rows, wide), bf16),
            pltpu.VMEM((PAD + rows, wide), bf16), pltpu.VMEM((rows, inner), bf16),
            pltpu.VMEM((rows, wide), bf16), pltpu.VMEM((chunks, CHUNK, LANES), f32),
            pltpu.VMEM((chunks, LANES, CHUNK), f32), pltpu.VMEM((2 * heads, inner), bf16),
            pltpu.VMEM((8, inner), f32), pltpu.VMEM((chunks, inner), f32),
            pltpu.VMEM((DECAY_ROWS, inner), bf16), pltpu.VMEM((rows, heads), bf16),
            pltpu.VMEM((chunks, inner), f32), pltpu.VMEM((wide, rows), bf16),
            pltpu.VMEM((chunks, wide, inner), bf16), pltpu.VMEM((2, rows + PAD, LANES), f32),
            pltpu.VMEM((2, rows + PAD, LANES), f32), pltpu.VMEM((rows, QUAD), bf16),
            pltpu.VMEM((rows, QUAD), bf16),
            pltpu.VMEM((pairs, tall, LANES), bf16), pltpu.VMEM((half, tall, LANES), bf16),
            pltpu.VMEM((chips, tall, LANES), bf16), pltpu.VMEM((chips, tall, LANES), bf16),
            pltpu.VMEM((chips, wide, LANES), bf16), pltpu.VMEM((chips, wide, LANES), bf16),
            pltpu.VMEM((half, wide, LANES), bf16), pltpu.VMEM((half, wide, LANES), bf16),
            dma((pairs // 2,)), dma((2,)), dma((7,)), dma((pairs // 2 + 2,)),
            dma((pairs // 2 + 2,)), dma((half // 2,)),
            dma((half // 2,)), dma((chips,)), dma((chips,)), dma((chips,)), dma((chips,)),
            dma((2,)), dma((2,)),
        ],
        compiler_params=pltpu.CompilerParams(
            vmem_limit_bytes=FUSED_VMEM, collective_id=0, has_side_effects=True
        ),
        name="fused_mixer",
    )(inner_x, input_map, output_map, raw, kernel_x, kernel_b, kernel_c, rate, bias, gain)
    return pl.pallas_call(
        output_kernel,
        in_specs=[near] * 4,
        out_specs=pl.BlockSpec(memory_space=pl.ANY),
        out_shape=jax.ShapeDtypeStruct((rows, inner), bf16),
        scratch_shapes=[pltpu.VMEM((rows, inner), bf16), dma((chunks,))],
        compiler_params=pltpu.CompilerParams(vmem_limit_bytes=OUTPUT_VMEM),
        name="output_rows",
    )(y, cconv, decays, incoming)


FUSED_VMEM = (47 << 20) + (160 << 10)
OUTPUT_VMEM = 16 << 20


def on_device(
    inner_x, input_map, output_map, step_raw, kernel_x, kernel_b, kernel_c, log_rate, step_bias,
    skip_gain,
):
    rows, inner = inner_x.shape
    heads = log_rate.shape[0]
    members = lax.axis_size("seq")
    if members == 2 * FUSED_CHIPS and inner == members * LANES and rows % ROWS == 0:
        return fused(
            inner_x, input_map, output_map, step_raw.T, kernel_x, kernel_b, kernel_c,
            log_rate[None, :], step_bias[None, :], skip_gain[None, :],
        )
    last = jnp.concatenate([a[rows - HALO :] for a in (inner_x, input_map, output_map)], axis=1)
    tail = lax.ppermute(last, "seq", [(i, i + 1) for i in range(members - 1)])
    xconv, bc, aux, prefix, run = local_states(
        inner_x, input_map, output_map, step_raw, tail, kernel_x, kernel_b, kernel_c,
        log_rate[None, :], step_bias[None, :],
    )
    gain = jnp.repeat(skip_gain, inner // heads)[None, :]
    half = rows // CHUNK // 2
    got = exchange(regroup(run, members))
    ya = local_mix(0, half, xconv, bc, aux, prefix, gain)
    got, ya = lax.optimization_barrier((got, ya))
    back = exchange(scan_members(got))
    yb = local_mix(half, half, xconv, bc, aux, prefix, gain)
    incoming = regroup(back, inner // LANES)
    return finish(heads, ya, yb, bc, aux, incoming)


def solution(mesh):
    split = P(("groups", "seq"), None)
    return jax.shard_map(
        on_device, mesh=mesh, in_specs=(split,) * 4 + (P(),) * 6, out_specs=split, check_vma=False
    )
```
